128 devices in a mesh: gx: 8 (over y, core), gy: 16 (over z, x).
Axes of the slice: x: 4, y: 4, z: 4, core: 2. Of those that a mesh axis runs over, the one named last changes fastest.
Arguments:
- raw_window: float32 [8192, 16384], P('gx', 'gy'), may hold values from -6 to 6
- source_ids: int32 [256], P(('gx', 'gy')), may hold values from 0 to 8191, as said below
- pair_source: int32 [16384], P(('gx', 'gy')), may hold values from 0 to 255
- pair_holder: int32 [16384, 1], P(('gx', 'gy')), may hold values from 0 to 127; in each aligned block of 128 rows (0 to 127, 128 to 255, ...) at most 2 rows name the same one
- pair_receiver: int32 [16384], P(('gx', 'gy')), may hold values from 0 to 63
Outputs:
- correlations: float32 [16384, 512], P(('gx', 'gy'))
The draws below stay inside these ranges and needn't reach their ends.
Inputs may be any that keep to these rules, and one draw needn't show every extreme that they name: The ids are distinct, and source k is a channel of the device that holds channels from (k // 2) * 64 on: source_ids[k] // 64 == k // 2. `pair_holder`: among the 128 pairs of one device, at most 2 name the same holder, a bound that some block reaches; every device is named by some pair.
All inputs are finite; a program needn't handle non-finite values.
Results may differ from the reference program's by a relative error of at most 0.0095.
Values may be sent and summed in bfloat16 or wider, within the bound.
No kernel may reach another device: no remote copies, remote signals or barrier semaphores. Data moves between devices by JAX's collectives and lax.ppermute only.
A program may use at most 128 MiB of HBM per device.

```python
import math
import jax
import jax.numpy as jnp
import numpy as np
from jax import lax

NBIN = 2048
SEGLEN = 4096
NSEG = 4
BAND = 64
NLAG = 512
VS = 256
CH_DEV = 64
PAIRS_DEV = 128
CHANNELS = 8192
TIME = 16384
SRC_DEV = 2
CAP = 2
PAIRS = 16384
N_GX = 8
N_GY = 16


def draw_source_ids(key, part):
    blocks = VS // SRC_DEV
    scores = jax.random.randint(key, (blocks, CH_DEV), 0, 1 << 20)
    scores = scores * CH_DEV + jnp.arange(CH_DEV, dtype=jnp.int32)[None, :]
    order = jnp.argsort(scores, axis=1, stable=True)[:, :SRC_DEV].astype(jnp.int32)
    offsets = CH_DEV * jnp.arange(blocks, dtype=jnp.int32)[:, None]
    return (order + offsets).reshape(VS).astype(jnp.int32)


def plant(result, rng, low, high):
    index_at = [jax.random.randint(jax.random.fold_in(rng, axis), (), 0, length) for axis, length in enumerate(result.shape)]
    main_axis = result.shape.index(max(result.shape))
    neighbour = index_at[:main_axis] + [(index_at[main_axis] + 1) % result.shape[main_axis]] + index_at[main_axis + 1:]
    return result.at[tuple(index_at)].set(low).at[tuple(neighbour)].set(high)


def block_scale(stream_key, dims, pieces, smallest, high):
    loudness = 1.0
    for position, blocks in pieces:
        heights = jax.random.uniform(jax.random.fold_in(jax.random.fold_in(stream_key, 6), position), (blocks,), jnp.float32, smallest / len(pieces), high / len(pieces))
        loudness = loudness * jnp.repeat(jnp.exp(heights), dims[position] // blocks).reshape((-1,) + (1,) * (len(dims) - 1 - position))
    return loudness


def rank_bounds(count, slope):
    loads = [(1 << 20) // math.isqrt(rank ** slope) + 1 for rank in range(1, count + 1)]
    scale = 1 + sum(loads) // (1 << 30)
    return np.cumsum(np.array([max(1, weight // scale) for weight in loads]))


def skewed_ids(rng, extent, amount, skew):
    grid = rank_bounds(amount, skew)
    lot = jax.random.randint(jax.random.fold_in(rng, 1), extent, 0, int(grid[amount - 1]))
    rank = jnp.searchsorted(jnp.asarray(grid, jnp.int32), lot, side="right")
    return jax.random.permutation(jax.random.fold_in(rng, 2), amount)[rank].astype(jnp.int32)


def deal_out(key, own, number, rows, number_of, top, bound, lean):
    ranking = jax.random.permutation(key, number_of)
    crowded, ordinary = load_shares(number_of, rows * top, bound, lean, True), load_shares(number_of, rows * top, bound, lean, False)
    places = jnp.arange(number_of)

    def named(lengths, turn):
        used = int((lengths > 0).sum())
        fixed = max(1, used // 4)
        passed = fixed + (places - fixed + turn * (used - fixed)) % max(1, number_of - fixed)
        return jnp.zeros((number_of,), jnp.int32).at[ranking[jnp.where(places < fixed, places, passed)]].set(jnp.asarray(lengths, jnp.int32))

    lengths = jnp.where(number % 4 == 0, named(crowded, number // 4), named(ordinary, number - number // 4 - 1))
    mixed = jax.random.permutation(jax.random.fold_in(own, 3), number_of)
    source_of, receiver = mixed[0:number_of // 2 * 2:2], mixed[1:number_of // 2 * 2:2]
    room = jnp.minimum(lengths[source_of] - 1, bound - lengths[receiver]) // 2
    room = jnp.where((source_of == ranking[0]) | (receiver == ranking[0]) | (lengths[receiver] == 0), 0, jnp.maximum(room, 0))
    passed = jax.random.randint(jax.random.fold_in(own, 4), (number_of // 2,), 0, 1 << 20) % (room + 1)
    lengths = lengths.at[source_of].add(-passed).at[receiver].add(passed)
    items = jnp.searchsorted(jnp.cumsum(lengths), jnp.arange(rows * top), side="right").astype(jnp.int32)
    table = items.reshape(top, rows).T
    table = table[jax.random.permutation(jax.random.fold_in(own, 1), rows)]
    turn = jax.random.randint(jax.random.fold_in(own, 2), (rows, 1), 0, top)
    return jnp.take_along_axis(table, (jnp.arange(top)[None, :] + turn) % top, axis=1)


def load_shares(count, total, most, skew, full):
    weights = [(1 << 20) // math.isqrt(grade ** skew) + 1 for grade in range(1, count + 1)]
    largest = most if full else min(most, max(-(-total // count), total * weights[0] // sum(weights)))
    least = 1 if total - largest >= count - 1 else 0
    counts, surplus = [largest] + [least] * (count - 1), total - largest - least * (count - 1)
    while surplus > 0:
        free = [i for i in range(1, count) if counts[i] < largest] or [i for i in range(1, count) if counts[i] < most]
        pool, budget = sum([weights[i] for i in free]), surplus
        for i in free:
            addition = min(most - counts[i], max(1, budget * weights[i] // pool), surplus)
            counts[i] = counts[i] + addition
            surplus = surplus - addition
    return np.array(counts)


def normal_values(stream_key, dims, deviation, most, shards=(), kind=jnp.bfloat16):
    values = deviation * jax.random.normal(stream_key, dims, jnp.float32)
    if shards:
        values = values * block_scale(stream_key, dims, shards, -0.22, 0.18)
    return jnp.clip(values, -most, most).astype(kind)


def setup_inputs(seed: int = 0) -> dict:
    streams_of = jax.random.split(jax.random.key(seed), 6)
    raw_window = normal_values(streams_of[0], (CHANNELS, TIME), 1.0, 6.0, ((0, 8), (1, 16)), jnp.float32)
    source_ids = draw_source_ids(jax.random.fold_in(streams_of[5], 71), 0)
    pair_source = plant(skewed_ids(streams_of[2], (PAIRS,), VS, 2), jax.random.fold_in(streams_of[2], 3), 0, VS - 1).astype(jnp.int32)
    pair_holder_keys = jax.random.split(jax.random.fold_in(streams_of[3], 1), PAIRS // PAIRS_DEV)
    pair_holder_turns = jax.random.permutation(jax.random.fold_in(streams_of[3], 3), PAIRS // PAIRS_DEV)
    pair_holder = jax.vmap(lambda own, number: deal_out(jax.random.fold_in(streams_of[3], 2), own, number, PAIRS_DEV, N_GX * N_GY, 1, CAP, 2))(pair_holder_keys, pair_holder_turns).reshape((PAIRS, 1))
    pair_receiver = plant(jax.random.randint(streams_of[4], (PAIRS,), 0, CH_DEV), jax.random.fold_in(streams_of[4], 1), 0, CH_DEV - 1).astype(jnp.int32)
    return {"raw_window": raw_window, "source_ids": source_ids, "pair_source": pair_source, "pair_holder": pair_holder, "pair_receiver": pair_receiver}


def inverse_table():
    bins = jnp.arange(NBIN, dtype=jnp.int32)
    lags = (jnp.arange(NLAG, dtype=jnp.int32) - NLAG // 2) % SEGLEN
    phase = bins[:, None] * lags[None, :] % SEGLEN
    angle = phase.astype(jnp.float32) * (2.0 * math.pi / SEGLEN)
    weight = jnp.where(bins == 0, 1.0, 2.0).astype(jnp.float32) * (0.5 / math.sqrt(NSEG * NBIN))
    return jnp.concatenate([weight[:, None] * jnp.cos(angle), -weight[:, None] * jnp.sin(angle)], axis=0)

def reference(raw_window, source_ids, pair_source, pair_holder, pair_receiver):
    samples = jnp.arange(SEGLEN, dtype=jnp.float32)
    taper = jnp.sin(math.pi * (samples + 0.5) / SEGLEN) ** 2

    def whiten(block):
        tapered = (block.reshape(CH_DEV, NSEG, SEGLEN) * taper).astype(jnp.bfloat16)
        spectrum = jnp.fft.rfft(tapered.astype(jnp.float32), axis=-1)[..., :NBIN]
        real_part = jnp.real(spectrum)
        imag_part = jnp.imag(spectrum)
        power = (real_part * real_part + imag_part * imag_part).reshape(CH_DEV, NSEG, NBIN // BAND, BAND)
        level = jnp.sqrt(lax.optimization_barrier(jnp.mean(power, axis=3)) + 1e-06)
        level = jnp.repeat(level, BAND, axis=2)
        return jnp.stack([real_part / level, imag_part / level], axis=2).astype(jnp.bfloat16)
    whitened = lax.map(whiten, raw_window.reshape(CHANNELS // CH_DEV, CH_DEV, TIME))
    whitened = whitened.reshape(CHANNELS, NSEG, 2, NBIN)
    receiver_channel = (pair_holder[:, 0] * CH_DEV + pair_receiver).astype(jnp.int32)
    source_channel = jnp.take(source_ids, pair_source).astype(jnp.int32)
    table = inverse_table()

    def pair_block(indices):
        source_rows = jnp.take(whitened, indices[0], axis=0).astype(jnp.float32)
        receiver_rows = jnp.take(whitened, indices[1], axis=0).astype(jnp.float32)
        real_part = lax.optimization_barrier(jnp.sum(source_rows[:, :, 0] * receiver_rows[:, :, 0] + source_rows[:, :, 1] * receiver_rows[:, :, 1], axis=1))
        imag_part = lax.optimization_barrier(jnp.sum(source_rows[:, :, 1] * receiver_rows[:, :, 0] - source_rows[:, :, 0] * receiver_rows[:, :, 1], axis=1))
        cross = jnp.concatenate([real_part, imag_part], axis=1).astype(jnp.bfloat16)
        return jnp.dot(cross.astype(jnp.float32), table, precision=lax.Precision.HIGHEST, preferred_element_type=jnp.float32)
    blocks = PAIRS // PAIRS_DEV
    indices = jnp.stack([source_channel.reshape(blocks, PAIRS_DEV), receiver_channel.reshape(blocks, PAIRS_DEV)], axis=1)
    return lax.map(pair_block, indices).reshape(PAIRS, NLAG)
```

```python
import math

import jax
import jax.numpy as jnp
from jax import lax
from jax.experimental import pallas as pl
from jax.experimental.pallas import tpu as pltpu
from jax.sharding import PartitionSpec as P

NBIN = 2048
SEGLEN = 4096
NSEG = 4
BAND = 64
NLAG = 512
SIDE = 4
RADIX = 16
INNER = SEGLEN // RADIX
LANES = 128
HALF_ROWS = 2 * (RADIX // 2)


def split_table(table):
    upper = table.astype(jnp.bfloat16)
    lower = (table - upper.astype(jnp.float32)).astype(jnp.bfloat16)
    return (upper, lower)


def lane_bins():
    lane = jnp.arange(LANES, dtype=jnp.int32)
    return 4 * (lane % 32) + lane // 32


def inner_table():
    times = jnp.arange(INNER, dtype=jnp.int32)
    low = lane_bins()
    high = INNER - 1 - low
    turn = 2.0 * math.pi / INNER

    def block(bins, sign):
        angle = (times[:, None] * bins[None, :] % INNER).astype(jnp.float32) * turn
        cos, sin = jnp.cos(angle), jnp.sin(angle)
        top = jnp.concatenate([cos, -sign * sin], axis=1)
        bottom = jnp.concatenate([sin, sign * cos], axis=1)
        return jnp.concatenate([top, bottom], axis=0)

    return split_table(jnp.concatenate([block(low, 1.0), block(high, -1.0)], axis=1))


def twiddle_table():
    rows = jnp.arange(RADIX, dtype=jnp.int32)
    times = jnp.arange(INNER, dtype=jnp.int32)
    angle = (rows[:, None] * times[None, :] % SEGLEN).astype(jnp.float32) * (2.0 * math.pi / SEGLEN)
    return jnp.stack([jnp.cos(angle), -jnp.sin(angle)], axis=0)


def inverse_table(core):
    row = jnp.arange(NBIN, dtype=jnp.int32)
    part = row // (NBIN // 2)
    outer = core * (RADIX // 2) + row // LANES % (RADIX // 2)
    lane = row % LANES
    bins = outer + RADIX * (4 * (lane % 32) + lane // 32)
    lags = (jnp.arange(NLAG, dtype=jnp.int32) - NLAG // 2) % SEGLEN
    phase = (bins[:, None] * lags[None, :] + part[:, None] * (SEGLEN // 4)) % SEGLEN
    angle = phase.astype(jnp.float32) * (2.0 * math.pi / SEGLEN)
    weight = jnp.where(bins == 0, 1.0, 2.0).astype(jnp.float32) * (0.5 / math.sqrt(NSEG * NBIN))
    return (weight[:, None] * jnp.cos(angle)).astype(jnp.bfloat16)


def real_dft(values):
    n = len(values)
    if n == 2:
        return [(values[0] + values[1], None), (values[0] - values[1], None)]
    even = real_dft(values[0::2])
    odd = real_dft(values[1::2])
    out = [None] * (n // 2 + 1)
    for k in range(n // 4 + 1):
        er, ei = even[k]
        pr, pi = odd[k]
        c, s = math.cos(2 * math.pi * k / n), math.sin(2 * math.pi * k / n)
        if k == 0:
            out[0] = (er + pr, None)
            out[n // 2] = (er - pr, None)
        elif 4 * k == n:
            out[k] = (er, -pr)
        else:
            if 8 * k == n:
                tr, ti = (pr + pi) * c, (pi - pr) * c
            else:
                tr, ti = pr * c + pi * s, pi * c - pr * s
            out[k] = (er + tr, ei + ti)
            out[n // 2 - k] = (er - tr, ti - ei)
    return out


def whiten_kernel(core_ref, x_ref, tw_ref, upper_ref, lower_ref, mine_ref, other_ref, hi_ref, lo_ref, out_ref):
    rows = x_ref.shape[1]
    slices = []
    for t in range(RADIX):
        q, u = t // SIDE, t % SIDE
        slices.append(x_ref[q, :, u * INNER:(u + 1) * INNER].astype(jnp.float32))
    outer = real_dft(slices)
    for f in range(RADIX // 2 + 1):
        re, im = outer[f]
        c, s = tw_ref[0, f:f + 1, :], tw_ref[1, f:f + 1, :]
        if f == 0:
            pair = (re, jnp.zeros_like(re))
        elif im is None:
            pair = (re * c, re * s)
        else:
            pair = (re * c - im * s, re * s + im * c)
        for k in range(2):
            hi = pair[k].astype(jnp.bfloat16)
            hi_ref[f * rows:(f + 1) * rows, k * INNER:(k + 1) * INNER] = hi
            lo_ref[f * rows:(f + 1) * rows, k * INNER:(k + 1) * INNER] = (pair[k] - hi.astype(jnp.float32)).astype(jnp.bfloat16)
    hi, lo = hi_ref[...], lo_ref[...]
    upper, lower = upper_ref[...], lower_ref[...]
    spectrum = jnp.dot(hi, upper, preferred_element_type=jnp.float32)
    spectrum += jnp.dot(hi, lower, preferred_element_type=jnp.float32)
    spectrum += jnp.dot(lo, upper, preferred_element_type=jnp.float32)

    def part(f, k):
        g, base = (f, 0) if f <= RADIX // 2 else (RADIX - f, 2)
        return spectrum[g * rows:(g + 1) * rows, (base + k) * LANES:(base + k + 1) * LANES]

    power = None
    for f in range(RADIX):
        re, im = part(f, 0), part(f, 1)
        both = re * re + im * im
        power = both if power is None else power + both
    power = power + pltpu.roll(power, 64, 1)
    power = power + pltpu.roll(power, 32, 1)
    scale = 1.0 / jnp.sqrt(power * (1.0 / BAND) + 1e-06)
    for f in range(RADIX):
        for k in range(2):
            index = (f // 8) * HALF_ROWS + k * 8 + f % 8
            out_ref[:, index, :] = part(f, k) * scale
    core = core_ref[0]
    mine_ref[...] = out_ref[:, pl.ds(pl.multiple_of(core * HALF_ROWS, HALF_ROWS), HALF_ROWS), :].astype(jnp.bfloat16)
    other_ref[...] = out_ref[:, pl.ds(pl.multiple_of((1 - core) * HALF_ROWS, HALF_ROWS), HALF_ROWS), :].astype(jnp.bfloat16)


def whiten(core, samples, twiddle, upper, lower):
    rows = samples.shape[1]
    out = jax.ShapeDtypeStruct((rows, NSEG * HALF_ROWS, LANES), jnp.bfloat16)
    spec = pl.BlockSpec((rows, HALF_ROWS, LANES), lambda s, c: (0, s, 0))
    count = RADIX // 2 + 1
    return pl.pallas_call(
        whiten_kernel,
        out_shape=(out, out),
        grid_spec=pltpu.PrefetchScalarGridSpec(
            num_scalar_prefetch=1,
            grid=(NSEG,),
            in_specs=[
                pl.BlockSpec((SIDE, rows, SEGLEN // SIDE), lambda s, c: (s, 0, 0)),
                pl.BlockSpec((2, RADIX, INNER), lambda s, c: (0, 0, 0)),
                pl.BlockSpec((2 * INNER, 4 * LANES), lambda s, c: (0, 0)),
                pl.BlockSpec((2 * INNER, 4 * LANES), lambda s, c: (0, 0)),
            ],
            out_specs=(spec, spec),
            scratch_shapes=[
                pltpu.VMEM((count * rows, 2 * INNER), jnp.bfloat16),
                pltpu.VMEM((count * rows, 2 * INNER), jnp.bfloat16),
                pltpu.VMEM((rows, 2 * HALF_ROWS, LANES), jnp.float32),
            ],
        ),
        compiler_params=pltpu.CompilerParams(vmem_limit_bytes=48 << 20),
        name="whiten",
    )(core, samples, twiddle, upper, lower)


def correlate_kernel(src_ref, rcv_ref, sources_ref, mine_ref, sister_ref, table_ref, out_ref, cross_ref):
    chunk = out_ref.shape[0]
    base = pl.program_id(0) * chunk

    def run(receivers_ref):
        def one(i, carry):
            a = sources_ref[src_ref[base + i]].astype(jnp.float32)
            b = receivers_ref[rcv_ref[base + i]].astype(jnp.float32)
            re = im = None
            for s in range(NSEG):
                ar, ai = a[s * 16:s * 16 + 8], a[s * 16 + 8:s * 16 + 16]
                br, bi = b[s * 16:s * 16 + 8], b[s * 16 + 8:s * 16 + 16]
                r = ar * br + ai * bi
                m = ai * br - ar * bi
                re = r if re is None else re + r
                im = m if im is None else im + m
            cross_ref[i, 0:8, :] = re
            cross_ref[i, 8:16, :] = im
            return carry

        lax.fori_loop(0, chunk, one, 0, unroll=8)

    half = pl.num_programs(0) // 2

    @pl.when(pl.program_id(0) < half)
    def _():
        run(mine_ref)

    @pl.when(pl.program_id(0) >= half)
    def _():
        run(sister_ref)

    cross = jnp.concatenate([cross_ref[:, g, :].astype(jnp.bfloat16) for g in range(HALF_ROWS)], axis=1)
    out_ref[...] = jnp.dot(cross, table_ref[...], preferred_element_type=jnp.float32).astype(jnp.bfloat16)


def correlate(source_at, receiver_at, sources, mine, sister, table):
    slots = source_at.shape[0]
    chunk = 128
    whole = lambda a: pl.BlockSpec(a.shape, lambda i, s, r: (0,) * a.ndim)
    return pl.pallas_call(
        correlate_kernel,
        out_shape=jax.ShapeDtypeStruct((slots, NLAG), jnp.bfloat16),
        grid_spec=pltpu.PrefetchScalarGridSpec(
            num_scalar_prefetch=2,
            grid=(slots // chunk,),
            in_specs=[whole(sources), whole(mine), whole(sister), whole(table)],
            out_specs=pl.BlockSpec((chunk, NLAG), lambda i, s, r: (i, 0)),
            scratch_shapes=[pltpu.VMEM((chunk, HALF_ROWS, LANES), jnp.float32)],
        ),
        compiler_params=pltpu.CompilerParams(vmem_limit_bytes=48 << 20),
        name="correlate",
    )(source_at, receiver_at, sources, mine, sister, table)


def shift(value, axis, step):
    if axis == "core":
        return lax.ppermute(value, "gx", [(g, g ^ 1) for g in range(2 * SIDE)])
    if axis == "y":
        return lax.ppermute(value, "gx", [(g, (g + 2 * step) % (2 * SIDE)) for g in range(2 * SIDE)])
    if axis == "z":
        return lax.ppermute(value, "gy", [(g, (g + SIDE * step) % (SIDE * SIDE)) for g in range(SIDE * SIDE)])
    return lax.ppermute(value, "gy", [(g, g // SIDE * SIDE + (g + step) % SIDE) for g in range(SIDE * SIDE)])


def gather_ring(value, axis):
    return jnp.stack([value] + [shift(value, axis, d) for d in (1, 2, 3)], axis=0)


def gather_last(value, axis):
    ahead, behind = shift(value, axis, 1), shift(value, axis, 3)
    n = value.shape[0] // 2
    far = jnp.concatenate([shift(ahead[:n], axis, 1), shift(behind[n:], axis, 3)], axis=0)
    return jnp.stack([value, ahead, far, behind], axis=0)


def body(raw_window, source_ids, pair_source, pair_holder, pair_receiver):
    groups = lax.axis_size("gy")
    devices = lax.axis_size("gx") * groups
    gx, gy = lax.axis_index("gx"), lax.axis_index("gy")
    place = {"core": gx % 2, "y": gx // 2, "z": gy // SIDE, "x": gy % SIDE}
    core = place["core"]
    span = raw_window.shape[1]
    sample = (gy * span + jnp.arange(span, dtype=jnp.int32)) % SEGLEN
    taper = jnp.sin(math.pi * (sample.astype(jnp.float32) + 0.5) / SEGLEN) ** 2
    tapered = (raw_window * taper[None, :]).astype(jnp.bfloat16)
    channels = raw_window.shape[0] // groups
    samples = lax.all_to_all(tapered.reshape(groups, channels, span), "gy", split_axis=0, concat_axis=0, tiled=True)

    pairs = pair_source.shape[0]
    holder = pair_holder[:, 0]
    order = jnp.arange(pairs, dtype=jnp.int32)
    same = (holder[:, None] == holder[None, :]) & (order[None, :] < order[:, None])
    rank = jnp.sum(same.astype(jnp.int32), axis=1)
    slot = holder * 2 + rank
    packed = pair_receiver * 256 + pair_source
    named = jnp.arange(2 * devices, dtype=jnp.int32)[:, None] == slot[None, :]
    outgoing = jnp.sum(jnp.where(named, packed[None, :], 0), axis=1).reshape(devices, 2)
    incoming = lax.all_to_all(outgoing, ("gx", "gy"), split_axis=0, concat_axis=0, tiled=True).reshape(-1)
    asked = jnp.concatenate([incoming, shift(incoming, "core", 1)])
    receiver_at, source_no = asked // 256, asked % 256

    twiddle = twiddle_table()
    upper, lower = inner_table()
    table = inverse_table(core)

    mine, other = whiten(core.reshape(1), samples, twiddle, upper, lower)
    sister = shift(other, "core", 1)
    here = gx * groups + gy
    local = source_ids - here * channels
    own = jnp.take(mine, local, axis=0)
    theirs = shift(jnp.take(other, local, axis=0), "core", 1)
    block = jnp.stack([own, theirs], axis=0)
    axes = ("x", "z", "y")
    block = gather_ring(block, axes[0])
    block = gather_ring(block, axes[1])
    sources = gather_last(block, axes[2]).reshape(devices * 2, NSEG * HALF_ROWS, LANES)

    device_no = source_no // 2
    at = {"y": device_no // (2 * groups), "z": device_no % groups // SIDE, "x": device_no % SIDE}
    core_at = device_no // groups % 2
    source_at = 0
    for axis in reversed(axes):
        source_at = source_at * SIDE + (place[axis] - at[axis]) % SIDE
    source_at = (source_at * 2 + (core_at ^ core)) * 2 + source_no % 2

    partial = correlate(source_at, receiver_at, sources, mine, sister, table)
    outgoing = jnp.transpose(partial.reshape(2, devices, 2, NLAG), (1, 0, 2, 3))
    returned = lax.all_to_all(outgoing, ("gx", "gy"), split_axis=0, concat_axis=0, tiled=True)
    returned = returned.reshape(devices * 4, NLAG)
    holder_core = holder // groups % 2
    row = jnp.arange(4 * devices, dtype=jnp.int32)
    row_dev, row_rel, row_rank = row // 4, row // 2 % 2, row % 2
    row_holder = jnp.where(row_rel == 0, row_dev, row_dev ^ groups)
    pick = (row_holder[None, :] == holder[:, None]) & (row_rank[None, :] == rank[:, None])
    return jnp.dot(pick.astype(jnp.bfloat16), returned, preferred_element_type=jnp.float32)


def solution(mesh):
    return jax.shard_map(
        body,
        mesh=mesh,
        in_specs=(
            P("gx", "gy"),
            P(("gx", "gy")),
            P(("gx", "gy")),
            P(("gx", "gy"), None),
            P(("gx", "gy")),
        ),
        out_specs=P(("gx", "gy"), None),
        check_vma=False,
    )
```

```python
import math

import jax
import jax.numpy as jnp
from jax import lax
from jax.experimental import pallas as pl
from jax.experimental.pallas import tpu as pltpu
from jax.sharding import PartitionSpec as P

NBIN = 2048
SEGLEN = 4096
NSEG = 4
BAND = 64
NLAG = 512
SIDE = 4
RADIX = 16
INNER = SEGLEN // RADIX
LANES = 128
HALF_ROWS = 2 * (RADIX // 2)


def split_table(table):
    upper = table.astype(jnp.bfloat16)
    lower = (table - upper.astype(jnp.float32)).astype(jnp.bfloat16)
    return (upper, lower)


def lane_bins():
    lane = jnp.arange(LANES, dtype=jnp.int32)
    return 4 * (lane % 32) + lane // 32


def inner_table():
    times = jnp.arange(INNER, dtype=jnp.int32)
    low = lane_bins()
    high = INNER - 1 - low
    turn = 2.0 * math.pi / INNER

    def block(bins, sign):
        angle = (times[:, None] * bins[None, :] % INNER).astype(jnp.float32) * turn
        cos, sin = jnp.cos(angle), jnp.sin(angle)
        top = jnp.concatenate([cos, -sign * sin], axis=1)
        bottom = jnp.concatenate([sin, sign * cos], axis=1)
        return jnp.concatenate([top, bottom], axis=0)

    return split_table(jnp.concatenate([block(low, 1.0), block(high, -1.0)], axis=1))


def twiddle_table():
    rows = jnp.arange(RADIX, dtype=jnp.int32)
    times = jnp.arange(INNER, dtype=jnp.int32)
    angle = (rows[:, None] * times[None, :] % SEGLEN).astype(jnp.float32) * (2.0 * math.pi / SEGLEN)
    return jnp.stack([jnp.cos(angle), -jnp.sin(angle)], axis=0)


def turns(count, lags):
    angle = (count[:, None] * lags[None, :] % SEGLEN).astype(jnp.float32) * (2.0 * math.pi / SEGLEN)
    return jnp.cos(angle), jnp.sin(angle)


def inverse_table(core):
    outer = core * (RADIX // 2) + jnp.arange(RADIX // 2, dtype=jnp.int32)
    inner = RADIX * lane_bins()
    lags = (jnp.arange(NLAG, dtype=jnp.int32) - NLAG // 2) % SEGLEN
    (c1, s1), (c2, s2) = lax.optimization_barrier((turns(outer, lags), turns(inner, lags)))
    c1, s1, c2, s2 = c1[:, None], s1[:, None], c2[None], s2[None]
    bins = outer[:, None, None] + inner[None, :, None]
    weight = jnp.where(bins == 0, 1.0, 2.0).astype(jnp.float32) * (0.5 / math.sqrt(NSEG * NBIN))
    table = jnp.stack([weight * (c1 * c2 - s1 * s2), -weight * (s1 * c2 + c1 * s2)], axis=0)
    return table.astype(jnp.bfloat16).reshape(NBIN, NLAG)


def real_dft(values):
    n = len(values)
    if n == 2:
        return [(values[0] + values[1], None), (values[0] - values[1], None)]
    even = real_dft(values[0::2])
    odd = real_dft(values[1::2])
    out = [None] * (n // 2 + 1)
    for k in range(n // 4 + 1):
        er, ei = even[k]
        pr, pi = odd[k]
        c, s = math.cos(2 * math.pi * k / n), math.sin(2 * math.pi * k / n)
        if k == 0:
            out[0] = (er + pr, None)
            out[n // 2] = (er - pr, None)
        elif 4 * k == n:
            out[k] = (er, -pr)
        else:
            if 8 * k == n:
                tr, ti = (pr + pi) * c, (pi - pr) * c
            else:
                tr, ti = pr * c + pi * s, pi * c - pr * s
            out[k] = (er + tr, ei + ti)
            out[n // 2 - k] = (er - tr, ti - ei)
    return out


def whiten_kernel(core_ref, x_ref, tw_ref, upper_ref, lower_ref, mine_ref, other_ref, hi_ref, lo_ref, out_ref):
    rows = x_ref.shape[1]
    slices = []
    for t in range(RADIX):
        q, u = t // SIDE, t % SIDE
        slices.append(x_ref[q, :, u * INNER:(u + 1) * INNER].astype(jnp.float32))
    outer = real_dft(slices)
    for f in range(RADIX // 2 + 1):
        re, im = outer[f]
        c, s = tw_ref[0, f:f + 1, :], tw_ref[1, f:f + 1, :]
        if f == 0:
            pair = (re, jnp.zeros_like(re))
        elif im is None:
            pair = (re * c, re * s)
        else:
            pair = (re * c - im * s, re * s + im * c)
        for k in range(2):
            hi = pair[k].astype(jnp.bfloat16)
            hi_ref[f * rows:(f + 1) * rows, k * INNER:(k + 1) * INNER] = hi
            lo_ref[f * rows:(f + 1) * rows, k * INNER:(k + 1) * INNER] = (pair[k] - hi.astype(jnp.float32)).astype(jnp.bfloat16)
    hi, lo = hi_ref[...], lo_ref[...]
    upper, lower = upper_ref[...], lower_ref[...]
    spectrum = jnp.dot(hi, upper, preferred_element_type=jnp.float32)
    spectrum += jnp.dot(hi, lower, preferred_element_type=jnp.float32)
    spectrum += jnp.dot(lo, upper, preferred_element_type=jnp.float32)

    def part(f, k):
        g, base = (f, 0) if f <= RADIX // 2 else (RADIX - f, 2)
        return spectrum[g * rows:(g + 1) * rows, (base + k) * LANES:(base + k + 1) * LANES]

    power = None
    for f in range(RADIX):
        re, im = part(f, 0), part(f, 1)
        both = re * re + im * im
        power = both if power is None else power + both
    power = power + pltpu.roll(power, 64, 1)
    power = power + pltpu.roll(power, 32, 1)
    scale = 1.0 / jnp.sqrt(power * (1.0 / BAND) + 1e-06)
    for f in range(RADIX):
        for k in range(2):
            index = (f // 8) * HALF_ROWS + k * 8 + f % 8
            out_ref[:, index, :] = part(f, k) * scale
    core = core_ref[0]
    mine_ref[...] = out_ref[:, pl.ds(pl.multiple_of(core * HALF_ROWS, HALF_ROWS), HALF_ROWS), :].astype(jnp.bfloat16)
    other_ref[...] = out_ref[:, pl.ds(pl.multiple_of((1 - core) * HALF_ROWS, HALF_ROWS), HALF_ROWS), :].astype(jnp.bfloat16)


def whiten(core, samples, twiddle, upper, lower):
    rows = samples.shape[1]
    out = jax.ShapeDtypeStruct((rows, NSEG * HALF_ROWS, LANES), jnp.bfloat16)
    spec = pl.BlockSpec((rows, HALF_ROWS, LANES), lambda s, c: (0, s, 0))
    count = RADIX // 2 + 1
    return pl.pallas_call(
        whiten_kernel,
        out_shape=(out, out),
        grid_spec=pltpu.PrefetchScalarGridSpec(
            num_scalar_prefetch=1,
            grid=(NSEG,),
            in_specs=[
                pl.BlockSpec((SIDE, rows, SEGLEN // SIDE), lambda s, c: (s, 0, 0)),
                pl.BlockSpec((2, RADIX, INNER), lambda s, c: (0, 0, 0)),
                pl.BlockSpec((2 * INNER, 4 * LANES), lambda s, c: (0, 0)),
                pl.BlockSpec((2 * INNER, 4 * LANES), lambda s, c: (0, 0)),
            ],
            out_specs=(spec, spec),
            scratch_shapes=[
                pltpu.VMEM((count * rows, 2 * INNER), jnp.bfloat16),
                pltpu.VMEM((count * rows, 2 * INNER), jnp.bfloat16),
                pltpu.VMEM((rows, 2 * HALF_ROWS, LANES), jnp.float32),
            ],
        ),
        compiler_params=pltpu.CompilerParams(vmem_limit_bytes=48 << 20),
        name="whiten",
    )(core, samples, twiddle, upper, lower)


GROUP = 8


def correlate_kernel(count_ref, src_ref, rcv_ref, slot_ref, *refs):
    pieces = refs[:-6]
    table_ref, out_ref, sources_ref, receivers_ref, cross_ref, sems = refs[-6:]
    copies = []
    at = {0: 0, 1: 0}
    for n, piece in enumerate(pieces):
        which = 1 if n >= len(pieces) - 2 else 0
        target = receivers_ref if which else sources_ref
        rows = piece.shape[0]
        copies.append(pltpu.make_async_copy(piece, target.at[at[which]:at[which] + rows], sems.at[n]))
        at[which] += rows
    for copy in copies:
        copy.start()
    cross_ref[...] = jnp.zeros_like(cross_ref)
    for copy in copies:
        copy.wait()

    def group(g, carry):
        for u in range(GROUP):
            i = g * GROUP + u
            a = sources_ref[src_ref[i]].astype(jnp.float32)
            b = receivers_ref[rcv_ref[i]].astype(jnp.float32)
            re = im = None
            for s in range(NSEG):
                ar, ai = a[s * 16:s * 16 + 8], a[s * 16 + 8:s * 16 + 16]
                br, bi = b[s * 16:s * 16 + 8], b[s * 16 + 8:s * 16 + 16]
                r = ar * br + ai * bi
                m = ai * br - ar * bi
                re = r if re is None else re + r
                im = m if im is None else im + m
            slot = slot_ref[i]
            cross_ref[slot, 0:8, :] = re
            cross_ref[slot, 8:16, :] = im
        return carry

    lax.fori_loop(0, (count_ref[0] + GROUP - 1) // GROUP, group, 0)
    slots = out_ref.shape[0]
    chunk = 128
    for c in range(slots // chunk):
        cross = jnp.concatenate(
            [cross_ref[c * chunk:(c + 1) * chunk, g, :].astype(jnp.bfloat16) for g in range(HALF_ROWS)], axis=1
        )
        product = jnp.dot(cross, table_ref[...], preferred_element_type=jnp.float32)
        out_ref[c * chunk:(c + 1) * chunk, :] = product.astype(jnp.bfloat16)


def correlate(count, source_at, receiver_at, slot_at, pieces, table):
    slots = slot_at.shape[0]
    any_spec = pl.BlockSpec(memory_space=pl.ANY)
    row = pieces[0].shape[1:]
    n_src = sum(p.shape[0] for p in pieces[:-2])
    n_rcv = sum(p.shape[0] for p in pieces[-2:])
    return pl.pallas_call(
        correlate_kernel,
        out_shape=jax.ShapeDtypeStruct((slots, NLAG), jnp.bfloat16),
        grid_spec=pltpu.PrefetchScalarGridSpec(
            num_scalar_prefetch=4,
            grid=(1,),
            in_specs=[any_spec] * len(pieces) + [pl.BlockSpec(table.shape, lambda *_: (0, 0))],
            out_specs=pl.BlockSpec((slots, NLAG), lambda *_: (0, 0)),
            scratch_shapes=[
                pltpu.VMEM((n_src,) + row, jnp.bfloat16),
                pltpu.VMEM((n_rcv,) + row, jnp.bfloat16),
                pltpu.VMEM((slots + GROUP, HALF_ROWS, LANES), jnp.float32),
                pltpu.SemaphoreType.DMA((len(pieces),)),
            ],
        ),
        compiler_params=pltpu.CompilerParams(vmem_limit_bytes=48 << 20),
        name="correlate",
    )(count, source_at, receiver_at, slot_at, *pieces, table)


def shift(value, axis, step):
    if axis == "core":
        return lax.ppermute(value, "gx", [(g, g ^ 1) for g in range(2 * SIDE)])
    if axis == "y":
        return lax.ppermute(value, "gx", [(g, (g + 2 * step) % (2 * SIDE)) for g in range(2 * SIDE)])
    if axis == "z":
        return lax.ppermute(value, "gy", [(g, (g + SIDE * step) % (SIDE * SIDE)) for g in range(SIDE * SIDE)])
    return lax.ppermute(value, "gy", [(g, g // SIDE * SIDE + (g + step) % SIDE) for g in range(SIDE * SIDE)])


def gather_ring(value, axis):
    return jnp.stack([value] + [shift(value, axis, d) for d in (1, 2, 3)], axis=0)


def body(raw_window, source_ids, pair_source, pair_holder, pair_receiver):
    groups = lax.axis_size("gy")
    devices = lax.axis_size("gx") * groups
    gx, gy = lax.axis_index("gx"), lax.axis_index("gy")
    place = {"core": gx % 2, "y": gx // 2, "z": gy // SIDE, "x": gy % SIDE}
    core = place["core"]
    here = gx * groups + gy
    span = raw_window.shape[1]
    channels = raw_window.shape[0] // groups
    sample = (gy * span + jnp.arange(span, dtype=jnp.int32)) % SEGLEN
    taper = jnp.sin(math.pi * (sample.astype(jnp.float32) + 0.5) / SEGLEN) ** 2

    pairs = pair_source.shape[0]
    holder = pair_holder[:, 0]
    order = jnp.arange(pairs, dtype=jnp.int32)
    same = (holder[:, None] == holder[None, :]) & (order[None, :] < order[:, None])
    rank = jnp.sum(same.astype(jnp.int32), axis=1)
    packed = ((holder * 2 + rank) * channels + pair_receiver) * 256 + pair_source
    with jax.named_scope("ids"):
        ids = gather_ring(gather_ring(source_ids - gx * groups * channels, "x"), "z")
    with jax.named_scope("requests"):
        notes = gather_ring(gather_ring(packed, "x"), "z")
        notes = gather_ring(notes, "y")
        notes = jnp.stack([notes, shift(notes, "core", 1)], axis=0).reshape(devices, pairs)

    per = source_ids.shape[0]
    step = jnp.arange(groups, dtype=jnp.int32)
    mate = (place["z"] - step // SIDE) % SIDE * SIDE + (place["x"] - step % SIDE) % SIDE
    place_of = jnp.sum(jnp.where(mate[None, :] == step[:, None], step[None, :], 0), axis=1)
    wanted = (ids.reshape(groups, per)[place_of]).reshape(-1)
    with jax.named_scope("early"):
        first = (jnp.take(raw_window, wanted, axis=0) * taper[None, :]).astype(jnp.bfloat16)
        first = jnp.broadcast_to(first[None], (groups,) + first.shape)
        first = lax.all_to_all(first, "gy", split_axis=0, concat_axis=0, tiled=True)
    with jax.named_scope("main"):
        tapered = (raw_window * taper[None, :]).astype(jnp.bfloat16)
        samples = lax.all_to_all(tapered.reshape(groups, channels, span), "gy", split_axis=0, concat_axis=0, tiled=True)

    twiddle = twiddle_table()
    upper, lower = inner_table()
    near0, away = whiten(core.reshape(1), first, twiddle, upper, lower)
    near1 = shift(away, "core", 1)
    ahead0, behind0 = shift(near0, "y", 1), shift(near0, "y", 3)
    ahead1, behind1 = shift(near1, "y", 1), shift(near1, "y", 3)
    far0, far1 = shift(ahead0, "y", 1), shift(behind1, "y", 3)

    late, _ = lax.optimization_barrier((core, near0))
    table = inverse_table(late)

    mine, other = whiten(core.reshape(1), samples, twiddle, upper, lower)
    sister = shift(other, "core", 1)

    dev = jnp.arange(devices, dtype=jnp.int32)
    own = (
        (((dev // 64) ^ core) + (place["y"] - dev // 16 % SIDE) % SIDE * 2) * groups
        + (place["z"] - dev // SIDE % SIDE) % SIDE * SIDE
        + (place["x"] - dev % SIDE) % SIDE
    )
    key = notes // (channels * 256)
    low = notes % (channels * 256)
    kinds = jnp.stack([here * 2, here * 2 + 1, (here ^ groups) * 2, (here ^ groups) * 2 + 1])
    found = jnp.sum(jnp.where(key[None] == kinds[:, None, None], low[None] + 1, 0), axis=2)
    asked = jnp.sum(jnp.where(own[None, None, :] == dev[None, :, None], found[:, None, :], 0), axis=2)
    asked = jnp.transpose(asked.reshape(2, 2, devices), (2, 0, 1)).reshape(-1)
    valid = asked > 0
    asked = jnp.maximum(asked - 1, 0)
    slots = asked.shape[0]
    source_no = asked % 256
    source_gx = source_no // (2 * groups)
    rel_y = (place["y"] - source_gx // 2) % SIDE
    source_at = (rel_y * 2 + (source_gx % 2 ^ core)) * (2 * groups) + source_no % (2 * groups)
    slot_no = jnp.arange(slots, dtype=jnp.int32)
    receiver_at = asked // 256 + slot_no // 2 % 2 * channels
    spot = jnp.sum((valid[None, :] & (slot_no[None, :] < slot_no[:, None])).astype(jnp.int32), axis=1)
    hit = valid[None, :] & (spot[None, :] == slot_no[:, None])
    lists = jnp.sum(jnp.where(hit[None], jnp.stack([source_at, receiver_at, slot_no - slots])[:, None, :], 0), axis=2)
    count = jnp.sum(valid.astype(jnp.int32)).reshape(1)

    pieces = [near0, near1, ahead0, ahead1, far0, far1, behind0, behind1, mine, sister]
    partial = correlate(count, lists[0], lists[1], lists[2] + slots, pieces, table)
    with jax.named_scope("results"):
        returned = lax.all_to_all(partial.reshape(devices, 4, NLAG), ("gx", "gy"), split_axis=0, concat_axis=0, tiled=True)
    returned = returned.reshape(devices * 4, NLAG)
    row = jnp.arange(4 * devices, dtype=jnp.int32)
    row_dev, row_rel, row_rank = row // 4, row // 2 % 2, row % 2
    row_holder = jnp.where(row_rel == 0, row_dev, row_dev ^ groups)
    pick = (row_holder[None, :] == holder[:, None]) & (row_rank[None, :] == rank[:, None])
    return jnp.dot(pick.astype(jnp.bfloat16), returned, preferred_element_type=jnp.float32)


def solution(mesh):
    return jax.shard_map(
        body,
        mesh=mesh,
        in_specs=(
            P("gx", "gy"),
            P(("gx", "gy")),
            P(("gx", "gy")),
            P(("gx", "gy"), None),
            P(("gx", "gy")),
        ),
        out_specs=P(("gx", "gy"), None),
        check_vma=False,
    )
```

```python
import math

import jax
import jax.numpy as jnp
from jax import lax
from jax.experimental import pallas as pl
from jax.experimental.pallas import tpu as pltpu
from jax.sharding import PartitionSpec as P


NBIN = 2048
SEGLEN = 4096
NSEG = 4
BAND = 64
NLAG = 512
SIDE = 4
RADIX = 16
INNER = SEGLEN // RADIX
LANES = 128
HALF_ROWS = 2 * (RADIX // 2)


def split_table(table):
    upper = table.astype(jnp.bfloat16)
    lower = (table - upper.astype(jnp.float32)).astype(jnp.bfloat16)
    return (upper, lower)


def lane_bins():
    lane = jnp.arange(LANES, dtype=jnp.int32)
    return 4 * (lane % 32) + lane // 32


def inner_table():
    times = jnp.arange(INNER, dtype=jnp.int32)
    low = lane_bins()
    high = INNER - 1 - low
    turn = 2.0 * math.pi / INNER

    def block(bins, sign):
        angle = (times[:, None] * bins[None, :] % INNER).astype(jnp.float32) * turn
        cos, sin = jnp.cos(angle), jnp.sin(angle)
        top = jnp.concatenate([cos, -sign * sin], axis=1)
        bottom = jnp.concatenate([sin, sign * cos], axis=1)
        return jnp.concatenate([top, bottom], axis=0)

    return split_table(jnp.concatenate([block(low, 1.0), block(high, -1.0)], axis=1))


def twiddle_table():
    rows = jnp.arange(RADIX, dtype=jnp.int32)
    times = jnp.arange(INNER, dtype=jnp.int32)
    angle = (rows[:, None] * times[None, :] % SEGLEN).astype(jnp.float32) * (2.0 * math.pi / SEGLEN)
    return jnp.stack([jnp.cos(angle), -jnp.sin(angle)], axis=0)


def turns(count, lags):
    angle = (count[:, None] * lags[None, :] % SEGLEN).astype(jnp.float32) * (2.0 * math.pi / SEGLEN)
    return jnp.cos(angle), jnp.sin(angle)


def inverse_table(core, zero):
    outer = core * (RADIX // 2) + jnp.arange(RADIX // 2, dtype=jnp.int32)
    inner = RADIX * lane_bins() + zero
    lags = (jnp.arange(NLAG, dtype=jnp.int32) - NLAG // 2) % SEGLEN
    (c1, s1), (c2, s2) = lax.optimization_barrier((turns(outer, lags), turns(inner, lags)))
    c1, s1, c2, s2 = c1[:, None], s1[:, None], c2[None], s2[None]
    bins = outer[:, None, None] + inner[None, :, None]
    weight = jnp.where(bins == 0, 1.0, 2.0).astype(jnp.float32) * (0.5 / math.sqrt(NSEG * NBIN))
    table = jnp.stack([weight * (c1 * c2 - s1 * s2), -weight * (s1 * c2 + c1 * s2)], axis=0)
    return table.astype(jnp.bfloat16).reshape(NBIN, NLAG)


def real_dft(values):
    n = len(values)
    if n == 2:
        return [(values[0] + values[1], None), (values[0] - values[1], None)]
    even = real_dft(values[0::2])
    odd = real_dft(values[1::2])
    out = [None] * (n // 2 + 1)
    for k in range(n // 4 + 1):
        er, ei = even[k]
        pr, pi = odd[k]
        c, s = math.cos(2 * math.pi * k / n), math.sin(2 * math.pi * k / n)
        if k == 0:
            out[0] = (er + pr, None)
            out[n // 2] = (er - pr, None)
        elif 4 * k == n:
            out[k] = (er, -pr)
        else:
            if 8 * k == n:
                tr, ti = (pr + pi) * c, (pi - pr) * c
            else:
                tr, ti = pr * c + pi * s, pi * c - pr * s
            out[k] = (er + tr, ei + ti)
            out[n // 2 - k] = (er - tr, ti - ei)
    return out


def whiten_kernel(core_ref, x_ref, tw_ref, upper_ref, lower_ref, mine_ref, other_ref, hi_ref, lo_ref, out_ref):
    rows = x_ref.shape[1]
    slices = []
    for t in range(RADIX):
        q, u = t // SIDE, t % SIDE
        slices.append(x_ref[q, :, u * INNER:(u + 1) * INNER].astype(jnp.float32))
    outer = real_dft(slices)
    for f in range(RADIX // 2 + 1):
        re, im = outer[f]
        c, s = tw_ref[0, f:f + 1, :], tw_ref[1, f:f + 1, :]
        if f == 0:
            pair = (re, jnp.zeros_like(re))
        elif im is None:
            pair = (re * c, re * s)
        else:
            pair = (re * c - im * s, re * s + im * c)
        for k in range(2):
            hi = pair[k].astype(jnp.bfloat16)
            hi_ref[f * rows:(f + 1) * rows, k * INNER:(k + 1) * INNER] = hi
            lo_ref[f * rows:(f + 1) * rows, k * INNER:(k + 1) * INNER] = (pair[k] - hi.astype(jnp.float32)).astype(jnp.bfloat16)
    hi, lo = hi_ref[...], lo_ref[...]
    upper, lower = upper_ref[...], lower_ref[...]
    spectrum = jnp.dot(hi, upper, preferred_element_type=jnp.float32)
    spectrum += jnp.dot(hi, lower, preferred_element_type=jnp.float32)
    spectrum += jnp.dot(lo, upper, preferred_element_type=jnp.float32)

    def part(f, k):
        g, base = (f, 0) if f <= RADIX // 2 else (RADIX - f, 2)
        return spectrum[g * rows:(g + 1) * rows, (base + k) * LANES:(base + k + 1) * LANES]

    power = None
    for f in range(RADIX):
        re, im = part(f, 0), part(f, 1)
        both = re * re + im * im
        power = both if power is None else power + both
    power = power + pltpu.roll(power, 64, 1)
    power = power + pltpu.roll(power, 32, 1)
    scale = 1.0 / jnp.sqrt(power * (1.0 / BAND) + 1e-06)
    for f in range(RADIX):
        for k in range(2):
            index = (f // 8) * HALF_ROWS + k * 8 + f % 8
            out_ref[:, index, :] = part(f, k) * scale
    core = core_ref[0]
    mine_ref[...] = out_ref[:, pl.ds(pl.multiple_of(core * HALF_ROWS, HALF_ROWS), HALF_ROWS), :].astype(jnp.bfloat16)
    other_ref[...] = out_ref[:, pl.ds(pl.multiple_of((1 - core) * HALF_ROWS, HALF_ROWS), HALF_ROWS), :].astype(jnp.bfloat16)


def whiten(core, samples, twiddle, upper, lower):
    samples = pltpu.with_memory_space_constraint(samples, pltpu.MemorySpace.HBM)
    rows = samples.shape[1]
    out = jax.ShapeDtypeStruct((rows, NSEG * HALF_ROWS, LANES), jnp.bfloat16)
    spec = pl.BlockSpec((rows, HALF_ROWS, LANES), lambda s, c: (0, s, 0))
    count = RADIX // 2 + 1
    return pl.pallas_call(
        whiten_kernel,
        out_shape=(out, out),
        grid_spec=pltpu.PrefetchScalarGridSpec(
            num_scalar_prefetch=1,
            grid=(NSEG,),
            in_specs=[
                pl.BlockSpec((SIDE, rows, SEGLEN // SIDE), lambda s, c: (s, 0, 0)),
                pl.BlockSpec((2, RADIX, INNER), lambda s, c: (0, 0, 0)),
                pl.BlockSpec((2 * INNER, 4 * LANES), lambda s, c: (0, 0)),
                pl.BlockSpec((2 * INNER, 4 * LANES), lambda s, c: (0, 0)),
            ],
            out_specs=(spec, spec),
            scratch_shapes=[
                pltpu.VMEM((count * rows, 2 * INNER), jnp.bfloat16),
                pltpu.VMEM((count * rows, 2 * INNER), jnp.bfloat16),
                pltpu.VMEM((rows, 2 * HALF_ROWS, LANES), jnp.float32),
            ],
        ),
        compiler_params=pltpu.CompilerParams(vmem_limit_bytes=48 << 20),
        name="whiten",
    )(core, samples, twiddle, upper, lower)


GROUP = 8
CHUNK = 128


def load_pieces(pieces, targets, sems):
    copies = []
    n = 0
    for group, target in zip(pieces, targets):
        at = 0
        for piece in group:
            copies.append(pltpu.make_async_copy(piece, target.at[at:at + piece.shape[0]], sems.at[n]))
            at += piece.shape[0]
            n += 1
    for copy in copies:
        copy.start()
    return copies


def cross_slots(count, src_ref, rcv_ref, row_of, sources_ref, receivers_ref, cross_ref):
    def group(g, carry):
        for u in range(GROUP):
            i = g * GROUP + u
            a = sources_ref[src_ref[i]].astype(jnp.float32)
            b = receivers_ref[rcv_ref[i]].astype(jnp.float32)
            re = im = None
            for s in range(NSEG):
                ar, ai = a[s * 16:s * 16 + 8], a[s * 16 + 8:s * 16 + 16]
                br, bi = b[s * 16:s * 16 + 8], b[s * 16 + 8:s * 16 + 16]
                r = ar * br + ai * bi
                m = ai * br - ar * bi
                re = r if re is None else re + r
                im = m if im is None else im + m
            row = row_of(i)
            cross_ref[row, 0:8, :] = re
            cross_ref[row, 8:16, :] = im
        return carry

    lax.fori_loop(0, (count + GROUP - 1) // GROUP, group, 0)


def lags_of(cross_ref, first, table_ref):
    cross = jnp.concatenate(
        [cross_ref[pl.ds(first, CHUNK), g, :].astype(jnp.bfloat16) for g in range(HALF_ROWS)], axis=1
    )
    return jnp.dot(cross, table_ref[...], preferred_element_type=jnp.float32)


def near_kernel(count_ref, src_ref, rcv_ref, slot_ref, *refs):
    pieces = refs[:8]
    table_ref, out_ref, sources_ref, receivers_ref, cross_ref, sems = refs[8:]
    copies = load_pieces((pieces[:6], pieces[6:]), (sources_ref, receivers_ref), sems)
    cross_ref[...] = jnp.zeros_like(cross_ref)
    for copy in copies:
        copy.wait()
    cross_slots(count_ref[0], src_ref, rcv_ref, lambda i: slot_ref[i], sources_ref, receivers_ref, cross_ref)
    for c in range(out_ref.shape[0] // CHUNK):
        out_ref[c * CHUNK:(c + 1) * CHUNK, :] = lags_of(cross_ref, c * CHUNK, table_ref)


def far_kernel(count_ref, src_ref, rcv_ref, slot_ref, *refs):
    pieces = refs[:4]
    table_ref, near_ref, out_ref, sources_ref, receivers_ref, cross_ref, rows_ref, product_ref, sems = refs[4:]
    copies = load_pieces((pieces[:2], pieces[2:]), (sources_ref, receivers_ref), sems)
    slots = out_ref.shape[0]
    rows_ref[0:slots, :] = near_ref[...]
    for copy in copies:
        copy.wait()
    count = count_ref[0]
    cross_slots(count, src_ref, rcv_ref, lambda i: i, sources_ref, receivers_ref, cross_ref)

    def chunk(c, carry):
        first = pl.multiple_of(c * CHUNK, CHUNK)
        product_ref[...] = lags_of(cross_ref, first, table_ref)

        def place(g, inner):
            for u in range(GROUP):
                i = g * GROUP + u
                rows_ref[pl.ds(slot_ref[first + i], 1), :] = product_ref[pl.ds(i, 1), :]
            return inner

        return lax.fori_loop(0, (jnp.minimum(count - first, CHUNK) + GROUP - 1) // GROUP, place, carry)

    lax.fori_loop(0, (count + CHUNK - 1) // CHUNK, chunk, 0)
    out_ref[...] = rows_ref[0:slots, :].astype(jnp.bfloat16)


def correlate(kernel, lists, pieces, receivers, blocks, dtype, extra):
    slots = lists[1].shape[0]
    row = pieces[0].shape[1:]
    whole = lambda a: pl.BlockSpec(a.shape, lambda *_: (0,) * a.ndim)
    return pl.pallas_call(
        kernel,
        out_shape=jax.ShapeDtypeStruct((slots, NLAG), dtype),
        grid_spec=pltpu.PrefetchScalarGridSpec(
            num_scalar_prefetch=4,
            grid=(1,),
            in_specs=[pl.BlockSpec(memory_space=pl.ANY)] * (len(pieces) + len(receivers)) + [whole(b) for b in blocks],
            out_specs=pl.BlockSpec((slots, NLAG), lambda *_: (0, 0)),
            scratch_shapes=[
                pltpu.VMEM((sum(p.shape[0] for p in pieces),) + row, jnp.bfloat16),
                pltpu.VMEM((sum(p.shape[0] for p in receivers),) + row, jnp.bfloat16),
                pltpu.VMEM((slots + GROUP, HALF_ROWS, LANES), jnp.float32),
                *extra,
                pltpu.SemaphoreType.DMA((len(pieces) + len(receivers),)),
            ],
        ),
        compiler_params=pltpu.CompilerParams(vmem_limit_bytes=40 << 20),
    )(*lists, *pieces, *receivers, *blocks)


def pick_kernel(wanted_ref, raw_ref, taper_ref, out_ref, rows_ref, sems):
    rows = rows_ref.shape[0]
    copies = [
        pltpu.make_async_copy(raw_ref.at[pl.ds(wanted_ref[r], 1), :], rows_ref.at[pl.ds(r, 1), :], sems.at[r])
        for r in range(rows)
    ]
    for copy in copies:
        copy.start()
    for copy in copies:
        copy.wait()
    value = (rows_ref[...] * taper_ref[...]).astype(jnp.bfloat16)
    for g in range(out_ref.shape[0]):
        out_ref[g] = value


def pick_rows(wanted, raw_window, taper, copies):
    rows, span = wanted.shape[0], raw_window.shape[1]
    return pl.pallas_call(
        pick_kernel,
        out_shape=jax.ShapeDtypeStruct((copies, rows, span), jnp.bfloat16),
        grid_spec=pltpu.PrefetchScalarGridSpec(
            num_scalar_prefetch=1,
            grid=(1,),
            in_specs=[pl.BlockSpec(memory_space=pl.ANY), pl.BlockSpec((1, span), lambda *_: (0, 0))],
            out_specs=pl.BlockSpec((copies, rows, span), lambda *_: (0, 0, 0)),
            scratch_shapes=[pltpu.VMEM((rows, span), jnp.float32), pltpu.SemaphoreType.DMA((rows,))],
        ),
        name="pick",
    )(wanted, raw_window, taper.reshape(1, span))


def taper_kernel(raw_ref, taper_ref, out_ref):
    out_ref[...] = (raw_ref[...] * taper_ref[...]).astype(jnp.bfloat16)


def taper_rows(raw_window, taper):
    rows, span = raw_window.shape
    block = rows // 8
    return pl.pallas_call(
        taper_kernel,
        out_shape=jax.ShapeDtypeStruct((rows, span), jnp.bfloat16),
        grid=(rows // block,),
        in_specs=[pl.BlockSpec((block, span), lambda i: (i, 0)), pl.BlockSpec((1, span), lambda i: (0, 0))],
        out_specs=pl.BlockSpec((block, span), lambda i: (i, 0)),
        name="taper",
    )(raw_window, taper.reshape(1, span))


def shift(value, axis, step):
    if axis == "core":
        return lax.ppermute(value, "gx", [(g, g ^ 1) for g in range(2 * SIDE)])
    if axis == "y":
        return lax.ppermute(value, "gx", [(g, (g + 2 * step) % (2 * SIDE)) for g in range(2 * SIDE)])
    if axis == "z":
        return lax.ppermute(value, "gy", [(g, (g + SIDE * step) % (SIDE * SIDE)) for g in range(SIDE * SIDE)])
    return lax.ppermute(value, "gy", [(g, g // SIDE * SIDE + (g + step) % SIDE) for g in range(SIDE * SIDE)])


def gather_ring(value, axis):
    return jnp.stack([value] + [shift(value, axis, d) for d in (1, 2, 3)], axis=0)


def program(raw_window, source_ids, pair_source, pair_holder, pair_receiver):
    groups = lax.axis_size("gy")
    devices = lax.axis_size("gx") * groups
    gx, gy = lax.axis_index("gx"), lax.axis_index("gy")
    place = {"core": gx % 2, "y": gx // 2, "z": gy // SIDE, "x": gy % SIDE}
    core = place["core"]
    here = gx * groups + gy
    span = raw_window.shape[1]
    channels = raw_window.shape[0] // groups
    sample = (gy * span + jnp.arange(span, dtype=jnp.int32)) % SEGLEN
    taper = jnp.sin(math.pi * (sample.astype(jnp.float32) + 0.5) / SEGLEN) ** 2

    pairs = pair_source.shape[0]
    per = source_ids.shape[0]
    holder = pair_holder[:, 0]
    order = jnp.arange(pairs, dtype=jnp.int32)
    same = (holder[:, None] == holder[None, :]) & (order[None, :] < order[:, None])
    rank = jnp.sum(same.astype(jnp.int32), axis=1)
    packed = ((holder * 2 + rank) * channels + pair_receiver) * 256 + pair_source
    notes = jnp.concatenate([packed, source_ids - gx * groups * channels])
    notes = gather_ring(notes, "x")
    notes = gather_ring(notes, "z")
    ids, notes = notes[:, :, pairs:].reshape(groups, per), notes[:, :, :pairs]

    step = jnp.arange(groups, dtype=jnp.int32)
    mate = (place["z"] - step // SIDE) % SIDE * SIDE + (place["x"] - step % SIDE) % SIDE
    wanted = jnp.sum(jnp.where(mate[None, :, None] == step[:, None, None], ids[None], 0), axis=1).reshape(-1)
    first = pick_rows(wanted, raw_window, taper, groups)
    first = lax.all_to_all(first, "gy", split_axis=0, concat_axis=0, tiled=True)
    tapered = taper_rows(raw_window, taper)
    samples = lax.all_to_all(tapered.reshape(groups, channels, span), "gy", split_axis=0, concat_axis=0, tiled=True)
    notes = gather_ring(notes, "y")
    notes = jnp.stack([notes, shift(notes, "core", 1)], axis=0).reshape(devices, pairs)

    twiddle = twiddle_table()
    upper, lower = inner_table()
    near0, away = whiten(core.reshape(1), first, twiddle, upper, lower)
    near1 = shift(away, "core", 1)
    ahead0 = shift(near0, "y", 1)
    behind0 = shift(near0, "y", 3)
    ahead1 = shift(near1, "y", 1)
    behind1 = shift(near1, "y", 3)
    far0 = shift(ahead0, "y", 1)
    far1 = shift(behind1, "y", 3)

    notes, late, _ = lax.optimization_barrier((notes, core, near1))
    table = inverse_table(late, late - core)

    mine, other = whiten(core.reshape(1), samples, twiddle, upper, lower)
    sister = shift(other, "core", 1)

    dev = jnp.arange(devices, dtype=jnp.int32)
    own = (
        (((dev // 64) ^ late) + (place["y"] - dev // 16 % SIDE) % SIDE * 2) * groups
        + (place["z"] - dev // SIDE % SIDE) % SIDE * SIDE
        + (place["x"] - dev % SIDE) % SIDE
    )
    key = notes // (channels * 256)
    low = notes % (channels * 256)
    kinds = jnp.stack([here * 2, here * 2 + 1, (here ^ groups) * 2, (here ^ groups) * 2 + 1])
    found = jnp.sum(jnp.where(key[None] == kinds[:, None, None], low[None] + 1, 0), axis=2)
    asked = jnp.sum(jnp.where(own[None, None, :] == dev[None, :, None], found[:, None, :], 0), axis=2)
    valid = asked > 0
    asked = jnp.maximum(asked - 1, 0)
    slots = asked.size
    source_no = asked % 256
    source_gx = source_no // (2 * groups)
    rel_y = (place["y"] - source_gx // 2) % SIDE
    far = rel_y == 2
    piece = jnp.where(far, 0, jnp.minimum(rel_y, 2))
    source_at = (piece * 2 + (source_gx % 2 ^ core)) * (2 * groups) + source_no % (2 * groups)
    kind = jnp.arange(4, dtype=jnp.int32)[:, None]
    slot_no = dev[None, :] * 4 + kind
    receiver_at = asked // 256 + kind // 2 * channels
    entry = ((slot_no - slots) * 256 + receiver_at) * 256 + source_at
    index = jnp.arange(slots, dtype=jnp.int32)

    def compact(chosen):
        chosen = chosen.reshape(-1)
        spot = jnp.sum((chosen[None, :] & (index[None, :] < index[:, None])).astype(jnp.int32), axis=1)
        hit = chosen[None, :] & (spot[None, :] == index[:, None])
        line = jnp.sum(jnp.where(hit, entry.reshape(1, -1), 0), axis=1) + slots * 65536
        return jnp.sum(chosen.astype(jnp.int32)).reshape(1), line % 256, line // 256 % 256, line // 65536

    near_lists = compact(valid & ~far)
    far_lists = compact(valid & far)

    receivers = [mine, sister]
    near = correlate(
        near_kernel, near_lists, [near0, near1, ahead0, ahead1, behind0, behind1], receivers, [table], jnp.float32, []
    )
    extra = [pltpu.VMEM((slots + GROUP, NLAG), jnp.float32), pltpu.VMEM((CHUNK, NLAG), jnp.float32)]
    partial = correlate(far_kernel, far_lists, [far0, far1], receivers, [table, near], jnp.bfloat16, extra)
    returned = lax.all_to_all(partial.reshape(devices, 4, NLAG), ("gx", "gy"), split_axis=0, concat_axis=0, tiled=True)
    returned = returned.reshape(devices * 4, NLAG)
    row = jnp.arange(4 * devices, dtype=jnp.int32)
    row_dev, row_rel, row_rank = row // 4, row // 2 % 2, row % 2
    row_holder = jnp.where(row_rel == 0, row_dev, row_dev ^ groups)
    pick = (row_holder[None, :] == holder[:, None]) & (row_rank[None, :] == rank[:, None])
    return jnp.dot(pick.astype(jnp.bfloat16), returned, preferred_element_type=jnp.float32)


def solution(mesh):
    return jax.shard_map(
        program,
        mesh=mesh,
        in_specs=(
            P("gx", "gy"),
            P(("gx", "gy")),
            P(("gx", "gy")),
            P(("gx", "gy"), None),
            P(("gx", "gy")),
        ),
        out_specs=P(("gx", "gy"), None),
        check_vma=False,
    )
```

```python
import math

import jax
import jax.numpy as jnp
from jax import lax
from jax.experimental import pallas as pl
from jax.experimental.pallas import tpu as pltpu
from jax.sharding import PartitionSpec as P


NBIN = 2048
SEGLEN = 4096
NSEG = 4
BAND = 64
NLAG = 512
SIDE = 4
RADIX = 16
INNER = SEGLEN // RADIX
LANES = 128
HALF_ROWS = 2 * (RADIX // 2)


def split_table(table):
    upper = table.astype(jnp.bfloat16)
    lower = (table - upper.astype(jnp.float32)).astype(jnp.bfloat16)
    return (upper, lower)


def lane_bins():
    lane = jnp.arange(LANES, dtype=jnp.int32)
    return 4 * (lane % 32) + lane // 32


def inner_table():
    times = jnp.arange(INNER, dtype=jnp.int32)
    low = lane_bins()
    high = INNER - 1 - low
    turn = 2.0 * math.pi / INNER

    def block(bins, sign):
        angle = (times[:, None] * bins[None, :] % INNER).astype(jnp.float32) * turn
        cos, sin = jnp.cos(angle), jnp.sin(angle)
        top = jnp.concatenate([cos, -sign * sin], axis=1)
        bottom = jnp.concatenate([sin, sign * cos], axis=1)
        return jnp.concatenate([top, bottom], axis=0)

    return split_table(jnp.concatenate([block(low, 1.0), block(high, -1.0)], axis=1))


def twiddle_table():
    rows = jnp.arange(RADIX, dtype=jnp.int32)
    times = jnp.arange(INNER, dtype=jnp.int32)
    angle = (rows[:, None] * times[None, :] % SEGLEN).astype(jnp.float32) * (2.0 * math.pi / SEGLEN)
    return jnp.stack([jnp.cos(angle), -jnp.sin(angle)], axis=0)


def turns(count, lags):
    angle = (count[:, None] * lags[None, :] % SEGLEN).astype(jnp.float32) * (2.0 * math.pi / SEGLEN)
    return jnp.cos(angle), jnp.sin(angle)


def inverse_table(core, zero):
    outer = core * (RADIX // 2) + jnp.arange(RADIX // 2, dtype=jnp.int32)
    inner = RADIX * lane_bins() + zero
    lags = (jnp.arange(NLAG, dtype=jnp.int32) - NLAG // 2) % SEGLEN
    (c1, s1), (c2, s2) = lax.optimization_barrier((turns(outer, lags), turns(inner, lags)))
    c1, s1, c2, s2 = c1[:, None], s1[:, None], c2[None], s2[None]
    bins = outer[:, None, None] + inner[None, :, None]
    weight = jnp.where(bins == 0, 1.0, 2.0).astype(jnp.float32) * (0.5 / math.sqrt(NSEG * NBIN))
    table = jnp.stack([weight * (c1 * c2 - s1 * s2), -weight * (s1 * c2 + c1 * s2)], axis=0)
    return table.astype(jnp.bfloat16).reshape(NBIN, NLAG)


def real_dft(values):
    n = len(values)
    if n == 2:
        return [(values[0] + values[1], None), (values[0] - values[1], None)]
    even = real_dft(values[0::2])
    odd = real_dft(values[1::2])
    out = [None] * (n // 2 + 1)
    for k in range(n // 4 + 1):
        er, ei = even[k]
        pr, pi = odd[k]
        c, s = math.cos(2 * math.pi * k / n), math.sin(2 * math.pi * k / n)
        if k == 0:
            out[0] = (er + pr, None)
            out[n // 2] = (er - pr, None)
        elif 4 * k == n:
            out[k] = (er, -pr)
        else:
            if 8 * k == n:
                tr, ti = (pr + pi) * c, (pi - pr) * c
            else:
                tr, ti = pr * c + pi * s, pi * c - pr * s
            out[k] = (er + tr, ei + ti)
            out[n // 2 - k] = (er - tr, ti - ei)
    return out


def whiten_kernel(core_ref, x_ref, tw_ref, upper_ref, lower_ref, mine_ref, other_ref, hi_ref, lo_ref, out_ref):
    rows = x_ref.shape[1]
    slices = []
    for t in range(RADIX):
        q, u = t // SIDE, t % SIDE
        slices.append(x_ref[q, :, u * INNER:(u + 1) * INNER].astype(jnp.float32))
    outer = real_dft(slices)
    for f in range(RADIX // 2 + 1):
        re, im = outer[f]
        c, s = tw_ref[0, f:f + 1, :], tw_ref[1, f:f + 1, :]
        if f == 0:
            pair = (re, jnp.zeros_like(re))
        elif im is None:
            pair = (re * c, re * s)
        else:
            pair = (re * c - im * s, re * s + im * c)
        for k in range(2):
            hi = pair[k].astype(jnp.bfloat16)
            hi_ref[f * rows:(f + 1) * rows, k * INNER:(k + 1) * INNER] = hi
            lo_ref[f * rows:(f + 1) * rows, k * INNER:(k + 1) * INNER] = (pair[k] - hi.astype(jnp.float32)).astype(jnp.bfloat16)
    hi, lo = hi_ref[...], lo_ref[...]
    upper, lower = upper_ref[...], lower_ref[...]
    spectrum = jnp.dot(hi, upper, preferred_element_type=jnp.float32)
    spectrum += jnp.dot(hi, lower, preferred_element_type=jnp.float32)
    spectrum += jnp.dot(lo, upper, preferred_element_type=jnp.float32)

    def part(f, k):
        g, base = (f, 0) if f <= RADIX // 2 else (RADIX - f, 2)
        return spectrum[g * rows:(g + 1) * rows, (base + k) * LANES:(base + k + 1) * LANES]

    power = None
    for f in range(RADIX):
        re, im = part(f, 0), part(f, 1)
        both = re * re + im * im
        power = both if power is None else power + both
    power = power + pltpu.roll(power, 64, 1)
    power = power + pltpu.roll(power, 32, 1)
    scale = 1.0 / jnp.sqrt(power * (1.0 / BAND) + 1e-06)
    for f in range(RADIX):
        for k in range(2):
            index = (f // 8) * HALF_ROWS + k * 8 + f % 8
            out_ref[:, index, :] = part(f, k) * scale
    core = core_ref[0]
    mine_ref[...] = out_ref[:, pl.ds(pl.multiple_of(core * HALF_ROWS, HALF_ROWS), HALF_ROWS), :].astype(jnp.bfloat16)
    other_ref[...] = out_ref[:, pl.ds(pl.multiple_of((1 - core) * HALF_ROWS, HALF_ROWS), HALF_ROWS), :].astype(jnp.bfloat16)


def whiten(core, samples, twiddle, upper, lower):
    samples = pltpu.with_memory_space_constraint(samples, pltpu.MemorySpace.HBM)
    rows = samples.shape[1]
    out = jax.ShapeDtypeStruct((rows, NSEG * HALF_ROWS, LANES), jnp.bfloat16)
    spec = pl.BlockSpec((rows, HALF_ROWS, LANES), lambda s, c: (0, s, 0))
    count = RADIX // 2 + 1
    return pl.pallas_call(
        whiten_kernel,
        out_shape=(out, out),
        grid_spec=pltpu.PrefetchScalarGridSpec(
            num_scalar_prefetch=1,
            grid=(NSEG,),
            in_specs=[
                pl.BlockSpec((SIDE, rows, SEGLEN // SIDE), lambda s, c: (s, 0, 0)),
                pl.BlockSpec((2, RADIX, INNER), lambda s, c: (0, 0, 0)),
                pl.BlockSpec((2 * INNER, 4 * LANES), lambda s, c: (0, 0)),
                pl.BlockSpec((2 * INNER, 4 * LANES), lambda s, c: (0, 0)),
            ],
            out_specs=(spec, spec),
            scratch_shapes=[
                pltpu.VMEM((count * rows, 2 * INNER), jnp.bfloat16),
                pltpu.VMEM((count * rows, 2 * INNER), jnp.bfloat16),
                pltpu.VMEM((rows, 2 * HALF_ROWS, LANES), jnp.float32),
            ],
        ),
        compiler_params=pltpu.CompilerParams(vmem_limit_bytes=48 << 20),
        name="whiten",
    )(core, samples, twiddle, upper, lower)


GROUP = 8
CHUNK = 128


def load_pieces(pieces, targets, sems):
    copies = []
    n = 0
    for group, target in zip(pieces, targets):
        at = 0
        for piece in group:
            copies.append(pltpu.make_async_copy(piece, target.at[at:at + piece.shape[0]], sems.at[n]))
            at += piece.shape[0]
            n += 1
    for copy in copies:
        copy.start()
    return copies


def cross_slots(count, src_ref, rcv_ref, row_of, sources_ref, receivers_ref, cross_ref):
    def group(g, carry):
        for u in range(GROUP):
            i = g * GROUP + u
            a = sources_ref[src_ref[i]].astype(jnp.float32)
            b = receivers_ref[rcv_ref[i]].astype(jnp.float32)
            re = im = None
            for s in range(NSEG):
                ar, ai = a[s * 16:s * 16 + 8], a[s * 16 + 8:s * 16 + 16]
                br, bi = b[s * 16:s * 16 + 8], b[s * 16 + 8:s * 16 + 16]
                r = ar * br + ai * bi
                m = ai * br - ar * bi
                re = r if re is None else re + r
                im = m if im is None else im + m
            row = row_of(i)
            cross_ref[row, 0:8, :] = re
            cross_ref[row, 8:16, :] = im
        return carry

    lax.fori_loop(0, (count + GROUP - 1) // GROUP, group, 0)


def lags_of(cross_ref, first, table_ref):
    cross = jnp.concatenate(
        [cross_ref[pl.ds(first, CHUNK), g, :].astype(jnp.bfloat16) for g in range(HALF_ROWS)], axis=1
    )
    return jnp.dot(cross, table_ref[...], preferred_element_type=jnp.float32)


def near_kernel(count_ref, src_ref, rcv_ref, slot_ref, *refs):
    pieces = refs[:8]
    table_ref, out_ref, sources_ref, receivers_ref, cross_ref, sems = refs[8:]
    copies = load_pieces((pieces[:6], pieces[6:]), (sources_ref, receivers_ref), sems)
    cross_ref[...] = jnp.zeros_like(cross_ref)
    for copy in copies:
        copy.wait()
    cross_slots(count_ref[0], src_ref, rcv_ref, lambda i: slot_ref[i], sources_ref, receivers_ref, cross_ref)
    for c in range(out_ref.shape[0] // CHUNK):
        out_ref[c * CHUNK:(c + 1) * CHUNK, :] = lags_of(cross_ref, c * CHUNK, table_ref)


def far_kernel(count_ref, src_ref, rcv_ref, slot_ref, *refs):
    pieces = refs[:4]
    table_ref, near_ref, out_ref, sources_ref, receivers_ref, cross_ref, rows_ref, product_ref, sems = refs[4:]
    copies = load_pieces((pieces[:2], pieces[2:]), (sources_ref, receivers_ref), sems)
    slots = out_ref.shape[0]
    rows_ref[0:slots, :] = near_ref[...]
    for copy in copies:
        copy.wait()
    count = count_ref[0]
    cross_slots(count, src_ref, rcv_ref, lambda i: i, sources_ref, receivers_ref, cross_ref)

    def chunk(c, carry):
        first = pl.multiple_of(c * CHUNK, CHUNK)
        product_ref[...] = lags_of(cross_ref, first, table_ref)

        def place(g, inner):
            for u in range(GROUP):
                i = g * GROUP + u
                rows_ref[pl.ds(slot_ref[first + i], 1), :] = product_ref[pl.ds(i, 1), :]
            return inner

        return lax.fori_loop(0, (jnp.minimum(count - first, CHUNK) + GROUP - 1) // GROUP, place, carry)

    lax.fori_loop(0, (count + CHUNK - 1) // CHUNK, chunk, 0)
    out_ref[...] = rows_ref[0:slots, :].astype(jnp.bfloat16)


def correlate(kernel, lists, pieces, receivers, blocks, dtype, extra):
    slots = lists[1].shape[0]
    row = pieces[0].shape[1:]
    whole = lambda a: pl.BlockSpec(a.shape, lambda *_: (0,) * a.ndim)
    return pl.pallas_call(
        kernel,
        out_shape=jax.ShapeDtypeStruct((slots, NLAG), dtype),
        grid_spec=pltpu.PrefetchScalarGridSpec(
            num_scalar_prefetch=4,
            grid=(1,),
            in_specs=[pl.BlockSpec(memory_space=pl.ANY)] * (len(pieces) + len(receivers)) + [whole(b) for b in blocks],
            out_specs=pl.BlockSpec((slots, NLAG), lambda *_: (0, 0)),
            scratch_shapes=[
                pltpu.VMEM((sum(p.shape[0] for p in pieces),) + row, jnp.bfloat16),
                pltpu.VMEM((sum(p.shape[0] for p in receivers),) + row, jnp.bfloat16),
                pltpu.VMEM((slots + GROUP, HALF_ROWS, LANES), jnp.float32),
                *extra,
                pltpu.SemaphoreType.DMA((len(pieces) + len(receivers),)),
            ],
        ),
        compiler_params=pltpu.CompilerParams(vmem_limit_bytes=40 << 20),
    )(*lists, *pieces, *receivers, *blocks)


def pick_kernel(wanted_ref, raw_ref, taper_ref, out_ref, rows_ref, sems):
    rows = rows_ref.shape[0]
    copies = [
        pltpu.make_async_copy(raw_ref.at[pl.ds(wanted_ref[r], 1), :], rows_ref.at[pl.ds(r, 1), :], sems.at[r])
        for r in range(rows)
    ]
    for copy in copies:
        copy.start()
    for copy in copies:
        copy.wait()
    value = (rows_ref[...] * taper_ref[...]).astype(jnp.bfloat16)
    for g in range(out_ref.shape[0]):
        out_ref[g] = value


def pick_rows(wanted, raw_window, taper, copies):
    rows, span = wanted.shape[0], raw_window.shape[1]
    return pl.pallas_call(
        pick_kernel,
        out_shape=jax.ShapeDtypeStruct((copies, rows, span), jnp.bfloat16),
        grid_spec=pltpu.PrefetchScalarGridSpec(
            num_scalar_prefetch=1,
            grid=(1,),
            in_specs=[pl.BlockSpec(memory_space=pl.ANY), pl.BlockSpec((1, span), lambda *_: (0, 0))],
            out_specs=pl.BlockSpec((copies, rows, span), lambda *_: (0, 0, 0)),
            scratch_shapes=[pltpu.VMEM((rows, span), jnp.float32), pltpu.SemaphoreType.DMA((rows,))],
        ),
        name="pick",
    )(wanted, raw_window, taper.reshape(1, span))


def shift(value, axis, step):
    if axis == "core":
        return lax.ppermute(value, "gx", [(g, g ^ 1) for g in range(2 * SIDE)])
    if axis == "y":
        return lax.ppermute(value, "gx", [(g, (g + 2 * step) % (2 * SIDE)) for g in range(2 * SIDE)])
    if axis == "z":
        return lax.ppermute(value, "gy", [(g, (g + SIDE * step) % (SIDE * SIDE)) for g in range(SIDE * SIDE)])
    return lax.ppermute(value, "gy", [(g, g // SIDE * SIDE + (g + step) % SIDE) for g in range(SIDE * SIDE)])


def gather_ring(value, axis):
    return jnp.stack([value] + [shift(value, axis, d) for d in (1, 2, 3)], axis=0)


def program(raw_window, source_ids, pair_source, pair_holder, pair_receiver):
    groups = lax.axis_size("gy")
    devices = lax.axis_size("gx") * groups
    gx, gy = lax.axis_index("gx"), lax.axis_index("gy")
    place = {"core": gx % 2, "y": gx // 2, "z": gy // SIDE, "x": gy % SIDE}
    core = place["core"]
    here = gx * groups + gy
    span = raw_window.shape[1]
    channels = raw_window.shape[0] // groups
    sample = (gy * span + jnp.arange(span, dtype=jnp.int32)) % SEGLEN
    taper = jnp.sin(math.pi * (sample.astype(jnp.float32) + 0.5) / SEGLEN) ** 2

    pairs = pair_source.shape[0]
    per = source_ids.shape[0]
    holder = pair_holder[:, 0]
    order = jnp.arange(pairs, dtype=jnp.int32)
    same = (holder[:, None] == holder[None, :]) & (order[None, :] < order[:, None])
    rank = jnp.sum(same.astype(jnp.int32), axis=1)
    packed = ((holder * 2 + rank) * channels + pair_receiver) * 256 + pair_source
    notes = jnp.concatenate([packed, source_ids - gx * groups * channels])
    notes = gather_ring(notes, "x")
    notes = gather_ring(notes, "z")
    ids, notes = notes[:, :, pairs:].reshape(groups, per), notes[:, :, :pairs]

    step = jnp.arange(groups, dtype=jnp.int32)
    mate = (place["z"] - step // SIDE) % SIDE * SIDE + (place["x"] - step % SIDE) % SIDE
    wanted = jnp.sum(jnp.where(mate[None, :, None] == step[:, None, None], ids[None], 0), axis=1).reshape(-1)
    first = pick_rows(wanted, raw_window, taper, groups)
    first = lax.all_to_all(first, "gy", split_axis=0, concat_axis=0, tiled=True)
    tapered = (raw_window * taper[None, :]).astype(jnp.bfloat16)
    samples = lax.all_to_all(tapered.reshape(groups, channels, span), "gy", split_axis=0, concat_axis=0, tiled=True)
    notes = gather_ring(notes, "y")
    notes = jnp.stack([notes, shift(notes, "core", 1)], axis=0).reshape(devices, pairs)

    twiddle = twiddle_table()
    upper, lower = inner_table()
    near0, away = whiten(core.reshape(1), first, twiddle, upper, lower)
    near1 = shift(away, "core", 1)
    ahead0 = shift(near0, "y", 1)
    behind0 = shift(near0, "y", 3)
    ahead1 = shift(near1, "y", 1)
    behind1 = shift(near1, "y", 3)
    far0 = shift(ahead0, "y", 1)
    far1 = shift(behind1, "y", 3)

    notes, late, _ = lax.optimization_barrier((notes, core, near1))
    table = inverse_table(late, late - core)

    mine, other = whiten(core.reshape(1), samples, twiddle, upper, lower)
    sister = shift(other, "core", 1)

    dev = jnp.arange(devices, dtype=jnp.int32)
    own = (
        (((dev // 64) ^ late) + (place["y"] - dev // 16 % SIDE) % SIDE * 2) * groups
        + (place["z"] - dev // SIDE % SIDE) % SIDE * SIDE
        + (place["x"] - dev % SIDE) % SIDE
    )
    key = notes // (channels * 256)
    low = notes % (channels * 256)
    kinds = jnp.stack([here * 2, here * 2 + 1, (here ^ groups) * 2, (here ^ groups) * 2 + 1])
    found = jnp.sum(jnp.where(key[None] == kinds[:, None, None], low[None] + 1, 0), axis=2)
    asked = jnp.sum(jnp.where(own[None, None, :] == dev[None, :, None], found[:, None, :], 0), axis=2)
    valid = asked > 0
    asked = jnp.maximum(asked - 1, 0)
    slots = asked.size
    source_no = asked % 256
    source_gx = source_no // (2 * groups)
    rel_y = (place["y"] - source_gx // 2) % SIDE
    far = rel_y == 2
    piece = jnp.where(far, 0, jnp.minimum(rel_y, 2))
    source_at = (piece * 2 + (source_gx % 2 ^ core)) * (2 * groups) + source_no % (2 * groups)
    kind = jnp.arange(4, dtype=jnp.int32)[:, None]
    slot_no = dev[None, :] * 4 + kind
    receiver_at = asked // 256 + kind // 2 * channels
    entry = ((slot_no - slots) * 256 + receiver_at) * 256 + source_at
    index = jnp.arange(slots, dtype=jnp.int32)

    def compact(chosen):
        chosen = chosen.reshape(-1)
        spot = jnp.sum((chosen[None, :] & (index[None, :] < index[:, None])).astype(jnp.int32), axis=1)
        hit = chosen[None, :] & (spot[None, :] == index[:, None])
        line = jnp.sum(jnp.where(hit, entry.reshape(1, -1), 0), axis=1) + slots * 65536
        return jnp.sum(chosen.astype(jnp.int32)).reshape(1), line % 256, line // 256 % 256, line // 65536

    near_lists = compact(valid & ~far)
    far_lists = compact(valid & far)

    receivers = [mine, sister]
    near = correlate(
        near_kernel, near_lists, [near0, near1, ahead0, ahead1, behind0, behind1], receivers, [table], jnp.float32, []
    )
    extra = [pltpu.VMEM((slots + GROUP, NLAG), jnp.float32), pltpu.VMEM((CHUNK, NLAG), jnp.float32)]
    partial = correlate(far_kernel, far_lists, [far0, far1], receivers, [table, near], jnp.bfloat16, extra)
    returned = lax.all_to_all(partial.reshape(devices, 4, NLAG), ("gx", "gy"), split_axis=0, concat_axis=0, tiled=True)
    returned = returned.reshape(devices * 4, NLAG)
    row = jnp.arange(4 * devices, dtype=jnp.int32)
    row_dev, row_rel, row_rank = row // 4, row // 2 % 2, row % 2
    row_holder = jnp.where(row_rel == 0, row_dev, row_dev ^ groups)
    pick = (row_holder[None, :] == holder[:, None]) & (row_rank[None, :] == rank[:, None])
    return jnp.dot(pick.astype(jnp.bfloat16), returned, preferred_element_type=jnp.float32)


def solution(mesh):
    return jax.shard_map(
        program,
        mesh=mesh,
        in_specs=(
            P("gx", "gy"),
            P(("gx", "gy")),
            P(("gx", "gy")),
            P(("gx", "gy"), None),
            P(("gx", "gy")),
        ),
        out_specs=P(("gx", "gy"), None),
        check_vma=False,
    )
```

```python
import math

import jax
import jax.numpy as jnp
from jax import lax
from jax.experimental import pallas as pl
from jax.experimental.pallas import tpu as pltpu
from jax.sharding import PartitionSpec as P


NBIN = 2048
SEGLEN = 4096
NSEG = 4
BAND = 64
NLAG = 512
SIDE = 4
RADIX = 16
INNER = SEGLEN // RADIX
LANES = 128
HALF_ROWS = 2 * (RADIX // 2)


def split_table(table):
    upper = table.astype(jnp.bfloat16)
    lower = (table - upper.astype(jnp.float32)).astype(jnp.bfloat16)
    return (upper, lower)


def lane_bins():
    lane = jnp.arange(LANES, dtype=jnp.int32)
    return 4 * (lane % 32) + lane // 32


def inner_table():
    times = jnp.arange(INNER, dtype=jnp.int32)
    low = lane_bins()
    high = INNER - 1 - low
    turn = 2.0 * math.pi / INNER

    def block(bins, sign):
        angle = (times[:, None] * bins[None, :] % INNER).astype(jnp.float32) * turn
        cos, sin = jnp.cos(angle), jnp.sin(angle)
        top = jnp.concatenate([cos, -sign * sin], axis=1)
        bottom = jnp.concatenate([sin, sign * cos], axis=1)
        return jnp.concatenate([top, bottom], axis=0)

    return split_table(jnp.concatenate([block(low, 1.0), block(high, -1.0)], axis=1))


def twiddle_table():
    rows = jnp.arange(RADIX, dtype=jnp.int32)
    times = jnp.arange(INNER, dtype=jnp.int32)
    angle = (rows[:, None] * times[None, :] % SEGLEN).astype(jnp.float32) * (2.0 * math.pi / SEGLEN)
    return jnp.stack([jnp.cos(angle), -jnp.sin(angle)], axis=0)


def turns(count, lags):
    angle = (count[:, None] * lags[None, :] % SEGLEN).astype(jnp.float32) * (2.0 * math.pi / SEGLEN)
    return jnp.cos(angle), jnp.sin(angle)


def inverse_table(core, zero):
    outer = core * (RADIX // 2) + jnp.arange(RADIX // 2, dtype=jnp.int32)
    inner = RADIX * lane_bins() + zero
    lags = (jnp.arange(NLAG, dtype=jnp.int32) - NLAG // 2) % SEGLEN
    (c1, s1), (c2, s2) = lax.optimization_barrier((turns(outer, lags), turns(inner, lags)))
    c1, s1, c2, s2 = c1[:, None], s1[:, None], c2[None], s2[None]
    bins = outer[:, None, None] + inner[None, :, None]
    weight = jnp.where(bins == 0, 1.0, 2.0).astype(jnp.float32) * (0.5 / math.sqrt(NSEG * NBIN))
    table = jnp.stack([weight * (c1 * c2 - s1 * s2), -weight * (s1 * c2 + c1 * s2)], axis=0)
    return table.astype(jnp.bfloat16).reshape(NBIN, NLAG)


def real_dft(values):
    n = len(values)
    if n == 2:
        return [(values[0] + values[1], None), (values[0] - values[1], None)]
    even = real_dft(values[0::2])
    odd = real_dft(values[1::2])
    out = [None] * (n // 2 + 1)
    for k in range(n // 4 + 1):
        er, ei = even[k]
        pr, pi = odd[k]
        c, s = math.cos(2 * math.pi * k / n), math.sin(2 * math.pi * k / n)
        if k == 0:
            out[0] = (er + pr, None)
            out[n // 2] = (er - pr, None)
        elif 4 * k == n:
            out[k] = (er, -pr)
        else:
            if 8 * k == n:
                tr, ti = (pr + pi) * c, (pi - pr) * c
            else:
                tr, ti = pr * c + pi * s, pi * c - pr * s
            out[k] = (er + tr, ei + ti)
            out[n // 2 - k] = (er - tr, ti - ei)
    return out


def whiten_kernel(core_ref, x_ref, tw_ref, upper_ref, lower_ref, mine_ref, other_ref, hi_ref, lo_ref):
    rows = x_ref.shape[1]
    half = RADIX // 2
    where = lambda f: (f - 1) % (half + 1)
    for block in range(rows // 16):
        r = slice(block * 16, block * 16 + 16)
        for k in range(INNER // LANES):
            slices = []
            for t in range(RADIX):
                at = (t % SIDE) * INNER + k * LANES
                slices.append(x_ref[t // SIDE, r, at:at + LANES].astype(jnp.float32))
            outer = real_dft(slices)
            for f in range(half + 1):
                re, im = outer[f]
                lanes = slice(k * LANES, (k + 1) * LANES)
                c, s = tw_ref[0, f:f + 1, lanes], tw_ref[1, f:f + 1, lanes]
                if f == 0:
                    parts = (re,)
                elif im is None:
                    parts = (re * c, re * s)
                else:
                    parts = (re * c - im * s, re * s + im * c)
                row = slice(where(f) * rows + block * 16, where(f) * rows + block * 16 + 16)
                for n, part in enumerate(parts):
                    hi = part.astype(jnp.bfloat16)
                    at = slice(n * INNER + k * LANES, n * INNER + (k + 1) * LANES)
                    hi_ref[row, at] = hi
                    lo_ref[row, at] = (part - hi.astype(jnp.float32)).astype(jnp.bfloat16)

    def spectrum(row, depth, width):
        hi, lo = hi_ref[row, :depth], lo_ref[row, :depth]
        upper, lower = upper_ref[:depth, :width], lower_ref[:depth, :width]
        out = jnp.dot(hi, upper, preferred_element_type=jnp.float32)
        out += jnp.dot(hi, lower, preferred_element_type=jnp.float32)
        return out + jnp.dot(lo, upper, preferred_element_type=jnp.float32)

    most = spectrum(slice(0, (half - 1) * rows), 2 * INNER, 4 * LANES)
    middle = spectrum(slice((half - 1) * rows, half * rows), 2 * INNER, 2 * LANES)
    first = spectrum(slice(half * rows, (half + 1) * rows), INNER, 2 * LANES)

    def part(f, k):
        if f == 0:
            return first[:, k * LANES:(k + 1) * LANES]
        if f == half:
            return middle[:, k * LANES:(k + 1) * LANES]
        g, base = (f, 0) if f < half else (RADIX - f, 2)
        return most[(g - 1) * rows:g * rows, (base + k) * LANES:(base + k + 1) * LANES]

    power = None
    for f in range(RADIX):
        re, im = part(f, 0), part(f, 1)
        both = re * re + im * im
        power = both if power is None else power + both
    power = power + pltpu.roll(power, 64, 1)
    power = power + pltpu.roll(power, 32, 1)
    scale = 1.0 / jnp.sqrt(power * (1.0 / BAND) + 1e-06)
    low = core_ref[0] == 0
    for block in range(rows // 8):
        r = slice(block * 8, block * 8 + 8)
        halves = []
        for h in range(2):
            tiles = [part(h * 8 + f, k)[r] * scale[r] for k in range(2) for f in range(8)]
            halves.append(jnp.transpose(jnp.stack(tiles, axis=0), (1, 0, 2)))
        mine_ref[r] = jnp.where(low, halves[0], halves[1]).astype(jnp.bfloat16)
        other_ref[r] = jnp.where(low, halves[1], halves[0]).astype(jnp.bfloat16)


def whiten(core, samples, twiddle, upper, lower):
    samples = pltpu.with_memory_space_constraint(samples, pltpu.MemorySpace.HBM)
    rows = samples.shape[1]
    out = jax.ShapeDtypeStruct((rows, NSEG * HALF_ROWS, LANES), jnp.bfloat16)
    spec = pl.BlockSpec((rows, HALF_ROWS, LANES), lambda s, c: (0, s, 0))
    count = RADIX // 2 + 1
    return pl.pallas_call(
        whiten_kernel,
        out_shape=(out, out),
        grid_spec=pltpu.PrefetchScalarGridSpec(
            num_scalar_prefetch=1,
            grid=(NSEG,),
            in_specs=[
                pl.BlockSpec((SIDE, rows, SEGLEN // SIDE), lambda s, c: (s, 0, 0)),
                pl.BlockSpec((2, RADIX, INNER), lambda s, c: (0, 0, 0)),
                pl.BlockSpec((2 * INNER, 4 * LANES), lambda s, c: (0, 0)),
                pl.BlockSpec((2 * INNER, 4 * LANES), lambda s, c: (0, 0)),
            ],
            out_specs=(spec, spec),
            scratch_shapes=[
                pltpu.VMEM((count * rows, 2 * INNER), jnp.bfloat16),
                pltpu.VMEM((count * rows, 2 * INNER), jnp.bfloat16),
            ],
        ),
        compiler_params=pltpu.CompilerParams(vmem_limit_bytes=48 << 20),
        name="whiten",
    )(core, samples, twiddle, upper, lower)


GROUP = 8
CHUNK = 128


def load_pieces(pieces, targets, sems):
    copies = []
    n = 0
    for group, target in zip(pieces, targets):
        at = 0
        for piece in group:
            copies.append(pltpu.make_async_copy(piece, target.at[at:at + piece.shape[0]], sems.at[n]))
            at += piece.shape[0]
            n += 1
    for copy in copies:
        copy.start()
    return copies


def cross_slots(count, src_ref, rcv_ref, row_of, sources_ref, receivers_ref, cross_ref):
    def group(g, carry):
        for u in range(GROUP):
            i = g * GROUP + u
            a = sources_ref[src_ref[i]].astype(jnp.float32)
            b = receivers_ref[rcv_ref[i]].astype(jnp.float32)
            re = im = None
            for s in range(NSEG):
                ar, ai = a[s * 16:s * 16 + 8], a[s * 16 + 8:s * 16 + 16]
                br, bi = b[s * 16:s * 16 + 8], b[s * 16 + 8:s * 16 + 16]
                r = ar * br + ai * bi
                m = ai * br - ar * bi
                re = r if re is None else re + r
                im = m if im is None else im + m
            row = row_of(i)
            at = pl.multiple_of(row * HALF_ROWS, HALF_ROWS)
            cross_ref[pl.ds(at, 8), :] = re
            cross_ref[pl.ds(at + 8, 8), :] = im
        return carry

    lax.fori_loop(0, (count + GROUP - 1) // GROUP, group, 0)


def lags_of(cross_ref, first, count, table_ref):
    cross = jnp.concatenate(
        [cross_ref[pl.ds(first * HALF_ROWS + g, count, stride=HALF_ROWS), :].astype(jnp.bfloat16) for g in range(HALF_ROWS)],
        axis=1,
    )
    return jnp.dot(cross, table_ref[...], preferred_element_type=jnp.float32)


def near_kernel(count_ref, src_ref, rcv_ref, slot_ref, *refs):
    pieces = refs[:8]
    table_ref, out_ref, sources_ref, receivers_ref, cross_ref, sems = refs[8:]
    copies = load_pieces((pieces[:6], pieces[6:]), (sources_ref, receivers_ref), sems)
    cross_ref[...] = jnp.zeros_like(cross_ref)
    for copy in copies:
        copy.wait()
    cross_slots(count_ref[0], src_ref, rcv_ref, lambda i: slot_ref[i], sources_ref, receivers_ref, cross_ref)
    out_ref[...] = lags_of(cross_ref, 0, out_ref.shape[0], table_ref)


def far_kernel(count_ref, src_ref, rcv_ref, slot_ref, *refs):
    pieces = refs[:4]
    table_ref, near_ref, out_ref, sources_ref, receivers_ref, cross_ref, rows_ref, product_ref, sems = refs[4:]
    copies = load_pieces((pieces[:2], pieces[2:]), (sources_ref, receivers_ref), sems)
    slots = out_ref.shape[0]
    rows_ref[0:slots, :] = near_ref[...]
    for copy in copies:
        copy.wait()
    count = count_ref[0]
    cross_slots(count, src_ref, rcv_ref, lambda i: i, sources_ref, receivers_ref, cross_ref)

    def chunk(c, carry):
        first = pl.multiple_of(c * CHUNK, CHUNK)
        product_ref[...] = lags_of(cross_ref, first, CHUNK, table_ref)

        def place(g, inner):
            for u in range(GROUP):
                i = g * GROUP + u
                rows_ref[pl.ds(slot_ref[first + i], 1), :] = product_ref[pl.ds(i, 1), :]
            return inner

        return lax.fori_loop(0, (jnp.minimum(count - first, CHUNK) + GROUP - 1) // GROUP, place, carry)

    lax.fori_loop(0, (count + CHUNK - 1) // CHUNK, chunk, 0)
    out_ref[...] = rows_ref[0:slots, :].astype(jnp.bfloat16)


def correlate(kernel, lists, pieces, receivers, blocks, dtype, extra):
    slots = lists[1].shape[0]
    row = pieces[0].shape[1:]
    whole = lambda a: pl.BlockSpec(a.shape, lambda *_: (0,) * a.ndim)
    return pl.pallas_call(
        kernel,
        out_shape=jax.ShapeDtypeStruct((slots, NLAG), dtype),
        grid_spec=pltpu.PrefetchScalarGridSpec(
            num_scalar_prefetch=4,
            grid=(1,),
            in_specs=[pl.BlockSpec(memory_space=pl.ANY)] * (len(pieces) + len(receivers)) + [whole(b) for b in blocks],
            out_specs=pl.BlockSpec((slots, NLAG), lambda *_: (0, 0)),
            scratch_shapes=[
                pltpu.VMEM((sum(p.shape[0] for p in pieces),) + row, jnp.bfloat16),
                pltpu.VMEM((sum(p.shape[0] for p in receivers),) + row, jnp.bfloat16),
                pltpu.VMEM(((slots + GROUP) * HALF_ROWS, LANES), jnp.float32),
                *extra,
                pltpu.SemaphoreType.DMA((len(pieces) + len(receivers),)),
            ],
        ),
        compiler_params=pltpu.CompilerParams(vmem_limit_bytes=40 << 20),
    )(*lists, *pieces, *receivers, *blocks)


def pick_kernel(wanted_ref, raw_ref, taper_ref, out_ref, rows_ref, sems):
    rows = rows_ref.shape[0]
    copies = [
        pltpu.make_async_copy(raw_ref.at[pl.ds(wanted_ref[r], 1), :], rows_ref.at[pl.ds(r, 1), :], sems.at[r])
        for r in range(rows)
    ]
    for copy in copies:
        copy.start()
    for copy in copies:
        copy.wait()
    value = (rows_ref[...] * taper_ref[...]).astype(jnp.bfloat16)
    for g in range(out_ref.shape[0]):
        out_ref[g] = value


def pick_rows(wanted, raw_window, taper, copies):
    rows, span = wanted.shape[0], raw_window.shape[1]
    return pl.pallas_call(
        pick_kernel,
        out_shape=jax.ShapeDtypeStruct((copies, rows, span), jnp.bfloat16),
        grid_spec=pltpu.PrefetchScalarGridSpec(
            num_scalar_prefetch=1,
            grid=(1,),
            in_specs=[pl.BlockSpec(memory_space=pl.ANY), pl.BlockSpec((1, span), lambda *_: (0, 0))],
            out_specs=pl.BlockSpec((copies, rows, span), lambda *_: (0, 0, 0)),
            scratch_shapes=[pltpu.VMEM((rows, span), jnp.float32), pltpu.SemaphoreType.DMA((rows,))],
        ),
        name="pick",
    )(wanted, raw_window, taper.reshape(1, span))


def shift(value, axis, step):
    if axis == "core":
        return lax.ppermute(value, "gx", [(g, g ^ 1) for g in range(2 * SIDE)])
    if axis == "y":
        return lax.ppermute(value, "gx", [(g, (g + 2 * step) % (2 * SIDE)) for g in range(2 * SIDE)])
    if axis == "z":
        return lax.ppermute(value, "gy", [(g, (g + SIDE * step) % (SIDE * SIDE)) for g in range(SIDE * SIDE)])
    return lax.ppermute(value, "gy", [(g, g // SIDE * SIDE + (g + step) % SIDE) for g in range(SIDE * SIDE)])


def gather_ring(value, axis):
    return jnp.stack([value] + [shift(value, axis, d) for d in (1, 2, 3)], axis=0)


def program(raw_window, source_ids, pair_source, pair_holder, pair_receiver):
    groups = lax.axis_size("gy")
    devices = lax.axis_size("gx") * groups
    gx, gy = lax.axis_index("gx"), lax.axis_index("gy")
    place = {"core": gx % 2, "y": gx // 2, "z": gy // SIDE, "x": gy % SIDE}
    core = place["core"]
    here = gx * groups + gy
    span = raw_window.shape[1]
    channels = raw_window.shape[0] // groups
    sample = (gy * span + jnp.arange(span, dtype=jnp.int32)) % SEGLEN
    taper = jnp.sin(math.pi * (sample.astype(jnp.float32) + 0.5) / SEGLEN) ** 2

    pairs = pair_source.shape[0]
    per = source_ids.shape[0]
    holder = pair_holder[:, 0]
    order = jnp.arange(pairs, dtype=jnp.int32)
    same = (holder[:, None] == holder[None, :]) & (order[None, :] < order[:, None])
    rank = jnp.sum(same.astype(jnp.int32), axis=1)
    packed = ((holder * 2 + rank) * channels + pair_receiver) * 256 + pair_source
    notes = jnp.concatenate([packed, source_ids - gx * groups * channels])
    notes = gather_ring(notes, "x")
    notes = gather_ring(notes, "z")
    ids, notes = notes[:, :, pairs:].reshape(groups, per), notes[:, :, :pairs]

    step = jnp.arange(groups, dtype=jnp.int32)
    mate = (place["z"] - step // SIDE) % SIDE * SIDE + (place["x"] - step % SIDE) % SIDE
    wanted = jnp.sum(jnp.where(mate[None, :, None] == step[:, None, None], ids[None], 0), axis=1).reshape(-1)
    first = pick_rows(wanted, raw_window, taper, groups)
    first = lax.all_to_all(first, "gy", split_axis=0, concat_axis=0, tiled=True)
    tapered = (raw_window * taper[None, :]).astype(jnp.bfloat16)
    samples = lax.all_to_all(tapered.reshape(groups, channels, span), "gy", split_axis=0, concat_axis=0, tiled=True)
    notes = gather_ring(notes, "y")
    notes = jnp.stack([notes, shift(notes, "core", 1)], axis=0).reshape(devices, pairs)

    twiddle = twiddle_table()
    upper, lower = inner_table()
    near0, away = whiten(core.reshape(1), first, twiddle, upper, lower)
    near1 = shift(away, "core", 1)
    ahead0 = shift(near0, "y", 1)
    behind0 = shift(near0, "y", 3)
    ahead1 = shift(near1, "y", 1)
    behind1 = shift(near1, "y", 3)
    far0 = shift(ahead0, "y", 1)
    far1 = shift(behind1, "y", 3)

    notes, late, _ = lax.optimization_barrier((notes, core, near1))
    table = inverse_table(late, late - core)

    mine, other = whiten(core.reshape(1), samples, twiddle, upper, lower)
    sister = shift(other, "core", 1)

    dev = jnp.arange(devices, dtype=jnp.int32)
    own = (
        (((dev // 64) ^ late) + (place["y"] - dev // 16 % SIDE) % SIDE * 2) * groups
        + (place["z"] - dev // SIDE % SIDE) % SIDE * SIDE
        + (place["x"] - dev % SIDE) % SIDE
    )
    key = notes // (channels * 256)
    low = notes % (channels * 256)
    kinds = jnp.stack([here * 2, here * 2 + 1, (here ^ groups) * 2, (here ^ groups) * 2 + 1])
    found = jnp.sum(jnp.where(key[None] == kinds[:, None, None], low[None] + 1, 0), axis=2)
    asked = jnp.sum(jnp.where(own[None, None, :] == dev[None, :, None], found[:, None, :], 0), axis=2)
    valid = asked > 0
    asked = jnp.maximum(asked - 1, 0)
    slots = asked.size
    source_no = asked % 256
    source_gx = source_no // (2 * groups)
    rel_y = (place["y"] - source_gx // 2) % SIDE
    far = rel_y == 2
    piece = jnp.where(far, 0, jnp.minimum(rel_y, 2))
    source_at = (piece * 2 + (source_gx % 2 ^ core)) * (2 * groups) + source_no % (2 * groups)
    kind = jnp.arange(4, dtype=jnp.int32)[:, None]
    slot_no = dev[None, :] * 4 + kind
    receiver_at = asked // 256 + kind // 2 * channels
    entry = ((slot_no - slots) * 256 + receiver_at) * 256 + source_at
    index = jnp.arange(slots, dtype=jnp.int32)

    def compact(chosen):
        chosen = chosen.reshape(-1)
        spot = jnp.sum((chosen[None, :] & (index[None, :] < index[:, None])).astype(jnp.int32), axis=1)
        hit = chosen[None, :] & (spot[None, :] == index[:, None])
        line = jnp.sum(jnp.where(hit, entry.reshape(1, -1), 0), axis=1) + slots * 65536
        return jnp.sum(chosen.astype(jnp.int32)).reshape(1), line % 256, line // 256 % 256, line // 65536

    near_lists = compact(valid & ~far)
    far_lists = compact(valid & far)

    receivers = [mine, sister]
    near = correlate(
        near_kernel, near_lists, [near0, near1, ahead0, ahead1, behind0, behind1], receivers, [table], jnp.float32, []
    )
    extra = [pltpu.VMEM((slots + GROUP, NLAG), jnp.float32), pltpu.VMEM((CHUNK, NLAG), jnp.float32)]
    partial = correlate(far_kernel, far_lists, [far0, far1], receivers, [table, near], jnp.bfloat16, extra)
    returned = lax.all_to_all(partial.reshape(devices, 4, NLAG), ("gx", "gy"), split_axis=0, concat_axis=0, tiled=True)
    returned = returned.reshape(devices * 4, NLAG)
    row = jnp.arange(4 * devices, dtype=jnp.int32)
    row_dev, row_rel, row_rank = row // 4, row // 2 % 2, row % 2
    row_holder = jnp.where(row_rel == 0, row_dev, row_dev ^ groups)
    pick = (row_holder[None, :] == holder[:, None]) & (row_rank[None, :] == rank[:, None])
    return jnp.dot(pick.astype(jnp.bfloat16), returned, preferred_element_type=jnp.float32)


def solution(mesh):
    return jax.shard_map(
        program,
        mesh=mesh,
        in_specs=(
            P("gx", "gy"),
            P(("gx", "gy")),
            P(("gx", "gy")),
            P(("gx", "gy"), None),
            P(("gx", "gy")),
        ),
        out_specs=P(("gx", "gy"), None),
        check_vma=False,
    )
```

```python
import math

import jax
import jax.numpy as jnp
from jax import lax
from jax.experimental import pallas as pl
from jax.experimental.pallas import tpu as pltpu
from jax.sharding import PartitionSpec as P


NBIN = 2048
SEGLEN = 4096
NSEG = 4
BAND = 64
NLAG = 512
SIDE = 4
RADIX = 16
INNER = SEGLEN // RADIX
LANES = 128
HALF_ROWS = 2 * (RADIX // 2)


def split_table(table):
    upper = table.astype(jnp.bfloat16)
    lower = (table - upper.astype(jnp.float32)).astype(jnp.bfloat16)
    return (upper, lower)


def lane_bins():
    lane = jnp.arange(LANES, dtype=jnp.int32)
    return 4 * (lane % 32) + lane // 32


def inner_table():
    times = jnp.arange(INNER, dtype=jnp.int32)
    low = lane_bins()
    high = INNER - 1 - low
    turn = 2.0 * math.pi / INNER

    def block(bins, sign):
        angle = (times[:, None] * bins[None, :] % INNER).astype(jnp.float32) * turn
        cos, sin = jnp.cos(angle), jnp.sin(angle)
        top = jnp.concatenate([cos, -sign * sin], axis=1)
        bottom = jnp.concatenate([sin, sign * cos], axis=1)
        return jnp.concatenate([top, bottom], axis=0)

    return split_table(jnp.concatenate([block(low, 1.0), block(high, -1.0)], axis=1))


def twiddle_table():
    rows = jnp.arange(RADIX, dtype=jnp.int32)
    times = jnp.arange(INNER, dtype=jnp.int32)
    angle = (rows[:, None] * times[None, :] % SEGLEN).astype(jnp.float32) * (2.0 * math.pi / SEGLEN)
    return jnp.stack([jnp.cos(angle), -jnp.sin(angle)], axis=0)


def turns(count, lags):
    angle = (count[:, None] * lags[None, :] % SEGLEN).astype(jnp.float32) * (2.0 * math.pi / SEGLEN)
    return jnp.cos(angle), jnp.sin(angle)


def inverse_table(core, zero):
    outer = core * (RADIX // 2) + jnp.arange(RADIX // 2, dtype=jnp.int32)
    inner = RADIX * lane_bins() + zero
    lags = (jnp.arange(NLAG, dtype=jnp.int32) - NLAG // 2) % SEGLEN
    (c1, s1), (c2, s2) = lax.optimization_barrier((turns(outer, lags), turns(inner, lags)))
    c1, s1, c2, s2 = c1[:, None], s1[:, None], c2[None], s2[None]
    bins = outer[:, None, None] + inner[None, :, None]
    weight = jnp.where(bins == 0, 1.0, 2.0).astype(jnp.float32) * (0.5 / math.sqrt(NSEG * NBIN))
    table = jnp.stack([weight * (c1 * c2 - s1 * s2), -weight * (s1 * c2 + c1 * s2)], axis=0)
    return table.astype(jnp.bfloat16).reshape(NBIN, NLAG)


def real_dft(values):
    n = len(values)
    if n == 2:
        return [(values[0] + values[1], None), (values[0] - values[1], None)]
    even = real_dft(values[0::2])
    odd = real_dft(values[1::2])
    out = [None] * (n // 2 + 1)
    for k in range(n // 4 + 1):
        er, ei = even[k]
        pr, pi = odd[k]
        c, s = math.cos(2 * math.pi * k / n), math.sin(2 * math.pi * k / n)
        if k == 0:
            out[0] = (er + pr, None)
            out[n // 2] = (er - pr, None)
        elif 4 * k == n:
            out[k] = (er, -pr)
        else:
            if 8 * k == n:
                tr, ti = (pr + pi) * c, (pi - pr) * c
            else:
                tr, ti = pr * c + pi * s, pi * c - pr * s
            out[k] = (er + tr, ei + ti)
            out[n // 2 - k] = (er - tr, ti - ei)
    return out


def whiten_kernel(core_ref, x_ref, tw_ref, upper_ref, lower_ref, mine_ref, other_ref, *scratch):
    count = x_ref.shape[0] // SIDE
    parts = [(x_ref.at[n * SIDE:(n + 1) * SIDE], scratch[2 * n], scratch[2 * n + 1]) for n in range(count)]
    butterflies(tw_ref, *parts[0])
    for n in range(count):
        spectra = products(x_ref.shape[1], upper_ref, lower_ref, *parts[n][1:])
        if n + 1 < count:
            butterflies(tw_ref, *parts[n + 1])
        at = slice(n * HALF_ROWS, (n + 1) * HALF_ROWS)
        finish(core_ref, x_ref.shape[1], spectra, mine_ref.at[:, at], other_ref.at[:, at])


def butterflies(tw_ref, x_ref, hi_ref, lo_ref):
    rows = x_ref.shape[1]
    half = RADIX // 2
    where = lambda f: (f - 1) % (half + 1)
    for block in range(rows // 16):
        r = slice(block * 16, block * 16 + 16)
        for k in range(INNER // LANES):
            slices = []
            for t in range(RADIX):
                at = (t % SIDE) * INNER + k * LANES
                slices.append(x_ref[t // SIDE, r, at:at + LANES].astype(jnp.float32))
            outer = real_dft(slices)
            for f in range(half + 1):
                re, im = outer[f]
                lanes = slice(k * LANES, (k + 1) * LANES)
                c, s = tw_ref[0, f:f + 1, lanes], tw_ref[1, f:f + 1, lanes]
                if f == 0:
                    parts = (re,)
                elif im is None:
                    parts = (re * c, re * s)
                else:
                    parts = (re * c - im * s, re * s + im * c)
                row = slice(where(f) * rows + block * 16, where(f) * rows + block * 16 + 16)
                for n, part in enumerate(parts):
                    hi = part.astype(jnp.bfloat16)
                    at = slice(n * INNER + k * LANES, n * INNER + (k + 1) * LANES)
                    hi_ref[row, at] = hi
                    lo_ref[row, at] = (part - hi.astype(jnp.float32)).astype(jnp.bfloat16)


def products(rows, upper_ref, lower_ref, hi_ref, lo_ref):
    half = RADIX // 2

    def spectrum(row, depth, width):
        hi, lo = hi_ref[row, :depth], lo_ref[row, :depth]
        upper, lower = upper_ref[:depth, :width], lower_ref[:depth, :width]
        out = jnp.dot(hi, upper, preferred_element_type=jnp.float32)
        out += jnp.dot(hi, lower, preferred_element_type=jnp.float32)
        return out + jnp.dot(lo, upper, preferred_element_type=jnp.float32)

    most = spectrum(slice(0, (half - 1) * rows), 2 * INNER, 4 * LANES)
    middle = spectrum(slice((half - 1) * rows, half * rows), 2 * INNER, 2 * LANES)
    first = spectrum(slice(half * rows, (half + 1) * rows), INNER, 2 * LANES)
    return first, middle, most


def finish(core_ref, rows, spectra, mine_ref, other_ref):
    half = RADIX // 2
    first, middle, most = spectra

    def part(f, k):
        if f == 0:
            return first[:, k * LANES:(k + 1) * LANES]
        if f == half:
            return middle[:, k * LANES:(k + 1) * LANES]
        g, base = (f, 0) if f < half else (RADIX - f, 2)
        return most[(g - 1) * rows:g * rows, (base + k) * LANES:(base + k + 1) * LANES]

    power = None
    for f in range(RADIX):
        re, im = part(f, 0), part(f, 1)
        both = re * re + im * im
        power = both if power is None else power + both
    power = power + pltpu.roll(power, 64, 1)
    power = power + pltpu.roll(power, 32, 1)
    scale = 1.0 / jnp.sqrt(power * (1.0 / BAND) + 1e-06)
    low = core_ref[0] == 0
    for block in range(rows // 8):
        r = slice(block * 8, block * 8 + 8)
        halves = []
        for h in range(2):
            tiles = [part(h * 8 + f, k)[r] * scale[r] for k in range(2) for f in range(8)]
            halves.append(jnp.transpose(jnp.stack(tiles, axis=0), (1, 0, 2)))
        mine_ref[r] = jnp.where(low, halves[0], halves[1]).astype(jnp.bfloat16)
        other_ref[r] = jnp.where(low, halves[1], halves[0]).astype(jnp.bfloat16)


def whiten(core, samples, twiddle, upper, lower, per):
    rows = samples.shape[1]
    out = jax.ShapeDtypeStruct((rows, NSEG * HALF_ROWS, LANES), jnp.bfloat16)
    spec = pl.BlockSpec((rows, per * HALF_ROWS, LANES), lambda s, c: (0, s, 0))
    count = RADIX // 2 + 1
    return pl.pallas_call(
        whiten_kernel,
        out_shape=(out, out),
        grid_spec=pltpu.PrefetchScalarGridSpec(
            num_scalar_prefetch=1,
            grid=(NSEG // per,),
            in_specs=[
                pl.BlockSpec((per * SIDE, rows, SEGLEN // SIDE), lambda s, c: (s, 0, 0)),
                pl.BlockSpec((2, RADIX, INNER), lambda s, c: (0, 0, 0)),
                pl.BlockSpec((2 * INNER, 4 * LANES), lambda s, c: (0, 0)),
                pl.BlockSpec((2 * INNER, 4 * LANES), lambda s, c: (0, 0)),
            ],
            out_specs=(spec, spec),
            scratch_shapes=[pltpu.VMEM((count * rows, 2 * INNER), jnp.bfloat16)] * (2 * per),
        ),
        compiler_params=pltpu.CompilerParams(vmem_limit_bytes=48 << 20),
        name="whiten",
    )(core, samples, twiddle, upper, lower)


GROUP = 8
CHUNK = 128


def load_pieces(pieces, targets, sems):
    copies = []
    n = 0
    for group, target in zip(pieces, targets):
        at = 0
        for piece in group:
            copies.append(pltpu.make_async_copy(piece, target.at[at:at + piece.shape[0]], sems.at[n]))
            at += piece.shape[0]
            n += 1
    for copy in copies:
        copy.start()
    return copies


def cross_slots(count, src_ref, rcv_ref, row_of, sources_ref, receivers_ref, cross_ref):
    def group(g, carry):
        for u in range(GROUP):
            i = g * GROUP + u
            a = sources_ref[src_ref[i]].astype(jnp.float32)
            b = receivers_ref[rcv_ref[i]].astype(jnp.float32)
            re = im = None
            for s in range(NSEG):
                ar, ai = a[s * 16:s * 16 + 8], a[s * 16 + 8:s * 16 + 16]
                br, bi = b[s * 16:s * 16 + 8], b[s * 16 + 8:s * 16 + 16]
                r = ar * br + ai * bi
                m = ai * br - ar * bi
                re = r if re is None else re + r
                im = m if im is None else im + m
            row = row_of(i)
            at = pl.multiple_of(row * HALF_ROWS, HALF_ROWS)
            cross_ref[pl.ds(at, 8), :] = re
            cross_ref[pl.ds(at + 8, 8), :] = im
        return carry

    lax.fori_loop(0, (count + GROUP - 1) // GROUP, group, 0)


def lags_of(cross_ref, first, count, table_ref):
    cross = jnp.concatenate(
        [cross_ref[pl.ds(first * HALF_ROWS + g, count, stride=HALF_ROWS), :].astype(jnp.bfloat16) for g in range(HALF_ROWS)],
        axis=1,
    )
    return jnp.dot(cross, table_ref[...], preferred_element_type=jnp.float32)


def near_kernel(count_ref, src_ref, rcv_ref, slot_ref, *refs):
    pieces = refs[:8]
    table_ref, out_ref, sources_ref, receivers_ref, cross_ref, sems = refs[8:]
    copies = load_pieces((pieces[:6], pieces[6:]), (sources_ref, receivers_ref), sems)
    cross_ref[...] = jnp.zeros_like(cross_ref)
    for copy in copies:
        copy.wait()
    cross_slots(count_ref[0], src_ref, rcv_ref, lambda i: slot_ref[i], sources_ref, receivers_ref, cross_ref)
    out_ref[...] = lags_of(cross_ref, 0, out_ref.shape[0], table_ref)


def far_kernel(count_ref, src_ref, rcv_ref, slot_ref, *refs):
    pieces = refs[:4]
    table_ref, near_ref, out_ref, sources_ref, receivers_ref, cross_ref, rows_ref, product_ref, sems = refs[4:]
    copies = load_pieces((pieces[:2], pieces[2:]), (sources_ref, receivers_ref), sems)
    slots = out_ref.shape[0]
    rows_ref[0:slots, :] = near_ref[...]
    for copy in copies:
        copy.wait()
    count = count_ref[0]
    cross_slots(count, src_ref, rcv_ref, lambda i: i, sources_ref, receivers_ref, cross_ref)

    def chunk(c, carry):
        first = pl.multiple_of(c * CHUNK, CHUNK)
        product_ref[...] = lags_of(cross_ref, first, CHUNK, table_ref)

        def place(g, inner):
            for u in range(GROUP):
                i = g * GROUP + u
                rows_ref[pl.ds(slot_ref[first + i], 1), :] = product_ref[pl.ds(i, 1), :]
            return inner

        return lax.fori_loop(0, (jnp.minimum(count - first, CHUNK) + GROUP - 1) // GROUP, place, carry)

    lax.fori_loop(0, (count + CHUNK - 1) // CHUNK, chunk, 0)
    out_ref[...] = rows_ref[0:slots, :].astype(jnp.bfloat16)


def correlate(kernel, lists, pieces, receivers, blocks, dtype, extra):
    slots = lists[1].shape[0]
    row = pieces[0].shape[1:]
    whole = lambda a: pl.BlockSpec(a.shape, lambda *_: (0,) * a.ndim)
    return pl.pallas_call(
        kernel,
        out_shape=jax.ShapeDtypeStruct((slots, NLAG), dtype),
        grid_spec=pltpu.PrefetchScalarGridSpec(
            num_scalar_prefetch=4,
            grid=(1,),
            in_specs=[pl.BlockSpec(memory_space=pl.ANY)] * (len(pieces) + len(receivers)) + [whole(b) for b in blocks],
            out_specs=pl.BlockSpec((slots, NLAG), lambda *_: (0, 0)),
            scratch_shapes=[
                pltpu.VMEM((sum(p.shape[0] for p in pieces),) + row, jnp.bfloat16),
                pltpu.VMEM((sum(p.shape[0] for p in receivers),) + row, jnp.bfloat16),
                pltpu.VMEM(((slots + GROUP) * HALF_ROWS, LANES), jnp.float32),
                *extra,
                pltpu.SemaphoreType.DMA((len(pieces) + len(receivers),)),
            ],
        ),
        compiler_params=pltpu.CompilerParams(vmem_limit_bytes=40 << 20),
    )(*lists, *pieces, *receivers, *blocks)


def pick_kernel(wanted_ref, raw_ref, taper_ref, out_ref, rows_ref, sems):
    rows = rows_ref.shape[0]
    copies = [
        pltpu.make_async_copy(raw_ref.at[pl.ds(wanted_ref[r], 1), :], rows_ref.at[pl.ds(r, 1), :], sems.at[r])
        for r in range(rows)
    ]
    for copy in copies:
        copy.start()
    for copy in copies:
        copy.wait()
    value = (rows_ref[...] * taper_ref[...]).astype(jnp.bfloat16)
    for g in range(out_ref.shape[0]):
        out_ref[g] = value


def pick_rows(wanted, raw_window, taper, copies):
    rows, span = wanted.shape[0], raw_window.shape[1]
    return pl.pallas_call(
        pick_kernel,
        out_shape=jax.ShapeDtypeStruct((copies, rows, span), jnp.bfloat16),
        grid_spec=pltpu.PrefetchScalarGridSpec(
            num_scalar_prefetch=1,
            grid=(1,),
            in_specs=[pl.BlockSpec(memory_space=pl.ANY), pl.BlockSpec((1, span), lambda *_: (0, 0))],
            out_specs=pl.BlockSpec((copies, rows, span), lambda *_: (0, 0, 0)),
            scratch_shapes=[pltpu.VMEM((rows, span), jnp.float32), pltpu.SemaphoreType.DMA((rows,))],
        ),
        name="pick",
    )(wanted, raw_window, taper.reshape(1, span))


def shift(value, axis, step):
    if axis == "core":
        return lax.ppermute(value, "gx", [(g, g ^ 1) for g in range(2 * SIDE)])
    if axis == "y":
        return lax.ppermute(value, "gx", [(g, (g + 2 * step) % (2 * SIDE)) for g in range(2 * SIDE)])
    if axis == "z":
        return lax.ppermute(value, "gy", [(g, (g + SIDE * step) % (SIDE * SIDE)) for g in range(SIDE * SIDE)])
    return lax.ppermute(value, "gy", [(g, g // SIDE * SIDE + (g + step) % SIDE) for g in range(SIDE * SIDE)])


def gather_ring(value, axis):
    return jnp.stack([value] + [shift(value, axis, d) for d in (1, 2, 3)], axis=0)


def program(raw_window, source_ids, pair_source, pair_holder, pair_receiver):
    groups = lax.axis_size("gy")
    devices = lax.axis_size("gx") * groups
    gx, gy = lax.axis_index("gx"), lax.axis_index("gy")
    place = {"core": gx % 2, "y": gx // 2, "z": gy // SIDE, "x": gy % SIDE}
    core = place["core"]
    here = gx * groups + gy
    span = raw_window.shape[1]
    channels = raw_window.shape[0] // groups
    sample = (gy * span + jnp.arange(span, dtype=jnp.int32)) % SEGLEN
    taper = jnp.sin(math.pi * (sample.astype(jnp.float32) + 0.5) / SEGLEN) ** 2

    pairs = pair_source.shape[0]
    per = source_ids.shape[0]
    holder = pair_holder[:, 0]
    order = jnp.arange(pairs, dtype=jnp.int32)
    packed = (holder * channels + pair_receiver) * 256 + pair_source
    notes = jnp.concatenate([packed, source_ids])
    notes = gather_ring(notes, "x")
    notes = gather_ring(notes, "z")
    ids, notes = notes[:, :, pairs:].reshape(groups, per), notes[:, :, :pairs]

    step = jnp.arange(groups, dtype=jnp.int32)
    mate = (place["z"] - step // SIDE) % SIDE * SIDE + (place["x"] - step % SIDE) % SIDE
    wanted = jnp.sum(jnp.where(mate[None, :, None] == step[:, None, None], ids[None], 0), axis=1).reshape(-1)
    wanted = wanted - gx * groups * channels
    first = pick_rows(wanted, raw_window, taper, groups)
    first = lax.all_to_all(first, "gy", split_axis=0, concat_axis=0, tiled=True)
    tapered = (raw_window * taper[None, :]).astype(jnp.bfloat16)
    samples = lax.all_to_all(tapered.reshape(groups, channels, span), "gy", split_axis=0, concat_axis=0, tiled=True)
    notes = gather_ring(notes, "y")
    notes = jnp.stack([notes, shift(notes, "core", 1)], axis=0).reshape(devices, pairs)

    twiddle = twiddle_table()
    upper, lower = inner_table()
    near0, away = whiten(core.reshape(1), first, twiddle, upper, lower, NSEG)
    near1 = shift(away, "core", 1)
    ahead0 = shift(near0, "y", 1)
    behind0 = shift(near0, "y", 3)
    ahead1 = shift(near1, "y", 1)
    behind1 = shift(near1, "y", 3)
    far0 = shift(ahead0, "y", 1)
    far1 = shift(behind1, "y", 3)

    notes, late, _ = lax.optimization_barrier((notes, core, near1))
    table = inverse_table(late, late - core)

    samples = pltpu.with_memory_space_constraint(samples, pltpu.MemorySpace.HBM)
    mine, other = whiten(core.reshape(1), samples, twiddle, upper, lower, 2)
    sister = shift(other, "core", 1)

    dev = jnp.arange(devices, dtype=jnp.int32)
    own = (
        (((dev // 64) ^ late) + (place["y"] - dev // 16 % SIDE) % SIDE * 2) * groups
        + (place["z"] - dev // SIDE % SIDE) % SIDE * SIDE
        + (place["x"] - dev % SIDE) % SIDE
    )
    each = channels * 256
    key = notes // each
    entry = order[None, :] * each + notes % each + 1
    first_last = []
    for name in (here, here ^ groups):
        match = key == name
        high = jnp.max(jnp.where(match, entry, 0), axis=1)
        low = jnp.max(jnp.where(match, pairs * each + 1 - entry, 0), axis=1)
        low = jnp.where(low > 0, pairs * each + 1 - low, 0)
        first_last += [low, jnp.where(high > low, high, 0)]
    found = jnp.stack(first_last)
    asked = jnp.sum(jnp.where(own[None, None, :] == dev[None, :, None], found[:, None, :], 0), axis=2)
    valid = asked > 0
    asked = jnp.maximum(asked - 1, 0) % each
    slots = asked.size
    source_no = asked % 256
    source_gx = source_no // (2 * groups)
    rel_y = (place["y"] - source_gx // 2) % SIDE
    far = rel_y == 2
    piece = jnp.where(far, 0, jnp.minimum(rel_y, 2))
    source_at = (piece * 2 + (source_gx % 2 ^ core)) * (2 * groups) + source_no % (2 * groups)
    kind = jnp.arange(4, dtype=jnp.int32)[:, None]
    slot_no = dev[None, :] * 4 + kind
    receiver_at = asked // 256 + kind // 2 * channels
    entry = ((slot_no - slots) * 256 + receiver_at) * 256 + source_at
    index = jnp.arange(slots, dtype=jnp.int32)

    def compact(chosen):
        chosen = chosen.reshape(-1)
        spot = jnp.sum((chosen[None, :] & (index[None, :] < index[:, None])).astype(jnp.int32), axis=1)
        hit = chosen[None, :] & (spot[None, :] == index[:, None])
        line = jnp.sum(jnp.where(hit, entry.reshape(1, -1), 0), axis=1) + slots * 65536
        return jnp.sum(chosen.astype(jnp.int32)).reshape(1), line % 256, line // 256 % 256, line // 65536

    near_lists = compact(valid & ~far)
    far_lists = compact(valid & far)

    receivers = [mine, sister]
    near = correlate(
        near_kernel, near_lists, [near0, near1, ahead0, ahead1, behind0, behind1], receivers, [table], jnp.float32, []
    )
    extra = [pltpu.VMEM((slots + GROUP, NLAG), jnp.float32), pltpu.VMEM((CHUNK, NLAG), jnp.float32)]
    partial = correlate(far_kernel, far_lists, [far0, far1], receivers, [table, near], jnp.bfloat16, extra)
    returned = lax.all_to_all(partial.reshape(devices, 4, NLAG), ("gx", "gy"), split_axis=0, concat_axis=0, tiled=True)
    returned = returned.reshape(devices * 4, NLAG)
    same = (holder[:, None] == holder[None, :]) & (order[None, :] < order[:, None])
    rank = jnp.sum(same.astype(jnp.int32), axis=1)
    row = jnp.arange(4 * devices, dtype=jnp.int32)
    row_dev, row_rel, row_rank = row // 4, row // 2 % 2, row % 2
    row_holder = jnp.where(row_rel == 0, row_dev, row_dev ^ groups)
    pick = (row_holder[None, :] == holder[:, None]) & (row_rank[None, :] == rank[:, None])
    return jnp.dot(pick.astype(jnp.bfloat16), returned, preferred_element_type=jnp.float32)


def solution(mesh):
    return jax.shard_map(
        program,
        mesh=mesh,
        in_specs=(
            P("gx", "gy"),
            P(("gx", "gy")),
            P(("gx", "gy")),
            P(("gx", "gy"), None),
            P(("gx", "gy")),
        ),
        out_specs=P(("gx", "gy"), None),
        check_vma=False,
    )
```

```python
import math

import jax
import jax.numpy as jnp
from jax import lax
from jax.experimental import pallas as pl
from jax.experimental.pallas import tpu as pltpu
from jax.sharding import PartitionSpec as P


NBIN = 2048
SEGLEN = 4096
NSEG = 4
BAND = 64
NLAG = 512
SIDE = 4
RADIX = 16
INNER = SEGLEN // RADIX
LANES = 128
HALF_ROWS = 2 * (RADIX // 2)


def split_table(table):
    upper = table.astype(jnp.bfloat16)
    lower = (table - upper.astype(jnp.float32)).astype(jnp.bfloat16)
    return (upper, lower)


def lane_bins():
    lane = jnp.arange(LANES, dtype=jnp.int32)
    return 4 * (lane % 32) + lane // 32


def inner_table():
    times = jnp.arange(INNER, dtype=jnp.int32)
    low = lane_bins()
    high = INNER - 1 - low
    turn = 2.0 * math.pi / INNER

    def block(bins, sign):
        angle = (times[:, None] * bins[None, :] % INNER).astype(jnp.float32) * turn
        cos, sin = jnp.cos(angle), jnp.sin(angle)
        top = jnp.concatenate([cos, -sign * sin], axis=1)
        bottom = jnp.concatenate([sin, sign * cos], axis=1)
        return jnp.concatenate([top, bottom], axis=0)

    return split_table(jnp.concatenate([block(low, 1.0), block(high, -1.0)], axis=1))


def twiddle_table():
    rows = jnp.arange(RADIX, dtype=jnp.int32)
    times = jnp.arange(INNER, dtype=jnp.int32)
    angle = (rows[:, None] * times[None, :] % SEGLEN).astype(jnp.float32) * (2.0 * math.pi / SEGLEN)
    return jnp.stack([jnp.cos(angle), -jnp.sin(angle)], axis=0)


def turns(count, lags):
    angle = (count[:, None] * lags[None, :] % SEGLEN).astype(jnp.float32) * (2.0 * math.pi / SEGLEN)
    return jnp.cos(angle), jnp.sin(angle)


def inverse_table(core, zero):
    outer = core * (RADIX // 2) + jnp.arange(RADIX // 2, dtype=jnp.int32)
    inner = RADIX * lane_bins() + zero
    lags = (jnp.arange(NLAG, dtype=jnp.int32) - NLAG // 2) % SEGLEN
    (c1, s1), (c2, s2) = lax.optimization_barrier((turns(outer, lags), turns(inner, lags)))
    c1, s1, c2, s2 = c1[:, None], s1[:, None], c2[None], s2[None]
    bins = outer[:, None, None] + inner[None, :, None]
    weight = jnp.where(bins == 0, 1.0, 2.0).astype(jnp.float32) * (0.5 / math.sqrt(NSEG * NBIN))
    table = jnp.stack([weight * (c1 * c2 - s1 * s2), -weight * (s1 * c2 + c1 * s2)], axis=0)
    return table.astype(jnp.bfloat16).reshape(NBIN, NLAG)


def real_dft(values):
    n = len(values)
    if n == 2:
        return [(values[0] + values[1], None), (values[0] - values[1], None)]
    even = real_dft(values[0::2])
    odd = real_dft(values[1::2])
    out = [None] * (n // 2 + 1)
    for k in range(n // 4 + 1):
        er, ei = even[k]
        pr, pi = odd[k]
        c, s = math.cos(2 * math.pi * k / n), math.sin(2 * math.pi * k / n)
        if k == 0:
            out[0] = (er + pr, None)
            out[n // 2] = (er - pr, None)
        elif 4 * k == n:
            out[k] = (er, -pr)
        else:
            if 8 * k == n:
                tr, ti = (pr + pi) * c, (pi - pr) * c
            else:
                tr, ti = pr * c + pi * s, pi * c - pr * s
            out[k] = (er + tr, ei + ti)
            out[n // 2 - k] = (er - tr, ti - ei)
    return out


def whiten_kernel(core_ref, x_ref, tw_ref, upper_ref, lower_ref, mine_ref, other_ref, *scratch):
    count = x_ref.shape[0] // SIDE
    parts = [(x_ref.at[n * SIDE:(n + 1) * SIDE], scratch[2 * n], scratch[2 * n + 1]) for n in range(count)]
    butterflies(tw_ref, *parts[0])
    for n in range(count):
        spectra = products(x_ref.shape[1], upper_ref, lower_ref, *parts[n][1:])
        if n + 1 < count:
            butterflies(tw_ref, *parts[n + 1])
        at = slice(n * HALF_ROWS, (n + 1) * HALF_ROWS)
        finish(core_ref, x_ref.shape[1], spectra, mine_ref.at[:, at], other_ref.at[:, at])


def butterflies(tw_ref, x_ref, hi_ref, lo_ref):
    rows = x_ref.shape[1]
    half = RADIX // 2
    where = lambda f: (f - 1) % (half + 1)
    for block in range(rows // 16):
        r = slice(block * 16, block * 16 + 16)
        for k in range(INNER // LANES):
            slices = []
            for t in range(RADIX):
                at = (t % SIDE) * INNER + k * LANES
                slices.append(x_ref[t // SIDE, r, at:at + LANES].astype(jnp.float32))
            outer = real_dft(slices)
            for f in range(half + 1):
                re, im = outer[f]
                lanes = slice(k * LANES, (k + 1) * LANES)
                c, s = tw_ref[0, f:f + 1, lanes], tw_ref[1, f:f + 1, lanes]
                if f == 0:
                    parts = (re,)
                elif im is None:
                    parts = (re * c, re * s)
                else:
                    parts = (re * c - im * s, re * s + im * c)
                row = slice(where(f) * rows + block * 16, where(f) * rows + block * 16 + 16)
                for n, part in enumerate(parts):
                    hi = part.astype(jnp.bfloat16)
                    at = slice(n * INNER + k * LANES, n * INNER + (k + 1) * LANES)
                    hi_ref[row, at] = hi
                    lo_ref[row, at] = (part - hi.astype(jnp.float32)).astype(jnp.bfloat16)


def products(rows, upper_ref, lower_ref, hi_ref, lo_ref):
    half = RADIX // 2

    def spectrum(row, depth, width):
        hi, lo = hi_ref[row, :depth], lo_ref[row, :depth]
        upper, lower = upper_ref[:depth, :width], lower_ref[:depth, :width]
        out = jnp.dot(hi, upper, preferred_element_type=jnp.float32)
        out += jnp.dot(hi, lower, preferred_element_type=jnp.float32)
        return out + jnp.dot(lo, upper, preferred_element_type=jnp.float32)

    most = spectrum(slice(0, (half - 1) * rows), 2 * INNER, 4 * LANES)
    middle = spectrum(slice((half - 1) * rows, half * rows), 2 * INNER, 2 * LANES)
    first = spectrum(slice(half * rows, (half + 1) * rows), INNER, 2 * LANES)
    return first, middle, most


def finish(core_ref, rows, spectra, mine_ref, other_ref):
    half = RADIX // 2
    first, middle, most = spectra

    def part(f, k):
        if f == 0:
            return first[:, k * LANES:(k + 1) * LANES]
        if f == half:
            return middle[:, k * LANES:(k + 1) * LANES]
        g, base = (f, 0) if f < half else (RADIX - f, 2)
        return most[(g - 1) * rows:g * rows, (base + k) * LANES:(base + k + 1) * LANES]

    power = None
    for f in range(RADIX):
        re, im = part(f, 0), part(f, 1)
        both = re * re + im * im
        power = both if power is None else power + both
    power = power + pltpu.roll(power, 64, 1)
    power = power + pltpu.roll(power, 32, 1)
    scale = 1.0 / jnp.sqrt(power * (1.0 / BAND) + 1e-06)
    low = core_ref[0] == 0
    for block in range(rows // 8):
        r = slice(block * 8, block * 8 + 8)
        halves = []
        for h in range(2):
            tiles = [part(h * 8 + f, k)[r] * scale[r] for k in range(2) for f in range(8)]
            halves.append(jnp.transpose(jnp.stack(tiles, axis=0), (1, 0, 2)))
        mine_ref[r] = jnp.where(low, halves[0], halves[1]).astype(jnp.bfloat16)
        other_ref[r] = jnp.where(low, halves[1], halves[0]).astype(jnp.bfloat16)


def whiten(core, samples, twiddle, upper, lower, per):
    rows = samples.shape[1]
    out = jax.ShapeDtypeStruct((rows, NSEG * HALF_ROWS, LANES), jnp.bfloat16)
    spec = pl.BlockSpec((rows, per * HALF_ROWS, LANES), lambda s, c: (0, s, 0))
    count = RADIX // 2 + 1
    return pl.pallas_call(
        whiten_kernel,
        out_shape=(out, out),
        grid_spec=pltpu.PrefetchScalarGridSpec(
            num_scalar_prefetch=1,
            grid=(NSEG // per,),
            in_specs=[
                pl.BlockSpec((per * SIDE, rows, SEGLEN // SIDE), lambda s, c: (s, 0, 0)),
                pl.BlockSpec((2, RADIX, INNER), lambda s, c: (0, 0, 0)),
                pl.BlockSpec((2 * INNER, 4 * LANES), lambda s, c: (0, 0)),
                pl.BlockSpec((2 * INNER, 4 * LANES), lambda s, c: (0, 0)),
            ],
            out_specs=(spec, spec),
            scratch_shapes=[pltpu.VMEM((count * rows, 2 * INNER), jnp.bfloat16)] * (2 * per),
        ),
        compiler_params=pltpu.CompilerParams(vmem_limit_bytes=48 << 20),
        name="whiten",
    )(core, samples, twiddle, upper, lower)


GROUP = 8
CHUNK = 128


def load_pieces(pieces, targets, sems):
    copies = []
    n = 0
    for group, target in zip(pieces, targets):
        at = 0
        for piece in group:
            copies.append(pltpu.make_async_copy(piece, target.at[at:at + piece.shape[0]], sems.at[n]))
            at += piece.shape[0]
            n += 1
    for copy in copies:
        copy.start()
    return copies


def cross_slots(count, src_ref, rcv_ref, row_of, sources_ref, receivers_ref, cross_ref):
    def group(g, carry):
        for u in range(GROUP):
            i = g * GROUP + u
            a = sources_ref[src_ref[i]].astype(jnp.float32)
            b = receivers_ref[rcv_ref[i]].astype(jnp.float32)
            re = im = None
            for s in range(NSEG):
                ar, ai = a[s * 16:s * 16 + 8], a[s * 16 + 8:s * 16 + 16]
                br, bi = b[s * 16:s * 16 + 8], b[s * 16 + 8:s * 16 + 16]
                r = ar * br + ai * bi
                m = ai * br - ar * bi
                re = r if re is None else re + r
                im = m if im is None else im + m
            row = row_of(i)
            at = pl.multiple_of(row * HALF_ROWS, HALF_ROWS)
            cross_ref[pl.ds(at, 8), :] = re
            cross_ref[pl.ds(at + 8, 8), :] = im
        return carry

    lax.fori_loop(0, (count + GROUP - 1) // GROUP, group, 0)


def lags_of(cross_ref, first, count, table_ref):
    cross = jnp.concatenate(
        [cross_ref[pl.ds(first * HALF_ROWS + g, count, stride=HALF_ROWS), :].astype(jnp.bfloat16) for g in range(HALF_ROWS)],
        axis=1,
    )
    return jnp.dot(cross, table_ref[...], preferred_element_type=jnp.float32)


def near_kernel(count_ref, src_ref, rcv_ref, slot_ref, *refs):
    pieces = refs[:8]
    table_ref, out_ref, sources_ref, receivers_ref, cross_ref, sems = refs[8:]
    copies = load_pieces((pieces[:6], pieces[6:]), (sources_ref, receivers_ref), sems)
    cross_ref[...] = jnp.zeros_like(cross_ref)
    for copy in copies:
        copy.wait()
    cross_slots(count_ref[0], src_ref, rcv_ref, lambda i: slot_ref[i], sources_ref, receivers_ref, cross_ref)
    out_ref[...] = lags_of(cross_ref, 0, out_ref.shape[0], table_ref)


def far_kernel(count_ref, src_ref, rcv_ref, slot_ref, *refs):
    pieces = refs[:4]
    table_ref, near_ref, out_ref, sources_ref, receivers_ref, cross_ref, rows_ref, product_ref, sems = refs[4:]
    copies = load_pieces((pieces[:2], pieces[2:]), (sources_ref, receivers_ref), sems)
    slots = near_ref.shape[0]
    rows_ref[0:slots, :] = near_ref[...]
    for copy in copies:
        copy.wait()
    count = count_ref[0]
    cross_slots(count, src_ref, rcv_ref, lambda i: i, sources_ref, receivers_ref, cross_ref)

    def chunk(c, carry):
        first = pl.multiple_of(c * CHUNK, CHUNK)
        product_ref[...] = lags_of(cross_ref, first, CHUNK, table_ref)

        def place(g, inner):
            for u in range(GROUP):
                i = g * GROUP + u
                rows_ref[pl.ds(slot_ref[first + i], 1), :] = product_ref[pl.ds(i, 1), :]
            return inner

        return lax.fori_loop(0, (jnp.minimum(count - first, CHUNK) + GROUP - 1) // GROUP, place, carry)

    lax.fori_loop(0, (count + CHUNK - 1) // CHUNK, chunk, 0)
    out_ref[...] = rows_ref[0:slots, :].reshape(out_ref.shape).astype(jnp.bfloat16)


def correlate(kernel, lists, pieces, receivers, blocks, shape, dtype, extra):
    slots = lists[1].shape[0]
    row = pieces[0].shape[1:]
    whole = lambda a: pl.BlockSpec(a.shape, lambda *_: (0,) * a.ndim)
    return pl.pallas_call(
        kernel,
        out_shape=jax.ShapeDtypeStruct(shape, dtype),
        grid_spec=pltpu.PrefetchScalarGridSpec(
            num_scalar_prefetch=4,
            grid=(1,),
            in_specs=[pl.BlockSpec(memory_space=pl.ANY)] * (len(pieces) + len(receivers)) + [whole(b) for b in blocks],
            out_specs=pl.BlockSpec(shape, lambda *_: (0,) * len(shape)),
            scratch_shapes=[
                pltpu.VMEM((sum(p.shape[0] for p in pieces),) + row, jnp.bfloat16),
                pltpu.VMEM((sum(p.shape[0] for p in receivers),) + row, jnp.bfloat16),
                pltpu.VMEM(((slots + GROUP) * HALF_ROWS, LANES), jnp.float32),
                *extra,
                pltpu.SemaphoreType.DMA((len(pieces) + len(receivers),)),
            ],
        ),
        compiler_params=pltpu.CompilerParams(vmem_limit_bytes=40 << 20),
    )(*lists, *pieces, *receivers, *blocks)


def pick_kernel(wanted_ref, raw_ref, taper_ref, out_ref, rows_ref, sems):
    rows = rows_ref.shape[0]
    copies = [
        pltpu.make_async_copy(raw_ref.at[pl.ds(wanted_ref[r], 1), :], rows_ref.at[pl.ds(r, 1), :], sems.at[r])
        for r in range(rows)
    ]
    for copy in copies:
        copy.start()
    for copy in copies:
        copy.wait()
    value = (rows_ref[...] * taper_ref[...]).astype(jnp.bfloat16)
    for g in range(out_ref.shape[0]):
        out_ref[g] = value


def pick_rows(wanted, raw_window, taper, copies):
    rows, span = wanted.shape[0], raw_window.shape[1]
    return pl.pallas_call(
        pick_kernel,
        out_shape=jax.ShapeDtypeStruct((copies, rows, span), jnp.bfloat16),
        grid_spec=pltpu.PrefetchScalarGridSpec(
            num_scalar_prefetch=1,
            grid=(1,),
            in_specs=[pl.BlockSpec(memory_space=pl.ANY), pl.BlockSpec((1, span), lambda *_: (0, 0))],
            out_specs=pl.BlockSpec((copies, rows, span), lambda *_: (0, 0, 0)),
            scratch_shapes=[pltpu.VMEM((rows, span), jnp.float32), pltpu.SemaphoreType.DMA((rows,))],
        ),
        name="pick",
    )(wanted, raw_window, taper.reshape(1, span))


def shift(value, axis, step):
    if axis == "core":
        return lax.ppermute(value, "gx", [(g, g ^ 1) for g in range(2 * SIDE)])
    return lax.ppermute(value, "gx", [(g, (g + 2 * step) % (2 * SIDE)) for g in range(2 * SIDE)])


def gather_ring(value, axis):
    return jnp.stack([value] + [shift(value, axis, d) for d in (1, 2, 3)], axis=0)


def program(raw_window, source_ids, pair_source, pair_holder, pair_receiver):
    groups = lax.axis_size("gy")
    devices = lax.axis_size("gx") * groups
    gx, gy = lax.axis_index("gx"), lax.axis_index("gy")
    place = {"core": gx % 2, "y": gx // 2}
    core = place["core"]
    here = gx * groups + gy
    span = raw_window.shape[1]
    channels = raw_window.shape[0] // groups
    sample = (gy * span + jnp.arange(span, dtype=jnp.int32)) % SEGLEN
    taper = jnp.sin(math.pi * (sample.astype(jnp.float32) + 0.5) / SEGLEN) ** 2

    pairs = pair_source.shape[0]
    holder = pair_holder[:, 0]
    order = jnp.arange(pairs, dtype=jnp.int32)
    packed = (holder * channels + pair_receiver) * 256 + pair_source
    notes = jnp.concatenate([packed, source_ids])
    notes = jnp.broadcast_to(notes[None], (groups,) + notes.shape)
    notes = lax.all_to_all(notes, "gy", split_axis=0, concat_axis=0, tiled=True)
    wanted = (notes[:, pairs:] - gx * groups * channels).reshape(-1)
    notes = notes[:, :pairs]
    first = pick_rows(wanted, raw_window, taper, groups)
    first = lax.all_to_all(first, "gy", split_axis=0, concat_axis=0, tiled=True)
    tapered = (raw_window * taper[None, :]).astype(jnp.bfloat16)
    samples = lax.all_to_all(tapered.reshape(groups, channels, span), "gy", split_axis=0, concat_axis=0, tiled=True)
    notes = gather_ring(notes, "y")
    notes = jnp.stack([notes, shift(notes, "core", 1)], axis=0).reshape(devices, pairs)

    twiddle = twiddle_table()
    upper, lower = inner_table()
    near0, away = whiten(core.reshape(1), first, twiddle, upper, lower, NSEG)
    near1 = shift(away, "core", 1)
    ahead0 = shift(near0, "y", 1)
    behind0 = shift(near0, "y", 3)
    ahead1 = shift(near1, "y", 1)
    behind1 = shift(near1, "y", 3)
    far0 = shift(ahead0, "y", 1)
    far1 = shift(behind1, "y", 3)

    notes, late, _ = lax.optimization_barrier((notes, core, near1))
    table = inverse_table(late, late - core)

    samples = pltpu.with_memory_space_constraint(samples, pltpu.MemorySpace.HBM)
    mine, other = whiten(core.reshape(1), samples, twiddle, upper, lower, 2)
    sister = shift(other, "core", 1)

    dev = jnp.arange(devices, dtype=jnp.int32)
    own = (
        (dev // (SIDE * groups) ^ late) + (place["y"] - dev // groups % SIDE) % SIDE * 2
    ) * groups + dev % groups
    each = channels * 256
    key = notes // each
    entry = order[None, :] * each + notes % each + 1
    first_last = []
    for name in (here, here ^ groups):
        match = key == name
        high = jnp.max(jnp.where(match, entry, 0), axis=1)
        low = jnp.max(jnp.where(match, pairs * each + 1 - entry, 0), axis=1)
        low = jnp.where(low > 0, pairs * each + 1 - low, 0)
        first_last += [low, jnp.where(high > low, high, 0)]
    found = jnp.stack(first_last)
    asked = jnp.sum(jnp.where(own[None, None, :] == dev[None, :, None], found[:, None, :], 0), axis=2)
    valid = asked > 0
    asked = jnp.maximum(asked - 1, 0) % each
    slots = asked.size
    source_no = asked % 256
    source_gx = source_no // (2 * groups)
    rel_y = (place["y"] - source_gx // 2) % SIDE
    far = rel_y == 2
    piece = jnp.where(far, 0, jnp.minimum(rel_y, 2))
    source_at = (piece * 2 + (source_gx % 2 ^ core)) * (2 * groups) + source_no % (2 * groups)
    kind = jnp.arange(4, dtype=jnp.int32)[:, None]
    slot_no = dev[None, :] * 4 + kind
    receiver_at = asked // 256 + kind // 2 * channels
    entry = ((slot_no - slots) * 256 + receiver_at) * 256 + source_at
    index = jnp.arange(slots, dtype=jnp.int32)

    def compact(chosen):
        chosen = chosen.reshape(-1)
        spot = jnp.sum((chosen[None, :] & (index[None, :] < index[:, None])).astype(jnp.int32), axis=1)
        hit = chosen[None, :] & (spot[None, :] == index[:, None])
        line = jnp.sum(jnp.where(hit, entry.reshape(1, -1), 0), axis=1) + slots * 65536
        return jnp.sum(chosen.astype(jnp.int32)).reshape(1), line % 256, line // 256 % 256, line // 65536

    near_lists = compact(valid & ~far)
    far_lists = compact(valid & far)

    receivers = [mine, sister]
    near = correlate(
        near_kernel, near_lists, [near0, near1, ahead0, ahead1, behind0, behind1], receivers, [table], (slots, NLAG), jnp.float32, []
    )
    extra = [pltpu.VMEM((slots + GROUP, NLAG), jnp.float32), pltpu.VMEM((CHUNK, NLAG), jnp.float32)]
    partial = correlate(far_kernel, far_lists, [far0, far1], receivers, [table, near], (devices, 4, NLAG), jnp.bfloat16, extra)
    returned = lax.all_to_all(partial, ("gx", "gy"), split_axis=0, concat_axis=0, tiled=True)
    returned = returned.reshape(devices * 4, NLAG)
    same = (holder[:, None] == holder[None, :]) & (order[None, :] < order[:, None])
    rank = jnp.sum(same.astype(jnp.int32), axis=1)
    row = jnp.arange(4 * devices, dtype=jnp.int32)
    row_dev, row_rel, row_rank = row // 4, row // 2 % 2, row % 2
    row_holder = jnp.where(row_rel == 0, row_dev, row_dev ^ groups)
    pick = (row_holder[None, :] == holder[:, None]) & (row_rank[None, :] == rank[:, None])
    return jnp.dot(pick.astype(jnp.bfloat16), returned, preferred_element_type=jnp.float32)


def solution(mesh):
    return jax.shard_map(
        program,
        mesh=mesh,
        in_specs=(
            P("gx", "gy"),
            P(("gx", "gy")),
            P(("gx", "gy")),
            P(("gx", "gy"), None),
            P(("gx", "gy")),
        ),
        out_specs=P(("gx", "gy"), None),
        check_vma=False,
    )
```

```python
import math

import jax
import jax.numpy as jnp
from jax import lax
from jax.experimental import pallas as pl
from jax.experimental.pallas import tpu as pltpu
from jax.sharding import PartitionSpec as P


NBIN = 2048
SEGLEN = 4096
NSEG = 4
BAND = 64
NLAG = 512
SIDE = 4
SOURCES = 256
PER_DEVICE = 64
RADIX = 16
INNER = SEGLEN // RADIX
LANES = 128
HALF_ROWS = 2 * (RADIX // 2)


def split_table(table):
    upper = table.astype(jnp.bfloat16)
    lower = (table - upper.astype(jnp.float32)).astype(jnp.bfloat16)
    return (upper, lower)


def lane_bins():
    lane = jnp.arange(LANES, dtype=jnp.int32)
    return 4 * (lane % 32) + lane // 32


def inner_table():
    times = jnp.arange(INNER, dtype=jnp.int32)
    low = lane_bins()
    high = INNER - 1 - low
    turn = 2.0 * math.pi / INNER

    def block(bins, sign):
        angle = (times[:, None] * bins[None, :] % INNER).astype(jnp.float32) * turn
        cos, sin = jnp.cos(angle), jnp.sin(angle)
        top = jnp.concatenate([cos, -sign * sin], axis=1)
        bottom = jnp.concatenate([sin, sign * cos], axis=1)
        return jnp.concatenate([top, bottom], axis=0)

    return split_table(jnp.concatenate([block(low, 1.0), block(high, -1.0)], axis=1))


def twiddle_table():
    rows = jnp.arange(RADIX, dtype=jnp.int32)
    times = jnp.arange(INNER, dtype=jnp.int32)
    angle = (rows[:, None] * times[None, :] % SEGLEN).astype(jnp.float32) * (2.0 * math.pi / SEGLEN)
    return jnp.stack([jnp.cos(angle), -jnp.sin(angle)], axis=0)


def turns(count, lags):
    angle = (count[:, None] * lags[None, :] % SEGLEN).astype(jnp.float32) * (2.0 * math.pi / SEGLEN)
    return jnp.cos(angle), jnp.sin(angle)


def inverse_table(core, zero):
    outer = core * (RADIX // 2) + jnp.arange(RADIX // 2, dtype=jnp.int32)
    inner = RADIX * lane_bins() + zero
    lags = (jnp.arange(NLAG, dtype=jnp.int32) - NLAG // 2) % SEGLEN
    (c1, s1), (c2, s2) = lax.optimization_barrier((turns(outer, lags), turns(inner, lags)))
    c1, s1, c2, s2 = c1[:, None], s1[:, None], c2[None], s2[None]
    bins = outer[:, None, None] + inner[None, :, None]
    weight = jnp.where(bins == 0, 1.0, 2.0).astype(jnp.float32) * (0.5 / math.sqrt(NSEG * NBIN))
    table = jnp.stack([weight * (c1 * c2 - s1 * s2), -weight * (s1 * c2 + c1 * s2)], axis=0)
    return table.astype(jnp.bfloat16).reshape(NBIN, NLAG)


def real_dft(values):
    n = len(values)
    if n == 2:
        return [(values[0] + values[1], None), (values[0] - values[1], None)]
    even = real_dft(values[0::2])
    odd = real_dft(values[1::2])
    out = [None] * (n // 2 + 1)
    for k in range(n // 4 + 1):
        er, ei = even[k]
        pr, pi = odd[k]
        c, s = math.cos(2 * math.pi * k / n), math.sin(2 * math.pi * k / n)
        if k == 0:
            out[0] = (er + pr, None)
            out[n // 2] = (er - pr, None)
        elif 4 * k == n:
            out[k] = (er, -pr)
        else:
            if 8 * k == n:
                tr, ti = (pr + pi) * c, (pi - pr) * c
            else:
                tr, ti = pr * c + pi * s, pi * c - pr * s
            out[k] = (er + tr, ei + ti)
            out[n // 2 - k] = (er - tr, ti - ei)
    return out


def whiten_kernel(core_ref, x_ref, tw_ref, upper_ref, lower_ref, mine_ref, other_ref, *scratch):
    count = x_ref.shape[0] // SIDE
    parts = [(x_ref.at[n * SIDE:(n + 1) * SIDE], scratch[2 * n], scratch[2 * n + 1]) for n in range(count)]
    butterflies(tw_ref, *parts[0])
    for n in range(count):
        spectra = products(x_ref.shape[1], upper_ref, lower_ref, *parts[n][1:])
        if n + 1 < count:
            butterflies(tw_ref, *parts[n + 1])
        at = slice(n * HALF_ROWS, (n + 1) * HALF_ROWS)
        finish(core_ref, x_ref.shape[1], spectra, mine_ref.at[:, at], other_ref.at[:, at])


def butterflies(tw_ref, x_ref, hi_ref, lo_ref):
    rows = x_ref.shape[1]
    half = RADIX // 2
    where = lambda f: (f - 1) % (half + 1)
    for block in range(rows // 16):
        r = slice(block * 16, block * 16 + 16)
        for k in range(INNER // LANES):
            slices = []
            for t in range(RADIX):
                at = (t % SIDE) * INNER + k * LANES
                slices.append(x_ref[t // SIDE, r, at:at + LANES].astype(jnp.float32))
            outer = real_dft(slices)
            for f in range(half + 1):
                re, im = outer[f]
                lanes = slice(k * LANES, (k + 1) * LANES)
                c, s = tw_ref[0, f:f + 1, lanes], tw_ref[1, f:f + 1, lanes]
                if f == 0:
                    parts = (re,)
                elif im is None:
                    parts = (re * c, re * s)
                else:
                    parts = (re * c - im * s, re * s + im * c)
                row = slice(where(f) * rows + block * 16, where(f) * rows + block * 16 + 16)
                for n, part in enumerate(parts):
                    hi = part.astype(jnp.bfloat16)
                    at = slice(n * INNER + k * LANES, n * INNER + (k + 1) * LANES)
                    hi_ref[row, at] = hi
                    lo_ref[row, at] = (part - hi.astype(jnp.float32)).astype(jnp.bfloat16)


def products(rows, upper_ref, lower_ref, hi_ref, lo_ref):
    half = RADIX // 2

    def spectrum(row, depth, width):
        hi, lo = hi_ref[row, :depth], lo_ref[row, :depth]
        upper, lower = upper_ref[:depth, :width], lower_ref[:depth, :width]
        out = jnp.dot(hi, upper, preferred_element_type=jnp.float32)
        out += jnp.dot(hi, lower, preferred_element_type=jnp.float32)
        return out + jnp.dot(lo, upper, preferred_element_type=jnp.float32)

    most = spectrum(slice(0, (half - 1) * rows), 2 * INNER, 4 * LANES)
    middle = spectrum(slice((half - 1) * rows, half * rows), 2 * INNER, 2 * LANES)
    first = spectrum(slice(half * rows, (half + 1) * rows), INNER, 2 * LANES)
    return first, middle, most


def finish(core_ref, rows, spectra, mine_ref, other_ref):
    half = RADIX // 2
    first, middle, most = spectra

    def part(f, k):
        if f == 0:
            return first[:, k * LANES:(k + 1) * LANES]
        if f == half:
            return middle[:, k * LANES:(k + 1) * LANES]
        g, base = (f, 0) if f < half else (RADIX - f, 2)
        return most[(g - 1) * rows:g * rows, (base + k) * LANES:(base + k + 1) * LANES]

    power = None
    for f in range(RADIX):
        re, im = part(f, 0), part(f, 1)
        both = re * re + im * im
        power = both if power is None else power + both
    power = power + pltpu.roll(power, 64, 1)
    power = power + pltpu.roll(power, 32, 1)
    scale = 1.0 / jnp.sqrt(power * (1.0 / BAND) + 1e-06)
    low = core_ref[0] == 0
    for block in range(rows // 8):
        r = slice(block * 8, block * 8 + 8)
        halves = []
        for h in range(2):
            tiles = [part(h * 8 + f, k)[r] * scale[r] for k in range(2) for f in range(8)]
            halves.append(jnp.transpose(jnp.stack(tiles, axis=0), (1, 0, 2)))
        mine_ref[r] = jnp.where(low, halves[0], halves[1]).astype(jnp.bfloat16)
        other_ref[r] = jnp.where(low, halves[1], halves[0]).astype(jnp.bfloat16)


def whiten(core, samples, twiddle, upper, lower, per):
    rows = samples.shape[1]
    out = jax.ShapeDtypeStruct((rows, NSEG * HALF_ROWS, LANES), jnp.bfloat16)
    spec = pl.BlockSpec((rows, per * HALF_ROWS, LANES), lambda s, c: (0, s, 0))
    count = RADIX // 2 + 1
    return pl.pallas_call(
        whiten_kernel,
        out_shape=(out, out),
        grid_spec=pltpu.PrefetchScalarGridSpec(
            num_scalar_prefetch=1,
            grid=(NSEG // per,),
            in_specs=[
                pl.BlockSpec((per * SIDE, rows, SEGLEN // SIDE), lambda s, c: (s, 0, 0)),
                pl.BlockSpec((2, RADIX, INNER), lambda s, c: (0, 0, 0)),
                pl.BlockSpec((2 * INNER, 4 * LANES), lambda s, c: (0, 0)),
                pl.BlockSpec((2 * INNER, 4 * LANES), lambda s, c: (0, 0)),
            ],
            out_specs=(spec, spec),
            scratch_shapes=[pltpu.VMEM((count * rows, 2 * INNER), jnp.bfloat16)] * (2 * per),
        ),
        compiler_params=pltpu.CompilerParams(vmem_limit_bytes=48 << 20),
        name="whiten",
    )(core, samples, twiddle, upper, lower)


GROUP = 8
CHUNK = 128


def load_pieces(pieces, targets, sems):
    copies = []
    n = 0
    for group, target in zip(pieces, targets):
        at = 0
        for piece in group:
            copies.append(pltpu.make_async_copy(piece, target.at[at:at + piece.shape[0]], sems.at[n]))
            at += piece.shape[0]
            n += 1
    for copy in copies:
        copy.start()
    return copies


def cross_slots(count, src_ref, rcv_ref, row_of, sources_ref, receivers_ref, cross_ref):
    def group(g, carry):
        for u in range(GROUP):
            i = g * GROUP + u
            a = sources_ref[src_ref[i]].astype(jnp.float32)
            b = receivers_ref[rcv_ref[i]].astype(jnp.float32)
            re = im = None
            for s in range(NSEG):
                ar, ai = a[s * 16:s * 16 + 8], a[s * 16 + 8:s * 16 + 16]
                br, bi = b[s * 16:s * 16 + 8], b[s * 16 + 8:s * 16 + 16]
                r = ar * br + ai * bi
                m = ai * br - ar * bi
                re = r if re is None else re + r
                im = m if im is None else im + m
            row = row_of(i)
            at = pl.multiple_of(row * HALF_ROWS, HALF_ROWS)
            cross_ref[pl.ds(at, 8), :] = re
            cross_ref[pl.ds(at + 8, 8), :] = im
        return carry

    lax.fori_loop(0, (count + GROUP - 1) // GROUP, group, 0)


def lags_of(cross_ref, first, count, table_ref):
    cross = jnp.concatenate(
        [cross_ref[pl.ds(first * HALF_ROWS + g, count, stride=HALF_ROWS), :].astype(jnp.bfloat16) for g in range(HALF_ROWS)],
        axis=1,
    )
    return jnp.dot(cross, table_ref[...], preferred_element_type=jnp.float32)


def near_kernel(count_ref, src_ref, rcv_ref, slot_ref, *refs):
    pieces = refs[:8]
    table_hbm, out_ref, sources_ref, receivers_ref, cross_ref, table_ref, sems = refs[8:]
    *copies, table_copy = load_pieces(
        (pieces[:6], pieces[6:], (table_hbm,)), (sources_ref, receivers_ref, table_ref), sems
    )
    cross_ref[...] = jnp.zeros_like(cross_ref)
    for copy in copies:
        copy.wait()
    cross_slots(count_ref[0], src_ref, rcv_ref, lambda i: slot_ref[i], sources_ref, receivers_ref, cross_ref)
    table_copy.wait()
    out_ref[...] = lags_of(cross_ref, 0, out_ref.shape[0], table_ref)


def far_kernel(count_ref, src_ref, rcv_ref, slot_ref, *refs):
    pieces = refs[:4]
    table_hbm, near_hbm, out_ref, sources_ref, receivers_ref, cross_ref, table_ref, rows_ref, product_ref, sems = refs[4:]
    slots = near_hbm.shape[0]
    *copies, table_copy, near_copy = load_pieces(
        (pieces[:2], pieces[2:], (table_hbm,), (near_hbm,)), (sources_ref, receivers_ref, table_ref, rows_ref), sems
    )
    for copy in copies:
        copy.wait()
    count = count_ref[0]
    cross_slots(count, src_ref, rcv_ref, lambda i: i, sources_ref, receivers_ref, cross_ref)

    table_copy.wait()
    near_copy.wait()

    def chunk(c, carry):
        first = pl.multiple_of(c * CHUNK, CHUNK)
        product_ref[...] = lags_of(cross_ref, first, CHUNK, table_ref)

        def place(g, inner):
            for u in range(GROUP):
                i = g * GROUP + u
                rows_ref[pl.ds(slot_ref[first + i], 1), :] = product_ref[pl.ds(i, 1), :]
            return inner

        return lax.fori_loop(0, (jnp.minimum(count - first, CHUNK) + GROUP - 1) // GROUP, place, carry)

    lax.fori_loop(0, (count + CHUNK - 1) // CHUNK, chunk, 0)
    out_ref[...] = rows_ref[0:slots, :].reshape(out_ref.shape).astype(jnp.bfloat16)


def correlate(kernel, lists, pieces, receivers, blocks, shape, dtype, extra):
    slots = lists[1].shape[0]
    row = pieces[0].shape[1:]
    inputs = len(pieces) + len(receivers) + len(blocks)
    return pl.pallas_call(
        kernel,
        out_shape=jax.ShapeDtypeStruct(shape, dtype),
        grid_spec=pltpu.PrefetchScalarGridSpec(
            num_scalar_prefetch=4,
            grid=(1,),
            in_specs=[pl.BlockSpec(memory_space=pl.ANY)] * inputs,
            out_specs=pl.BlockSpec(shape, lambda *_: (0,) * len(shape)),
            scratch_shapes=[
                pltpu.VMEM((sum(p.shape[0] for p in pieces),) + row, jnp.bfloat16),
                pltpu.VMEM((sum(p.shape[0] for p in receivers),) + row, jnp.bfloat16),
                pltpu.VMEM(((slots + GROUP) * HALF_ROWS, LANES), jnp.float32),
                pltpu.VMEM(blocks[0].shape, blocks[0].dtype),
                *extra,
                pltpu.SemaphoreType.DMA((inputs,)),
            ],
        ),
        compiler_params=pltpu.CompilerParams(vmem_limit_bytes=40 << 20),
    )(*lists, *pieces, *receivers, *blocks)


def pack_kernel(ids_ref, holder_ref, receiver_ref, source_ref, out_ref):
    pairs = holder_ref.shape[1]
    per = ids_ref.shape[0]
    packed = (holder_ref[...] * PER_DEVICE + receiver_ref[...]) * SOURCES + source_ref[...]
    lane = lax.broadcasted_iota(jnp.int32, (1, pairs), 1)
    ids = jnp.zeros((1, pairs), jnp.int32)
    for n in range(per):
        ids = jnp.where(lane == n, ids_ref[n], ids)
    row = jnp.concatenate([packed, ids], axis=1)
    for g in range(out_ref.shape[0]):
        out_ref[g] = row


def pack_notes(source_ids, holder, receiver, source, copies):
    pairs = holder.shape[0]
    line = lambda a: a.reshape(1, pairs)
    spec = pl.BlockSpec((1, pairs), lambda *_: (0, 0))
    return pl.pallas_call(
        pack_kernel,
        out_shape=jax.ShapeDtypeStruct((copies, 1, 2 * pairs), jnp.int32),
        grid_spec=pltpu.PrefetchScalarGridSpec(
            num_scalar_prefetch=1,
            grid=(1,),
            in_specs=[spec, spec, spec],
            out_specs=pl.BlockSpec((copies, 1, 2 * pairs), lambda *_: (0, 0, 0)),
        ),
        name="pack",
    )(source_ids, line(holder), line(receiver), line(source))


def pick_kernel(wanted_ref, raw_ref, taper_ref, out_ref, rows_ref, sems):
    rows = rows_ref.shape[0]
    copies = [
        pltpu.make_async_copy(raw_ref.at[pl.ds(wanted_ref[r], 1), :], rows_ref.at[pl.ds(r, 1), :], sems.at[r])
        for r in range(rows)
    ]
    for copy in copies:
        copy.start()
    for copy in copies:
        copy.wait()
    value = (rows_ref[...] * taper_ref[...]).astype(jnp.bfloat16)
    for g in range(out_ref.shape[0]):
        out_ref[g] = value


def pick_rows(wanted, raw_window, taper, copies):
    rows, span = wanted.shape[0], raw_window.shape[1]
    return pl.pallas_call(
        pick_kernel,
        out_shape=jax.ShapeDtypeStruct((copies, rows, span), jnp.bfloat16),
        grid_spec=pltpu.PrefetchScalarGridSpec(
            num_scalar_prefetch=1,
            grid=(1,),
            in_specs=[pl.BlockSpec(memory_space=pl.ANY), pl.BlockSpec((1, span), lambda *_: (0, 0))],
            out_specs=pl.BlockSpec((copies, rows, span), lambda *_: (0, 0, 0)),
            scratch_shapes=[pltpu.VMEM((rows, span), jnp.float32), pltpu.SemaphoreType.DMA((rows,))],
        ),
        name="pick",
    )(wanted, raw_window, taper.reshape(1, span))


def shift(value, axis, step):
    if axis == "core":
        return lax.ppermute(value, "gx", [(g, g ^ 1) for g in range(2 * SIDE)])
    return lax.ppermute(value, "gx", [(g, (g + 2 * step) % (2 * SIDE)) for g in range(2 * SIDE)])


def gather_ring(value, axis):
    return jnp.stack([value] + [shift(value, axis, d) for d in (1, 2, 3)], axis=0)


def program(raw_window, source_ids, pair_source, pair_holder, pair_receiver):
    groups = lax.axis_size("gy")
    devices = lax.axis_size("gx") * groups
    gx, gy = lax.axis_index("gx"), lax.axis_index("gy")
    place = {"core": gx % 2, "y": gx // 2}
    core = place["core"]
    here = gx * groups + gy
    span = raw_window.shape[1]
    channels = raw_window.shape[0] // groups
    sample = (gy * span + jnp.arange(span, dtype=jnp.int32)) % SEGLEN
    taper = jnp.sin(math.pi * (sample.astype(jnp.float32) + 0.5) / SEGLEN) ** 2

    pairs = pair_source.shape[0]
    holder = pair_holder[:, 0]
    order = jnp.arange(pairs, dtype=jnp.int32)
    per = source_ids.shape[0]
    notes = pack_notes(source_ids, holder, pair_receiver, pair_source, groups)
    notes = lax.all_to_all(notes, "gy", split_axis=0, concat_axis=0, tiled=True)
    wanted = (notes[:, 0, pairs:pairs + per] - gx * groups * channels).reshape(-1)
    notes = notes[:, 0, :pairs]
    first = pick_rows(wanted, raw_window, taper, groups)
    first = lax.all_to_all(first, "gy", split_axis=0, concat_axis=0, tiled=True)
    tapered = (raw_window * taper[None, :]).astype(jnp.bfloat16)
    samples = lax.all_to_all(tapered.reshape(groups, channels, span), "gy", split_axis=0, concat_axis=0, tiled=True)
    notes = gather_ring(notes, "y")
    notes = jnp.stack([notes, shift(notes, "core", 1)], axis=0).reshape(devices, pairs)

    twiddle = twiddle_table()
    upper, lower = inner_table()
    near0, away = whiten(core.reshape(1), first, twiddle, upper, lower, NSEG)
    near1 = shift(away, "core", 1)
    ahead0 = shift(near0, "y", 1)
    behind0 = shift(near0, "y", 3)
    ahead1 = shift(near1, "y", 1)
    behind1 = shift(near1, "y", 3)
    far0 = shift(ahead0, "y", 1)
    far1 = shift(behind1, "y", 3)

    notes, late, _ = lax.optimization_barrier((notes, core, near1))
    table = inverse_table(late, late - core)

    samples = pltpu.with_memory_space_constraint(samples, pltpu.MemorySpace.HBM)
    mine, other = whiten(core.reshape(1), samples, twiddle, upper, lower, 2)
    sister = shift(other, "core", 1)

    dev = jnp.arange(devices, dtype=jnp.int32)
    own = (
        (dev // (SIDE * groups) ^ late) + (place["y"] - dev // groups % SIDE) % SIDE * 2
    ) * groups + dev % groups
    each = channels * 256
    key = notes // each
    entry = order[None, :] * each + notes % each + 1
    first_last = []
    for name in (here, here ^ groups):
        match = key == name
        high = jnp.max(jnp.where(match, entry, 0), axis=1)
        low = jnp.max(jnp.where(match, pairs * each + 1 - entry, 0), axis=1)
        low = jnp.where(low > 0, pairs * each + 1 - low, 0)
        first_last += [low, jnp.where(high > low, high, 0)]
    found = jnp.stack(first_last)
    asked = jnp.sum(jnp.where(own[None, None, :] == dev[None, :, None], found[:, None, :], 0), axis=2)
    valid = asked > 0
    asked = jnp.maximum(asked - 1, 0) % each
    slots = asked.size
    source_no = asked % 256
    source_gx = source_no // (2 * groups)
    rel_y = (place["y"] - source_gx // 2) % SIDE
    far = rel_y == 2
    piece = jnp.where(far, 0, jnp.minimum(rel_y, 2))
    source_at = (piece * 2 + (source_gx % 2 ^ core)) * (2 * groups) + source_no % (2 * groups)
    kind = jnp.arange(4, dtype=jnp.int32)[:, None]
    slot_no = dev[None, :] * 4 + kind
    receiver_at = asked // 256 + kind // 2 * channels
    entry = ((slot_no - slots) * 256 + receiver_at) * 256 + source_at
    index = jnp.arange(slots, dtype=jnp.int32)

    def compact(chosen):
        chosen = chosen.reshape(-1)
        spot = jnp.sum((chosen[None, :] & (index[None, :] < index[:, None])).astype(jnp.int32), axis=1)
        hit = chosen[None, :] & (spot[None, :] == index[:, None])
        line = jnp.sum(jnp.where(hit, entry.reshape(1, -1), 0), axis=1) + slots * 65536
        return jnp.sum(chosen.astype(jnp.int32)).reshape(1), line % 256, line // 256 % 256, line // 65536

    near_lists = compact(valid & ~far)
    far_lists = compact(valid & far)

    receivers = [mine, sister]
    near = correlate(
        near_kernel, near_lists, [near0, near1, ahead0, ahead1, behind0, behind1], receivers, [table], (slots, NLAG), jnp.float32, []
    )
    extra = [pltpu.VMEM((slots + GROUP, NLAG), jnp.float32), pltpu.VMEM((CHUNK, NLAG), jnp.float32)]
    partial = correlate(far_kernel, far_lists, [far0, far1], receivers, [table, near], (devices, 4, NLAG), jnp.bfloat16, extra)
    returned = lax.all_to_all(partial, ("gx", "gy"), split_axis=0, concat_axis=0, tiled=True)
    returned = returned.reshape(devices * 4, NLAG)
    same = (holder[:, None] == holder[None, :]) & (order[None, :] < order[:, None])
    rank = jnp.sum(same.astype(jnp.int32), axis=1)
    row = jnp.arange(4 * devices, dtype=jnp.int32)
    row_dev, row_rel, row_rank = row // 4, row // 2 % 2, row % 2
    row_holder = jnp.where(row_rel == 0, row_dev, row_dev ^ groups)
    pick = (row_holder[None, :] == holder[:, None]) & (row_rank[None, :] == rank[:, None])
    return jnp.dot(pick.astype(jnp.bfloat16), returned, preferred_element_type=jnp.float32)


def solution(mesh):
    return jax.shard_map(
        program,
        mesh=mesh,
        in_specs=(
            P("gx", "gy"),
            P(("gx", "gy")),
            P(("gx", "gy")),
            P(("gx", "gy"), None),
            P(("gx", "gy")),
        ),
        out_specs=P(("gx", "gy"), None),
        check_vma=False,
    )
```

```python
import math

import jax
import jax.numpy as jnp
from jax import lax
from jax.experimental import pallas as pl
from jax.experimental.pallas import tpu as pltpu
from jax.sharding import PartitionSpec as P


NBIN = 2048
SEGLEN = 4096
NSEG = 4
BAND = 64
NLAG = 512
SIDE = 4
SOURCES = 256
PER_DEVICE = 64
RADIX = 16
INNER = SEGLEN // RADIX
LANES = 128
HALF_ROWS = 2 * (RADIX // 2)


def split_table(table):
    upper = table.astype(jnp.bfloat16)
    lower = (table - upper.astype(jnp.float32)).astype(jnp.bfloat16)
    return (upper, lower)


def lane_bins():
    lane = jnp.arange(LANES, dtype=jnp.int32)
    return 4 * (lane % 32) + lane // 32


def inner_table():
    times = jnp.arange(INNER, dtype=jnp.int32)
    low = lane_bins()
    high = INNER - 1 - low
    turn = 2.0 * math.pi / INNER

    def block(bins, sign):
        angle = (times[:, None] * bins[None, :] % INNER).astype(jnp.float32) * turn
        cos, sin = jnp.cos(angle), jnp.sin(angle)
        top = jnp.concatenate([cos, -sign * sin], axis=1)
        bottom = jnp.concatenate([sin, sign * cos], axis=1)
        return jnp.concatenate([top, bottom], axis=0)

    return split_table(jnp.concatenate([block(low, 1.0), block(high, -1.0)], axis=1))


def twiddle_table():
    rows = jnp.arange(RADIX, dtype=jnp.int32)
    times = jnp.arange(INNER, dtype=jnp.int32)
    angle = (rows[:, None] * times[None, :] % SEGLEN).astype(jnp.float32) * (2.0 * math.pi / SEGLEN)
    return jnp.stack([jnp.cos(angle), -jnp.sin(angle)], axis=0)


def turns(count, lags):
    angle = (count[:, None] * lags[None, :] % SEGLEN).astype(jnp.float32) * (2.0 * math.pi / SEGLEN)
    return jnp.cos(angle), jnp.sin(angle)


def inverse_table(core, zero):
    outer = core * (RADIX // 2) + jnp.arange(RADIX // 2, dtype=jnp.int32)
    inner = RADIX * lane_bins() + zero
    lags = (jnp.arange(NLAG, dtype=jnp.int32) - NLAG // 2) % SEGLEN
    (c1, s1), (c2, s2) = lax.optimization_barrier((turns(outer, lags), turns(inner, lags)))
    c1, s1, c2, s2 = c1[:, None], s1[:, None], c2[None], s2[None]
    bins = outer[:, None, None] + inner[None, :, None]
    weight = jnp.where(bins == 0, 1.0, 2.0).astype(jnp.float32) * (0.5 / math.sqrt(NSEG * NBIN))
    table = jnp.stack([weight * (c1 * c2 - s1 * s2), -weight * (s1 * c2 + c1 * s2)], axis=0)
    return table.astype(jnp.bfloat16).reshape(NBIN, NLAG)


def real_dft(values):
    n = len(values)
    if n == 2:
        return [(values[0] + values[1], None), (values[0] - values[1], None)]
    even = real_dft(values[0::2])
    odd = real_dft(values[1::2])
    out = [None] * (n // 2 + 1)
    for k in range(n // 4 + 1):
        er, ei = even[k]
        pr, pi = odd[k]
        c, s = math.cos(2 * math.pi * k / n), math.sin(2 * math.pi * k / n)
        if k == 0:
            out[0] = (er + pr, None)
            out[n // 2] = (er - pr, None)
        elif 4 * k == n:
            out[k] = (er, -pr)
        else:
            if 8 * k == n:
                tr, ti = (pr + pi) * c, (pi - pr) * c
            else:
                tr, ti = pr * c + pi * s, pi * c - pr * s
            out[k] = (er + tr, ei + ti)
            out[n // 2 - k] = (er - tr, ti - ei)
    return out


def whiten_kernel(core_ref, x_ref, tw_ref, upper_ref, lower_ref, mine_ref, other_ref, *scratch):
    count = x_ref.shape[0] // SIDE
    parts = [(x_ref.at[n * SIDE:(n + 1) * SIDE], scratch[2 * n], scratch[2 * n + 1]) for n in range(count)]
    butterflies(tw_ref, *parts[0])
    for n in range(count):
        spectra = products(x_ref.shape[1], upper_ref, lower_ref, *parts[n][1:])
        if n + 1 < count:
            butterflies(tw_ref, *parts[n + 1])
        at = slice(n * HALF_ROWS, (n + 1) * HALF_ROWS)
        finish(core_ref, x_ref.shape[1], spectra, mine_ref.at[:, at], other_ref.at[:, at])


def butterflies(tw_ref, x_ref, hi_ref, lo_ref):
    rows = x_ref.shape[1]
    half = RADIX // 2
    where = lambda f: (f - 1) % (half + 1)
    for block in range(rows // 16):
        r = slice(block * 16, block * 16 + 16)
        for k in range(INNER // LANES):
            slices = []
            for t in range(RADIX):
                at = (t % SIDE) * INNER + k * LANES
                slices.append(x_ref[t // SIDE, r, at:at + LANES].astype(jnp.float32))
            outer = real_dft(slices)
            for f in range(half + 1):
                re, im = outer[f]
                lanes = slice(k * LANES, (k + 1) * LANES)
                c, s = tw_ref[0, f:f + 1, lanes], tw_ref[1, f:f + 1, lanes]
                if f == 0:
                    parts = (re,)
                elif im is None:
                    parts = (re * c, re * s)
                else:
                    parts = (re * c - im * s, re * s + im * c)
                row = slice(where(f) * rows + block * 16, where(f) * rows + block * 16 + 16)
                for n, part in enumerate(parts):
                    hi = part.astype(jnp.bfloat16)
                    at = slice(n * INNER + k * LANES, n * INNER + (k + 1) * LANES)
                    hi_ref[row, at] = hi
                    lo_ref[row, at] = (part - hi.astype(jnp.float32)).astype(jnp.bfloat16)


def products(rows, upper_ref, lower_ref, hi_ref, lo_ref):
    half = RADIX // 2

    def spectrum(row, depth, width):
        hi, lo = hi_ref[row, :depth], lo_ref[row, :depth]
        upper, lower = upper_ref[:depth, :width], lower_ref[:depth, :width]
        out = jnp.dot(hi, upper, preferred_element_type=jnp.float32)
        out += jnp.dot(hi, lower, preferred_element_type=jnp.float32)
        return out + jnp.dot(lo, upper, preferred_element_type=jnp.float32)

    most = spectrum(slice(0, (half - 1) * rows), 2 * INNER, 4 * LANES)
    middle = spectrum(slice((half - 1) * rows, half * rows), 2 * INNER, 2 * LANES)
    first = spectrum(slice(half * rows, (half + 1) * rows), INNER, 2 * LANES)
    return first, middle, most


def finish(core_ref, rows, spectra, mine_ref, other_ref):
    half = RADIX // 2
    first, middle, most = spectra

    def part(f, k):
        if f == 0:
            return first[:, k * LANES:(k + 1) * LANES]
        if f == half:
            return middle[:, k * LANES:(k + 1) * LANES]
        g, base = (f, 0) if f < half else (RADIX - f, 2)
        return most[(g - 1) * rows:g * rows, (base + k) * LANES:(base + k + 1) * LANES]

    power = None
    for f in range(RADIX):
        re, im = part(f, 0), part(f, 1)
        both = re * re + im * im
        power = both if power is None else power + both
    power = power + pltpu.roll(power, 64, 1)
    power = power + pltpu.roll(power, 32, 1)
    scale = 1.0 / jnp.sqrt(power * (1.0 / BAND) + 1e-06)
    low = core_ref[0] == 0
    for block in range(rows // 8):
        r = slice(block * 8, block * 8 + 8)
        halves = []
        for h in range(2):
            tiles = [part(h * 8 + f, k)[r] * scale[r] for k in range(2) for f in range(8)]
            halves.append(jnp.transpose(jnp.stack(tiles, axis=0), (1, 0, 2)))
        mine_ref[r] = jnp.where(low, halves[0], halves[1]).astype(jnp.bfloat16)
        other_ref[r] = jnp.where(low, halves[1], halves[0]).astype(jnp.bfloat16)


def whiten(core, samples, twiddle, upper, lower, per):
    rows = samples.shape[1]
    out = jax.ShapeDtypeStruct((rows, NSEG * HALF_ROWS, LANES), jnp.bfloat16)
    spec = pl.BlockSpec((rows, per * HALF_ROWS, LANES), lambda s, c: (0, s, 0))
    count = RADIX // 2 + 1
    return pl.pallas_call(
        whiten_kernel,
        out_shape=(out, out),
        grid_spec=pltpu.PrefetchScalarGridSpec(
            num_scalar_prefetch=1,
            grid=(NSEG // per,),
            in_specs=[
                pl.BlockSpec((per * SIDE, rows, SEGLEN // SIDE), lambda s, c: (s, 0, 0)),
                pl.BlockSpec((2, RADIX, INNER), lambda s, c: (0, 0, 0)),
                pl.BlockSpec((2 * INNER, 4 * LANES), lambda s, c: (0, 0)),
                pl.BlockSpec((2 * INNER, 4 * LANES), lambda s, c: (0, 0)),
            ],
            out_specs=(spec, spec),
            scratch_shapes=[pltpu.VMEM((count * rows, 2 * INNER), jnp.bfloat16)] * (2 * per),
        ),
        compiler_params=pltpu.CompilerParams(vmem_limit_bytes=24 << 20),
        name="whiten",
    )(core, samples, twiddle, upper, lower)


GROUP = 8
CHUNK = 128


def load_pieces(pieces, targets, sems):
    copies = []
    n = 0
    for group, target in zip(pieces, targets):
        at = 0
        for piece in group:
            copies.append(pltpu.make_async_copy(piece, target.at[at:at + piece.shape[0]], sems.at[n]))
            at += piece.shape[0]
            n += 1
    for copy in copies:
        copy.start()
    return copies


def cross_slots(start, stop, src_ref, rcv_ref, row_of, sources_ref, receivers_ref, cross_ref):
    last = src_ref.shape[0] - 1

    def group(g, carry):
        for u in range(GROUP):
            i = start + g * GROUP + u
            entry = jnp.minimum(i, last)
            a = sources_ref[src_ref[entry]].astype(jnp.float32)
            b = receivers_ref[rcv_ref[entry]].astype(jnp.float32)
            re = im = None
            for s in range(NSEG):
                ar, ai = a[s * 16:s * 16 + 8], a[s * 16 + 8:s * 16 + 16]
                br, bi = b[s * 16:s * 16 + 8], b[s * 16 + 8:s * 16 + 16]
                r = ar * br + ai * bi
                m = ai * br - ar * bi
                re = r if re is None else re + r
                im = m if im is None else im + m
            at = pl.multiple_of(row_of(i, entry) * HALF_ROWS, HALF_ROWS)
            cross_ref[pl.ds(at, 8), :] = re
            cross_ref[pl.ds(at + 8, 8), :] = im
        return carry

    lax.fori_loop(0, (stop - start + GROUP - 1) // GROUP, group, 0)


def lags_of(cross_ref, first, count, table_ref):
    cross = jnp.concatenate(
        [cross_ref[pl.ds(first * HALF_ROWS + g, count, stride=HALF_ROWS), :].astype(jnp.bfloat16) for g in range(HALF_ROWS)],
        axis=1,
    )
    return jnp.dot(cross, table_ref[...], preferred_element_type=jnp.float32)


def near_kernel(count_ref, src_ref, rcv_ref, slot_ref, *refs):
    pieces = refs[:6]
    mine_ref, sister_ref, table_ref, out_ref, sources_ref, cross_ref, sems = refs[6:]
    copies = load_pieces((pieces,), (sources_ref,), sems)
    cross_ref[...] = jnp.zeros_like(cross_ref)
    for copy in copies:
        copy.wait()
    slot_of = lambda i, entry: slot_ref[entry]
    cross_slots(0, count_ref[0], src_ref, rcv_ref, slot_of, sources_ref, mine_ref, cross_ref)
    cross_slots(count_ref[0], count_ref[1], src_ref, rcv_ref, slot_of, sources_ref, sister_ref, cross_ref)
    out_ref[...] = lags_of(cross_ref, 0, out_ref.shape[0], table_ref)


def far_kernel(count_ref, src_ref, rcv_ref, slot_ref, *refs):
    pieces = refs[:2]
    mine_ref, sister_ref, table_ref, near_ref, out_ref, sources_ref, cross_ref, rows_ref, product_ref, sems = refs[2:]
    slots = near_ref.shape[0]
    copies = load_pieces((pieces,), (sources_ref,), sems)
    rows_ref[0:slots, :] = near_ref[...]
    for copy in copies:
        copy.wait()
    count = count_ref[1]
    row_of = lambda i, entry: i
    cross_slots(0, count_ref[0], src_ref, rcv_ref, row_of, sources_ref, mine_ref, cross_ref)
    cross_slots(count_ref[0], count, src_ref, rcv_ref, row_of, sources_ref, sister_ref, cross_ref)

    def chunk(c, carry):
        first = pl.multiple_of(c * CHUNK, CHUNK)
        product_ref[...] = lags_of(cross_ref, first, CHUNK, table_ref)

        def place(g, inner):
            for u in range(GROUP):
                i = g * GROUP + u
                rows_ref[pl.ds(slot_ref[first + i], 1), :] = product_ref[pl.ds(i, 1), :]
            return inner

        return lax.fori_loop(0, (jnp.minimum(count - first, CHUNK) + GROUP - 1) // GROUP, place, carry)

    lax.fori_loop(0, (count + CHUNK - 1) // CHUNK, chunk, 0)
    out_ref[...] = rows_ref[0:slots, :].reshape(out_ref.shape).astype(jnp.bfloat16)


def correlate(kernel, lists, pieces, receivers, blocks, shape, dtype, extra):
    slots = lists[1].shape[0]
    row = pieces[0].shape[1:]
    direct = (*receivers, *blocks)
    return pl.pallas_call(
        kernel,
        out_shape=jax.ShapeDtypeStruct(shape, dtype),
        grid_spec=pltpu.PrefetchScalarGridSpec(
            num_scalar_prefetch=4,
            grid=(1,),
            in_specs=[pl.BlockSpec(memory_space=pl.ANY)] * len(pieces) + [pl.BlockSpec(memory_space=pltpu.VMEM)] * len(direct),
            out_specs=pl.BlockSpec(shape, lambda *_: (0,) * len(shape)),
            scratch_shapes=[
                pltpu.VMEM((sum(p.shape[0] for p in pieces),) + row, jnp.bfloat16),
                pltpu.VMEM(((slots + GROUP) * HALF_ROWS, LANES), jnp.float32),
                *extra,
                pltpu.SemaphoreType.DMA((len(pieces),)),
            ],
        ),
        compiler_params=pltpu.CompilerParams(vmem_limit_bytes=24 << 20),
    )(*lists, *pieces, *direct)


def pack_kernel(ids_ref, holder_ref, receiver_ref, source_ref, out_ref):
    pairs = holder_ref.shape[1]
    per = ids_ref.shape[0]
    packed = (holder_ref[...] * PER_DEVICE + receiver_ref[...]) * SOURCES + source_ref[...]
    lane = lax.broadcasted_iota(jnp.int32, (1, pairs), 1)
    ids = jnp.zeros((1, pairs), jnp.int32)
    for n in range(per):
        ids = jnp.where(lane == n, ids_ref[n], ids)
    row = jnp.concatenate([packed, ids], axis=1)
    for g in range(out_ref.shape[0]):
        out_ref[g] = row


def pack_notes(source_ids, holder, receiver, source, copies):
    pairs = holder.shape[0]
    line = lambda a: a.reshape(1, pairs)
    spec = pl.BlockSpec((1, pairs), lambda *_: (0, 0))
    return pl.pallas_call(
        pack_kernel,
        out_shape=jax.ShapeDtypeStruct((copies, 1, 2 * pairs), jnp.int32),
        grid_spec=pltpu.PrefetchScalarGridSpec(
            num_scalar_prefetch=1,
            grid=(1,),
            in_specs=[spec, spec, spec],
            out_specs=pl.BlockSpec((copies, 1, 2 * pairs), lambda *_: (0, 0, 0)),
        ),
        name="pack",
    )(source_ids, line(holder), line(receiver), line(source))


def pick_kernel(wanted_ref, raw_ref, taper_ref, out_ref, rows_ref, sems):
    rows = rows_ref.shape[0]
    copies = [
        pltpu.make_async_copy(raw_ref.at[pl.ds(wanted_ref[r], 1), :], rows_ref.at[pl.ds(r, 1), :], sems.at[r])
        for r in range(rows)
    ]
    for copy in copies:
        copy.start()
    for copy in copies:
        copy.wait()
    value = (rows_ref[...] * taper_ref[...]).astype(jnp.bfloat16)
    for g in range(out_ref.shape[0]):
        out_ref[g] = value


def pick_rows(wanted, raw_window, taper, copies):
    rows, span = wanted.shape[0], raw_window.shape[1]
    return pl.pallas_call(
        pick_kernel,
        out_shape=jax.ShapeDtypeStruct((copies, rows, span), jnp.bfloat16),
        grid_spec=pltpu.PrefetchScalarGridSpec(
            num_scalar_prefetch=1,
            grid=(1,),
            in_specs=[pl.BlockSpec(memory_space=pl.ANY), pl.BlockSpec((1, span), lambda *_: (0, 0))],
            out_specs=pl.BlockSpec((copies, rows, span), lambda *_: (0, 0, 0)),
            scratch_shapes=[pltpu.VMEM((rows, span), jnp.float32), pltpu.SemaphoreType.DMA((rows,))],
        ),
        name="pick",
    )(wanted, raw_window, taper.reshape(1, span))


def shift(value, axis, step):
    if axis == "core":
        return lax.ppermute(value, "gx", [(g, g ^ 1) for g in range(2 * SIDE)])
    return lax.ppermute(value, "gx", [(g, (g + 2 * step) % (2 * SIDE)) for g in range(2 * SIDE)])


def gather_ring(value, axis):
    return jnp.stack([value] + [shift(value, axis, d) for d in (1, 2, 3)], axis=0)


def program(raw_window, source_ids, pair_source, pair_holder, pair_receiver):
    groups = lax.axis_size("gy")
    devices = lax.axis_size("gx") * groups
    gx, gy = lax.axis_index("gx"), lax.axis_index("gy")
    place = {"core": gx % 2, "y": gx // 2}
    core = place["core"]
    here = gx * groups + gy
    span = raw_window.shape[1]
    channels = raw_window.shape[0] // groups
    sample = (gy * span + jnp.arange(span, dtype=jnp.int32)) % SEGLEN
    taper = jnp.sin(math.pi * (sample.astype(jnp.float32) + 0.5) / SEGLEN) ** 2

    pairs = pair_source.shape[0]
    holder = pair_holder[:, 0]
    order = jnp.arange(pairs, dtype=jnp.int32)
    per = source_ids.shape[0]
    notes = pack_notes(source_ids, holder, pair_receiver, pair_source, groups)
    notes = lax.all_to_all(notes, "gy", split_axis=0, concat_axis=0, tiled=True)
    wanted = (notes[:, 0, pairs:pairs + per] - gx * groups * channels).reshape(-1)
    notes = notes[:, 0, :pairs]
    first = pick_rows(wanted, raw_window, taper, groups)
    first = lax.all_to_all(first, "gy", split_axis=0, concat_axis=0, tiled=True)
    tapered = (raw_window * taper[None, :]).astype(jnp.bfloat16)
    samples = lax.all_to_all(tapered.reshape(groups, channels, span), "gy", split_axis=0, concat_axis=0, tiled=True)
    notes = gather_ring(notes, "y")
    notes = jnp.stack([notes, shift(notes, "core", 1)], axis=0).reshape(devices, pairs)

    twiddle = twiddle_table()
    upper, lower = inner_table()
    near0, away = whiten(core.reshape(1), first, twiddle, upper, lower, NSEG)
    near1 = shift(away, "core", 1)
    ahead0 = shift(near0, "y", 1)
    behind0 = shift(near0, "y", 3)
    ahead1 = shift(near1, "y", 1)
    behind1 = shift(near1, "y", 3)
    far0 = shift(ahead0, "y", 1)
    far1 = shift(behind1, "y", 3)

    notes, late, _ = lax.optimization_barrier((notes, core, near1))
    table = inverse_table(late, late - core)

    samples = pltpu.with_memory_space_constraint(samples, pltpu.MemorySpace.HBM)
    mine, other = whiten(core.reshape(1), samples, twiddle, upper, lower, 2)
    sister = shift(other, "core", 1)

    dev = jnp.arange(devices, dtype=jnp.int32)
    own = (
        (dev // (SIDE * groups) ^ late) + (place["y"] - dev // groups % SIDE) % SIDE * 2
    ) * groups + dev % groups
    each = channels * 256
    key = notes // each
    entry = order[None, :] * each + notes % each + 1
    first_last = []
    for name in (here, here ^ groups):
        match = key == name
        high = jnp.max(jnp.where(match, entry, 0), axis=1)
        low = jnp.max(jnp.where(match, pairs * each + 1 - entry, 0), axis=1)
        low = jnp.where(low > 0, pairs * each + 1 - low, 0)
        first_last += [low, jnp.where(high > low, high, 0)]
    found = jnp.stack(first_last)
    asked = jnp.sum(jnp.where(own[None, None, :] == dev[None, :, None], found[:, None, :], 0), axis=2)
    valid = asked > 0
    asked = jnp.maximum(asked - 1, 0) % each
    slots = asked.size
    source_no = asked % 256
    source_gx = source_no // (2 * groups)
    rel_y = (place["y"] - source_gx // 2) % SIDE
    far = rel_y == 2
    piece = jnp.where(far, 0, jnp.minimum(rel_y, 2))
    source_at = (piece * 2 + (source_gx % 2 ^ core)) * (2 * groups) + source_no % (2 * groups)
    kind = jnp.arange(4, dtype=jnp.int32)[:, None]
    slot_no = dev[None, :] * 4 + kind
    receiver_at = asked // 256
    entry = ((slot_no - slots) * 256 + receiver_at) * 256 + source_at
    index = jnp.arange(slots, dtype=jnp.int32)

    def compact(chosen):
        chosen = chosen.reshape(-1)
        spot = jnp.sum((chosen[None, :] & (index[None, :] < index[:, None])).astype(jnp.int32), axis=1)
        hit = chosen[None, :] & (spot[None, :] == index[:, None])
        line = jnp.sum(jnp.where(hit, entry.reshape(1, -1), 0), axis=1) + slots * 65536
        ends = (jnp.arange(2, dtype=jnp.int32) + 1) * (slots // 2)
        counts = jnp.sum((chosen[None, :] & (index[None, :] < ends[:, None])).astype(jnp.int32), axis=1)
        return counts, line % 256, line // 256 % 256, line // 65536

    near_lists = compact(valid & ~far)
    far_lists = compact(valid & far)

    receivers = [mine, sister]
    near = correlate(
        near_kernel, near_lists, [near0, near1, ahead0, ahead1, behind0, behind1], receivers, [table], (slots, NLAG), jnp.float32, []
    )
    extra = [pltpu.VMEM((slots + GROUP, NLAG), jnp.float32), pltpu.VMEM((CHUNK, NLAG), jnp.float32)]
    partial = correlate(far_kernel, far_lists, [far0, far1], receivers, [table, near], (devices, 4, NLAG), jnp.bfloat16, extra)
    returned = lax.all_to_all(partial, ("gx", "gy"), split_axis=0, concat_axis=0, tiled=True)
    returned = returned.reshape(devices * 4, NLAG)
    same = (holder[:, None] == holder[None, :]) & (order[None, :] < order[:, None])
    rank = jnp.sum(same.astype(jnp.int32), axis=1)
    row = jnp.arange(4 * devices, dtype=jnp.int32)
    row_dev, row_rel, row_rank = row // 4, row // 2 % 2, row % 2
    row_holder = jnp.where(row_rel == 0, row_dev, row_dev ^ groups)
    pick = (row_holder[None, :] == holder[:, None]) & (row_rank[None, :] == rank[:, None])
    return jnp.dot(pick.astype(jnp.bfloat16), returned, preferred_element_type=jnp.float32)


def solution(mesh):
    return jax.shard_map(
        program,
        mesh=mesh,
        in_specs=(
            P("gx", "gy"),
            P(("gx", "gy")),
            P(("gx", "gy")),
            P(("gx", "gy"), None),
            P(("gx", "gy")),
        ),
        out_specs=P(("gx", "gy"), None),
        check_vma=False,
    )
```

```python
import math

import jax
import jax.numpy as jnp
from jax import lax
from jax.experimental import pallas as pl
from jax.experimental.pallas import tpu as pltpu
from jax.sharding import PartitionSpec as P


NBIN = 2048
SEGLEN = 4096
NSEG = 4
BAND = 64
NLAG = 512
SIDE = 4
SOURCES = 256
PER_DEVICE = 64
RADIX = 16
INNER = SEGLEN // RADIX
LANES = 128
HALF_ROWS = 2 * (RADIX // 2)


def split_table(table):
    upper = table.astype(jnp.bfloat16)
    lower = (table - upper.astype(jnp.float32)).astype(jnp.bfloat16)
    return (upper, lower)


def lane_bins():
    lane = jnp.arange(LANES, dtype=jnp.int32)
    return 4 * (lane % 32) + lane // 32


def inner_table():
    times = jnp.arange(INNER, dtype=jnp.int32)
    low = lane_bins()
    high = INNER - 1 - low
    turn = 2.0 * math.pi / INNER

    def block(bins, sign):
        angle = (times[:, None] * bins[None, :] % INNER).astype(jnp.float32) * turn
        cos, sin = jnp.cos(angle), jnp.sin(angle)
        top = jnp.concatenate([cos, -sign * sin], axis=1)
        bottom = jnp.concatenate([sin, sign * cos], axis=1)
        return jnp.concatenate([top, bottom], axis=0)

    return split_table(jnp.concatenate([block(low, 1.0), block(high, -1.0)], axis=1))


def twiddle_table():
    rows = jnp.arange(RADIX, dtype=jnp.int32)
    times = jnp.arange(INNER, dtype=jnp.int32)
    angle = (rows[:, None] * times[None, :] % SEGLEN).astype(jnp.float32) * (2.0 * math.pi / SEGLEN)
    return jnp.stack([jnp.cos(angle), -jnp.sin(angle)], axis=0)


def turns(count, lags):
    angle = (count[:, None] * lags[None, :] % SEGLEN).astype(jnp.float32) * (2.0 * math.pi / SEGLEN)
    return jnp.cos(angle), jnp.sin(angle)


def inverse_table(core, zero):
    outer = core * (RADIX // 2) + jnp.arange(RADIX // 2, dtype=jnp.int32)
    inner = RADIX * lane_bins() + zero
    lags = (jnp.arange(NLAG, dtype=jnp.int32) - NLAG // 2) % SEGLEN
    (c1, s1), (c2, s2) = lax.optimization_barrier((turns(outer, lags), turns(inner, lags)))
    c1, s1, c2, s2 = c1[:, None], s1[:, None], c2[None], s2[None]
    bins = outer[:, None, None] + inner[None, :, None]
    weight = jnp.where(bins == 0, 1.0, 2.0).astype(jnp.float32) * (0.5 / math.sqrt(NSEG * NBIN))
    table = jnp.stack([weight * (c1 * c2 - s1 * s2), -weight * (s1 * c2 + c1 * s2)], axis=0)
    return table.astype(jnp.bfloat16).reshape(NBIN, NLAG)


def real_dft(values):
    n = len(values)
    if n == 2:
        return [(values[0] + values[1], None), (values[0] - values[1], None)]
    even = real_dft(values[0::2])
    odd = real_dft(values[1::2])
    out = [None] * (n // 2 + 1)
    for k in range(n // 4 + 1):
        er, ei = even[k]
        pr, pi = odd[k]
        c, s = math.cos(2 * math.pi * k / n), math.sin(2 * math.pi * k / n)
        if k == 0:
            out[0] = (er + pr, None)
            out[n // 2] = (er - pr, None)
        elif 4 * k == n:
            out[k] = (er, -pr)
        else:
            if 8 * k == n:
                tr, ti = (pr + pi) * c, (pi - pr) * c
            else:
                tr, ti = pr * c + pi * s, pi * c - pr * s
            out[k] = (er + tr, ei + ti)
            out[n // 2 - k] = (er - tr, ti - ei)
    return out


def whiten_kernel(core_ref, x_ref, tw_ref, upper_ref, lower_ref, mine_ref, other_ref, *scratch):
    count = x_ref.shape[0] // SIDE
    parts = [(x_ref.at[n * SIDE:(n + 1) * SIDE], scratch[2 * n], scratch[2 * n + 1]) for n in range(count)]
    butterflies(tw_ref, *parts[0])
    for n in range(count):
        spectra = products(x_ref.shape[1], upper_ref, lower_ref, *parts[n][1:])
        if n + 1 < count:
            butterflies(tw_ref, *parts[n + 1])
        at = slice(n * HALF_ROWS, (n + 1) * HALF_ROWS)
        finish(core_ref, x_ref.shape[1], spectra, mine_ref.at[:, at], other_ref.at[:, at])


def butterflies(tw_ref, x_ref, hi_ref, lo_ref):
    rows = x_ref.shape[1]
    half = RADIX // 2
    where = lambda f: (f - 1) % (half + 1)
    for block in range(rows // 16):
        r = slice(block * 16, block * 16 + 16)
        for k in range(INNER // LANES):
            slices = []
            for t in range(RADIX):
                at = (t % SIDE) * INNER + k * LANES
                slices.append(x_ref[t // SIDE, r, at:at + LANES].astype(jnp.float32))
            outer = real_dft(slices)
            for f in range(half + 1):
                re, im = outer[f]
                lanes = slice(k * LANES, (k + 1) * LANES)
                c, s = tw_ref[0, f:f + 1, lanes], tw_ref[1, f:f + 1, lanes]
                if f == 0:
                    parts = (re,)
                elif im is None:
                    parts = (re * c, re * s)
                else:
                    parts = (re * c - im * s, re * s + im * c)
                row = slice(where(f) * rows + block * 16, where(f) * rows + block * 16 + 16)
                for n, part in enumerate(parts):
                    hi = part.astype(jnp.bfloat16)
                    at = slice(n * INNER + k * LANES, n * INNER + (k + 1) * LANES)
                    hi_ref[row, at] = hi
                    lo_ref[row, at] = (part - hi.astype(jnp.float32)).astype(jnp.bfloat16)


def products(rows, upper_ref, lower_ref, hi_ref, lo_ref):
    half = RADIX // 2

    def spectrum(row, depth, width):
        hi, lo = hi_ref[row, :depth], lo_ref[row, :depth]
        upper, lower = upper_ref[:depth, :width], lower_ref[:depth, :width]
        out = jnp.dot(hi, upper, preferred_element_type=jnp.float32)
        out += jnp.dot(hi, lower, preferred_element_type=jnp.float32)
        return out + jnp.dot(lo, upper, preferred_element_type=jnp.float32)

    most = spectrum(slice(0, (half - 1) * rows), 2 * INNER, 4 * LANES)
    middle = spectrum(slice((half - 1) * rows, half * rows), 2 * INNER, 2 * LANES)
    first = spectrum(slice(half * rows, (half + 1) * rows), INNER, 2 * LANES)
    return first, middle, most


def finish(core_ref, rows, spectra, mine_ref, other_ref):
    half = RADIX // 2
    first, middle, most = spectra

    def part(f, k):
        if f == 0:
            return first[:, k * LANES:(k + 1) * LANES]
        if f == half:
            return middle[:, k * LANES:(k + 1) * LANES]
        g, base = (f, 0) if f < half else (RADIX - f, 2)
        return most[(g - 1) * rows:g * rows, (base + k) * LANES:(base + k + 1) * LANES]

    power = None
    for f in range(RADIX):
        re, im = part(f, 0), part(f, 1)
        both = re * re + im * im
        power = both if power is None else power + both
    power = power + pltpu.roll(power, 64, 1)
    power = power + pltpu.roll(power, 32, 1)
    scale = 1.0 / jnp.sqrt(power * (1.0 / BAND) + 1e-06)
    low = core_ref[0] == 0
    for block in range(rows // 8):
        r = slice(block * 8, block * 8 + 8)
        halves = []
        for h in range(2):
            tiles = [part(h * 8 + f, k)[r] * scale[r] for k in range(2) for f in range(8)]
            halves.append(jnp.transpose(jnp.stack(tiles, axis=0), (1, 0, 2)))
        mine_ref[r] = jnp.where(low, halves[0], halves[1]).astype(jnp.bfloat16)
        other_ref[r] = jnp.where(low, halves[1], halves[0]).astype(jnp.bfloat16)


def whiten(core, samples, twiddle, upper, lower, per):
    rows = samples.shape[1]
    out = jax.ShapeDtypeStruct((rows, NSEG * HALF_ROWS, LANES), jnp.bfloat16)
    resident = pl.BlockSpec(memory_space=pltpu.VMEM)
    if per == NSEG:
        spec = samples_spec = resident
    else:
        spec = pl.BlockSpec((rows, per * HALF_ROWS, LANES), lambda s, c: (0, s, 0))
        samples_spec = pl.BlockSpec((per * SIDE, rows, SEGLEN // SIDE), lambda s, c: (s, 0, 0))
    count = RADIX // 2 + 1
    return pl.pallas_call(
        whiten_kernel,
        out_shape=(out, out),
        grid_spec=pltpu.PrefetchScalarGridSpec(
            num_scalar_prefetch=1,
            grid=(NSEG // per,),
            in_specs=[
                samples_spec,
                resident,
                resident,
                resident,
            ],
            out_specs=(spec, spec),
            scratch_shapes=[pltpu.VMEM((count * rows, 2 * INNER), jnp.bfloat16)] * (2 * per),
        ),
        compiler_params=pltpu.CompilerParams(vmem_limit_bytes=24 << 20),
        name="whiten",
    )(core, samples, twiddle, upper, lower)


GROUP = 8
CHUNK = 128


def load_pieces(pieces, targets, sems):
    copies = []
    n = 0
    for group, target in zip(pieces, targets):
        at = 0
        for piece in group:
            copies.append(pltpu.make_async_copy(piece, target.at[at:at + piece.shape[0]], sems.at[n]))
            at += piece.shape[0]
            n += 1
    for copy in copies:
        copy.start()
    return copies


def cross_slots(start, stop, src_ref, rcv_ref, row_of, sources_ref, receivers_ref, cross_ref):
    last = src_ref.shape[0] - 1

    def group(g, carry):
        for u in range(GROUP):
            i = start + g * GROUP + u
            entry = jnp.minimum(i, last)
            a = sources_ref[src_ref[entry]].astype(jnp.float32)
            b = receivers_ref[rcv_ref[entry]].astype(jnp.float32)
            re = im = None
            for s in range(NSEG):
                ar, ai = a[s * 16:s * 16 + 8], a[s * 16 + 8:s * 16 + 16]
                br, bi = b[s * 16:s * 16 + 8], b[s * 16 + 8:s * 16 + 16]
                r = ar * br + ai * bi
                m = ai * br - ar * bi
                re = r if re is None else re + r
                im = m if im is None else im + m
            at = pl.multiple_of(row_of(i, entry) * HALF_ROWS, HALF_ROWS)
            cross_ref[pl.ds(at, 8), :] = re
            cross_ref[pl.ds(at + 8, 8), :] = im
        return carry

    lax.fori_loop(0, (stop - start + GROUP - 1) // GROUP, group, 0)


def lags_of(cross_ref, first, count, table_ref):
    cross = jnp.concatenate(
        [cross_ref[pl.ds(first * HALF_ROWS + g, count, stride=HALF_ROWS), :].astype(jnp.bfloat16) for g in range(HALF_ROWS)],
        axis=1,
    )
    return jnp.dot(cross, table_ref[...], preferred_element_type=jnp.float32)


def near_kernel(count_ref, src_ref, rcv_ref, slot_ref, *refs):
    pieces = refs[:6]
    mine_ref, sister_ref, table_ref, out_ref, sources_ref, cross_ref, sems = refs[6:]
    copies = load_pieces((pieces,), (sources_ref,), sems)
    cross_ref[...] = jnp.zeros_like(cross_ref)
    for copy in copies:
        copy.wait()
    slot_of = lambda i, entry: slot_ref[entry]
    cross_slots(0, count_ref[0], src_ref, rcv_ref, slot_of, sources_ref, mine_ref, cross_ref)
    cross_slots(count_ref[0], count_ref[1], src_ref, rcv_ref, slot_of, sources_ref, sister_ref, cross_ref)
    out_ref[...] = lags_of(cross_ref, 0, out_ref.shape[0], table_ref)


def far_kernel(count_ref, src_ref, rcv_ref, slot_ref, *refs):
    pieces = refs[:2]
    mine_ref, sister_ref, table_ref, near_ref, out_ref, sources_ref, cross_ref, rows_ref, product_ref, sems = refs[2:]
    slots = near_ref.shape[0]
    copies = load_pieces((pieces,), (sources_ref,), sems)
    rows_ref[0:slots, :] = near_ref[...]
    for copy in copies:
        copy.wait()
    count = count_ref[1]
    row_of = lambda i, entry: i
    cross_slots(0, count_ref[0], src_ref, rcv_ref, row_of, sources_ref, mine_ref, cross_ref)
    cross_slots(count_ref[0], count, src_ref, rcv_ref, row_of, sources_ref, sister_ref, cross_ref)

    def chunk(c, carry):
        first = pl.multiple_of(c * CHUNK, CHUNK)
        product_ref[...] = lags_of(cross_ref, first, CHUNK, table_ref)

        def place(g, inner):
            for u in range(GROUP):
                i = g * GROUP + u
                rows_ref[pl.ds(slot_ref[first + i], 1), :] = product_ref[pl.ds(i, 1), :]
            return inner

        return lax.fori_loop(0, (jnp.minimum(count - first, CHUNK) + GROUP - 1) // GROUP, place, carry)

    lax.fori_loop(0, (count + CHUNK - 1) // CHUNK, chunk, 0)
    out_ref[...] = rows_ref[0:slots, :].reshape(out_ref.shape).astype(jnp.bfloat16)


def correlate(kernel, lists, pieces, receivers, blocks, shape, dtype, extra):
    slots = lists[1].shape[0]
    row = pieces[0].shape[1:]
    direct = (*receivers, *blocks)
    return pl.pallas_call(
        kernel,
        out_shape=jax.ShapeDtypeStruct(shape, dtype),
        grid_spec=pltpu.PrefetchScalarGridSpec(
            num_scalar_prefetch=4,
            grid=(1,),
            in_specs=[pl.BlockSpec(memory_space=pl.ANY)] * len(pieces) + [pl.BlockSpec(memory_space=pltpu.VMEM)] * len(direct),
            out_specs=pl.BlockSpec(shape, lambda *_: (0,) * len(shape)),
            scratch_shapes=[
                pltpu.VMEM((sum(p.shape[0] for p in pieces),) + row, jnp.bfloat16),
                pltpu.VMEM(((slots + GROUP) * HALF_ROWS, LANES), jnp.float32),
                *extra,
                pltpu.SemaphoreType.DMA((len(pieces),)),
            ],
        ),
        compiler_params=pltpu.CompilerParams(vmem_limit_bytes=24 << 20),
    )(*lists, *pieces, *direct)


def pack_kernel(ids_ref, holder_ref, receiver_ref, source_ref, out_ref):
    pairs = holder_ref.shape[1]
    per = ids_ref.shape[0]
    packed = (holder_ref[...] * PER_DEVICE + receiver_ref[...]) * SOURCES + source_ref[...]
    lane = lax.broadcasted_iota(jnp.int32, (1, pairs), 1)
    ids = jnp.zeros((1, pairs), jnp.int32)
    for n in range(per):
        ids = jnp.where(lane == n, ids_ref[n], ids)
    row = jnp.concatenate([packed, ids], axis=1)
    for g in range(out_ref.shape[0]):
        out_ref[g] = row


def pack_notes(source_ids, holder, receiver, source, copies):
    pairs = holder.shape[0]
    line = lambda a: a.reshape(1, pairs)
    spec = pl.BlockSpec((1, pairs), lambda *_: (0, 0))
    return pl.pallas_call(
        pack_kernel,
        out_shape=jax.ShapeDtypeStruct((copies, 1, 2 * pairs), jnp.int32),
        grid_spec=pltpu.PrefetchScalarGridSpec(
            num_scalar_prefetch=1,
            grid=(1,),
            in_specs=[spec, spec, spec],
            out_specs=pl.BlockSpec((copies, 1, 2 * pairs), lambda *_: (0, 0, 0)),
        ),
        name="pack",
    )(source_ids, line(holder), line(receiver), line(source))


def pick_kernel(wanted_ref, raw_ref, taper_ref, out_ref, rows_ref, sems):
    rows = rows_ref.shape[0]
    copies = [
        pltpu.make_async_copy(raw_ref.at[pl.ds(wanted_ref[r], 1), :], rows_ref.at[pl.ds(r, 1), :], sems.at[r])
        for r in range(rows)
    ]
    for copy in copies:
        copy.start()
    for copy in copies:
        copy.wait()
    value = (rows_ref[...] * taper_ref[...]).astype(jnp.bfloat16)
    for g in range(out_ref.shape[0]):
        out_ref[g] = value


def pick_rows(wanted, raw_window, taper, copies):
    rows, span = wanted.shape[0], raw_window.shape[1]
    return pl.pallas_call(
        pick_kernel,
        out_shape=jax.ShapeDtypeStruct((copies, rows, span), jnp.bfloat16),
        grid_spec=pltpu.PrefetchScalarGridSpec(
            num_scalar_prefetch=1,
            grid=(1,),
            in_specs=[pl.BlockSpec(memory_space=pl.ANY), pl.BlockSpec((1, span), lambda *_: (0, 0))],
            out_specs=pl.BlockSpec((copies, rows, span), lambda *_: (0, 0, 0)),
            scratch_shapes=[pltpu.VMEM((rows, span), jnp.float32), pltpu.SemaphoreType.DMA((rows,))],
        ),
        name="pick",
    )(wanted, raw_window, taper.reshape(1, span))


def shift(value, axis, step):
    if axis == "core":
        return lax.ppermute(value, "gx", [(g, g ^ 1) for g in range(2 * SIDE)])
    return lax.ppermute(value, "gx", [(g, (g + 2 * step) % (2 * SIDE)) for g in range(2 * SIDE)])


def gather_ring(value, axis):
    return jnp.stack([value] + [shift(value, axis, d) for d in (1, 2, 3)], axis=0)


def program(raw_window, source_ids, pair_source, pair_holder, pair_receiver):
    groups = lax.axis_size("gy")
    devices = lax.axis_size("gx") * groups
    gx, gy = lax.axis_index("gx"), lax.axis_index("gy")
    place = {"core": gx % 2, "y": gx // 2}
    core = place["core"]
    here = gx * groups + gy
    span = raw_window.shape[1]
    channels = raw_window.shape[0] // groups
    sample = (gy * span + jnp.arange(span, dtype=jnp.int32)) % SEGLEN
    taper = jnp.sin(math.pi * (sample.astype(jnp.float32) + 0.5) / SEGLEN) ** 2

    pairs = pair_source.shape[0]
    holder = pair_holder[:, 0]
    order = jnp.arange(pairs, dtype=jnp.int32)
    per = source_ids.shape[0]
    notes = pack_notes(source_ids, holder, pair_receiver, pair_source, groups)
    notes = lax.all_to_all(notes, "gy", split_axis=0, concat_axis=0, tiled=True)
    wanted = (notes[:, 0, pairs:pairs + per] - gx * groups * channels).reshape(-1)
    notes = notes[:, 0, :pairs]
    first = pick_rows(wanted, raw_window, taper, groups)
    first = lax.all_to_all(first, "gy", split_axis=0, concat_axis=0, tiled=True)
    tapered = (raw_window * taper[None, :]).astype(jnp.bfloat16)
    samples = lax.all_to_all(tapered.reshape(groups, channels, span), "gy", split_axis=0, concat_axis=0, tiled=True)
    notes = gather_ring(notes, "y")
    notes = jnp.stack([notes, shift(notes, "core", 1)], axis=0).reshape(devices, pairs)

    twiddle = twiddle_table()
    upper, lower = inner_table()
    near0, away = whiten(core.reshape(1), first, twiddle, upper, lower, NSEG)
    near1 = shift(away, "core", 1)
    ahead0 = shift(near0, "y", 1)
    behind0 = shift(near0, "y", 3)
    ahead1 = shift(near1, "y", 1)
    behind1 = shift(near1, "y", 3)
    far0 = shift(ahead0, "y", 1)
    far1 = shift(behind1, "y", 3)

    notes, late, _ = lax.optimization_barrier((notes, core, near1))
    table = inverse_table(late, late - core)

    samples = pltpu.with_memory_space_constraint(samples, pltpu.MemorySpace.HBM)
    mine, other = whiten(core.reshape(1), samples, twiddle, upper, lower, 2)
    sister = shift(other, "core", 1)

    dev = jnp.arange(devices, dtype=jnp.int32)
    own = (
        (dev // (SIDE * groups) ^ late) + (place["y"] - dev // groups % SIDE) % SIDE * 2
    ) * groups + dev % groups
    each = channels * 256
    key = notes // each
    entry = order[None, :] * each + notes % each + 1
    first_last = []
    for name in (here, here ^ groups):
        match = key == name
        high = jnp.max(jnp.where(match, entry, 0), axis=1)
        low = jnp.max(jnp.where(match, pairs * each + 1 - entry, 0), axis=1)
        low = jnp.where(low > 0, pairs * each + 1 - low, 0)
        first_last += [low, jnp.where(high > low, high, 0)]
    found = jnp.stack(first_last)
    asked = jnp.sum(jnp.where(own[None, None, :] == dev[None, :, None], found[:, None, :], 0), axis=2)
    valid = asked > 0
    asked = jnp.maximum(asked - 1, 0) % each
    slots = asked.size
    source_no = asked % 256
    source_gx = source_no // (2 * groups)
    rel_y = (place["y"] - source_gx // 2) % SIDE
    far = rel_y == 2
    piece = jnp.where(far, 0, jnp.minimum(rel_y, 2))
    source_at = (piece * 2 + (source_gx % 2 ^ core)) * (2 * groups) + source_no % (2 * groups)
    kind = jnp.arange(4, dtype=jnp.int32)[:, None]
    slot_no = dev[None, :] * 4 + kind
    receiver_at = asked // 256
    entry = ((slot_no - slots) * 256 + receiver_at) * 256 + source_at
    index = jnp.arange(slots, dtype=jnp.int32)

    def compact(chosen):
        chosen = chosen.reshape(-1)
        spot = jnp.sum((chosen[None, :] & (index[None, :] < index[:, None])).astype(jnp.int32), axis=1)
        hit = chosen[None, :] & (spot[None, :] == index[:, None])
        line = jnp.sum(jnp.where(hit, entry.reshape(1, -1), 0), axis=1) + slots * 65536
        ends = (jnp.arange(2, dtype=jnp.int32) + 1) * (slots // 2)
        counts = jnp.sum((chosen[None, :] & (index[None, :] < ends[:, None])).astype(jnp.int32), axis=1)
        return counts, line % 256, line // 256 % 256, line // 65536

    near_lists = compact(valid & ~far)
    far_lists = compact(valid & far)

    receivers = [mine, sister]
    near = correlate(
        near_kernel, near_lists, [near0, near1, ahead0, ahead1, behind0, behind1], receivers, [table], (slots, NLAG), jnp.float32, []
    )
    extra = [pltpu.VMEM((slots + GROUP, NLAG), jnp.float32), pltpu.VMEM((CHUNK, NLAG), jnp.float32)]
    partial = correlate(far_kernel, far_lists, [far0, far1], receivers, [table, near], (devices, 4, NLAG), jnp.bfloat16, extra)
    returned = lax.all_to_all(partial, ("gx", "gy"), split_axis=0, concat_axis=0, tiled=True)
    returned = returned.reshape(devices * 4, NLAG)
    same = (holder[:, None] == holder[None, :]) & (order[None, :] < order[:, None])
    rank = jnp.sum(same.astype(jnp.int32), axis=1)
    row = jnp.arange(4 * devices, dtype=jnp.int32)
    row_dev, row_rel, row_rank = row // 4, row // 2 % 2, row % 2
    row_holder = jnp.where(row_rel == 0, row_dev, row_dev ^ groups)
    pick = (row_holder[None, :] == holder[:, None]) & (row_rank[None, :] == rank[:, None])
    return jnp.dot(pick.astype(jnp.bfloat16), returned, preferred_element_type=jnp.float32)


def solution(mesh):
    return jax.shard_map(
        program,
        mesh=mesh,
        in_specs=(
            P("gx", "gy"),
            P(("gx", "gy")),
            P(("gx", "gy")),
            P(("gx", "gy"), None),
            P(("gx", "gy")),
        ),
        out_specs=P(("gx", "gy"), None),
        check_vma=False,
    )
```
